32 devices in a mesh: dp: 16 (over z, y, x), tensor: 2 (over core).
Axes of the slice: x: 2, y: 2, z: 4, core: 2. Of those that a mesh axis runs over, the one named last changes fastest.
Arguments:
- tokens: bfloat16 [768, 16, 768], P('dp', 'tensor'), may hold values from -6 to 6
- cotangent: bfloat16 [768, 16, 768], P('dp', 'tensor'), may hold values from -6 to 6
- block_route: int32 [768], P('dp'), may hold values from 0 to 767, as said below
- lengths: int32 [48, 3], P('dp'), may hold values from 1 to 170, 256 in all within a row
- w_query: bfloat16 [768, 768], P('dp', 'tensor'), may hold values from -0.3125 to 0.3125
- w_key: bfloat16 [768, 768], P('dp', 'tensor'), may hold values from -0.3125 to 0.3125
- w_value: bfloat16 [768, 768], P('dp', 'tensor'), may hold values from -0.21875 to 0.21875
- b_query: bfloat16 [2, 384], P('tensor'), may hold values from -3 to 3
- b_value: bfloat16 [2, 384], P('tensor'), may hold values from -3 to 3
- w_out: bfloat16 [768, 768], P('tensor', 'dp'), may hold values from -1.25 to 1.25
- b_out: bfloat16 [768], P('dp'), may hold values from -3 to 3
- gain_attn: bfloat16 [768], P('dp'), may hold values from 0.5 to 1.5
- shift_attn: bfloat16 [768], P('dp'), may hold values from -2 to 2
- w_inner: bfloat16 [768, 3072], P('dp', 'tensor'), may hold values from -0.21875 to 0.21875
- b_inner: bfloat16 [2, 1536], P('tensor', 'dp'), may hold values from -3 to 3
- w_outer: bfloat16 [3072, 768], P('tensor', 'dp'), may hold values from -0.15625 to 0.15625
- b_outer: bfloat16 [768], P('dp'), may hold values from -2 to 2
- gain_ffn: bfloat16 [768], P('dp'), may hold values from 0.5 to 1.5
- shift_ffn: bfloat16 [768], P('dp'), may hold values from -2 to 2
Outputs:
- layer_out: bfloat16 [768, 16, 768], P('dp', 'tensor')
- grad_tokens: bfloat16 [768, 16, 768], P('dp', 'tensor')
- grad_w_query: float32 [768, 768], P('dp', 'tensor')
- grad_w_key: float32 [768, 768], P('dp', 'tensor')
- grad_w_value: float32 [768, 768], P('dp', 'tensor')
- grad_b_query: float32 [2, 384], P('tensor')
- grad_b_value: float32 [2, 384], P('tensor')
- grad_w_out: float32 [768, 768], P('tensor', 'dp')
- grad_b_out: float32 [768], P('dp')
- grad_gain_attn: float32 [768], P('dp')
- grad_shift_attn: float32 [768], P('dp')
- grad_w_inner: float32 [768, 3072], P('dp', 'tensor')
- grad_b_inner: float32 [2, 1536], P('tensor', 'dp')
- grad_w_outer: float32 [3072, 768], P('tensor', 'dp')
- grad_b_outer: float32 [768], P('dp')
- grad_gain_ffn: float32 [768], P('dp')
- grad_shift_ffn: float32 [768], P('dp')
The draws below stay inside these ranges and needn't reach their ends.
Inputs may be any that keep to these rules, and one draw needn't show every extreme that they name: block_route is a permutation of the 768 block indices. Given block s * 3 * 16 + m * 16 + k goes to packed index d * 3 * 16 + m * 16 + j: it stays in micro-batch m; among the 16 blocks of one s and one m every d appears once, and bin (d, m) receives exactly one block from every s. `lengths`: each row sums to 256.
All inputs are finite; a program needn't handle non-finite values.
Results may differ from the reference program's by a relative error of at most 0.017.
Values may be sent and summed in bfloat16 or wider, within the bound.
A program may use at most 128 MiB of HBM per device.

```python
import math
import jax
import jax.numpy as jnp
import numpy as np
from jax import lax

D = 768
HEADS = 12
HD = 64
FF = 3072
BIN = 256
MB = 3
SEQS = 3
LONGEST = 170
BLK = 16
NBLK = 768
N_DP = 16
N_TENSOR = 2


def draw_block_route(key, part):
    devices = N_DP
    outward = jax.random.fold_in(key, 11)
    inward = jax.random.fold_in(key, 23)
    outgoing = jax.vmap(lambda subkey: jax.random.permutation(subkey, devices))(jax.random.split(outward, devices * MB))
    arrivals = jax.vmap(lambda subkey: jax.random.permutation(subkey, devices))(jax.random.split(inward, devices * MB))
    indices = jnp.arange(devices * MB * devices, dtype=jnp.int32)
    source = indices // (MB * devices)
    microbatch = indices // devices % MB
    slot_pos = indices % devices
    target = outgoing[source * MB + microbatch, slot_pos]
    placed = arrivals[target * MB + microbatch, source]
    return (target * (MB * devices) + microbatch * devices + placed).astype(jnp.int32)


def steps_of(stream_key, dims, pieces, smallest, largest):
    def one(position, blocks):
        steps = jax.random.uniform(jax.random.fold_in(jax.random.fold_in(stream_key, 6), position), (blocks,), jnp.float32, smallest / len(pieces), largest / len(pieces))
        return jnp.repeat(jnp.exp(steps), dims[position] // blocks).reshape((-1,) + (1,) * (len(dims) - position - 1))

    level = one(*pieces[0])
    for cut in pieces[1:]:
        level = level * one(*cut)
    return level


def length_profile(number_of, total, reach, skew):
    loads = [(1 << 20) // math.isqrt(grade ** skew) + 1 for grade in range(2, number_of + 1)]
    spare, counts = total - reach - (number_of - 1), [1] * (number_of - 1)
    while spare > 0:
        candidates = [i for i in range(number_of - 1) if counts[i] < reach]
        whole, budget = sum([loads[i] for i in candidates]), spare
        for i in candidates:
            addition = min(reach - counts[i], max(1, budget * loads[i] // whole), spare)
            counts[i] = counts[i] + addition
            spare = spare - addition
    return np.array([reach] + counts)


def uneven(own_key, count, total, most, skew):
    if count == 2:
        one = jax.random.randint(own_key, (), max(1, total - most), min(most, total - 1) + 1)
        return jnp.stack([one, total - one])
    sizes = jnp.asarray(length_profile(count, total, most, skew), jnp.int32)
    pairs = (count - 1) // 2
    donor, receiver = sizes[1:1 + 2 * pairs:2], sizes[2:2 + 2 * pairs:2]
    room = jnp.minimum(donor - 1, most - receiver)
    shifted = jax.random.randint(jax.random.fold_in(own_key, 1), (pairs,), 0, 1 << 20) % (room + 1)
    sizes = sizes.at[1:1 + 2 * pairs:2].set(donor - shifted).at[2:2 + 2 * pairs:2].set(receiver + shifted)
    return sizes[jax.random.permutation(jax.random.fold_in(own_key, 2), count)]


def gaussian(key, shape, width, reach, shards=(), kind=jnp.bfloat16):
    array = width * jax.random.normal(key, shape, jnp.float32)
    if shards:
        array = array * steps_of(key, shape, shards, -0.22, 0.18)
    return jnp.clip(array, -reach, reach).astype(kind)


def setup_inputs(seed: int = 0) -> dict:
    arg_keys = jax.random.split(jax.random.key(seed), 20)
    tokens = gaussian(arg_keys[0], (NBLK, BLK, D), 1.0, 6.0, ((0, 16), (1, 2)))
    cotangent = gaussian(arg_keys[1], (NBLK, BLK, D), 1.0, 6.0, ((0, 16), (1, 2)))
    block_route = draw_block_route(jax.random.fold_in(arg_keys[19], 71), 0)
    lengths = jax.vmap(lambda own: uneven(own, SEQS, BIN, LONGEST, 2))(jax.random.split(arg_keys[3], (N_DP * MB))).reshape((N_DP * MB, SEQS)).astype(jnp.int32)
    w_query = gaussian(arg_keys[4], (D, D), (D // 2) ** -0.5, 0.3125, ((0, 16), (1, 2)))
    w_key = gaussian(arg_keys[5], (D, D), (D // 2) ** -0.5, 0.3125, ((0, 16), (1, 2)))
    w_value = gaussian(arg_keys[6], (D, D), D ** -0.5, 0.21875, ((0, 16), (1, 2)))
    b_query = gaussian(arg_keys[7], (N_TENSOR, D // N_TENSOR), 0.5, 3.0, ((0, 2),))
    b_value = gaussian(arg_keys[8], (N_TENSOR, D // N_TENSOR), 0.5, 3.0, ((0, 2),))
    w_out = gaussian(arg_keys[9], (D, D), (D // 32) ** -0.5, 1.25, ((0, 2), (1, 16)))
    b_out = gaussian(arg_keys[10], (D,), 0.5, 3.0, ((0, 16),))
    gain_attn = jnp.clip(1.0 + 0.1 * jax.random.normal(arg_keys[11], (D,), jnp.float32), 0.5, 1.5).astype(jnp.bfloat16)
    shift_attn = gaussian(arg_keys[12], (D,), 0.3, 2.0, ((0, 16),))
    w_inner = gaussian(arg_keys[13], (D, FF), D ** -0.5, 0.21875, ((0, 16), (1, 2)))
    b_inner = gaussian(arg_keys[14], (N_TENSOR, FF // N_TENSOR), 0.5, 3.0, ((0, 2), (1, 16)))
    w_outer = gaussian(arg_keys[15], (FF, D), (FF // 2) ** -0.5, 0.15625, ((0, 2), (1, 16)))
    b_outer = gaussian(arg_keys[16], (D,), 0.3, 2.0, ((0, 16),))
    gain_ffn = jnp.clip(1.0 + 0.1 * jax.random.normal(arg_keys[17], (D,), jnp.float32), 0.5, 1.5).astype(jnp.bfloat16)
    shift_ffn = gaussian(arg_keys[18], (D,), 0.3, 2.0, ((0, 16),))
    return dict(tokens=tokens, cotangent=cotangent, block_route=block_route, lengths=lengths, w_query=w_query, w_key=w_key, w_value=w_value, b_query=b_query, b_value=b_value, w_out=w_out, b_out=b_out, gain_attn=gain_attn, shift_attn=shift_attn, w_inner=w_inner, b_inner=b_inner, w_outer=w_outer, b_outer=b_outer, gain_ffn=gain_ffn, shift_ffn=shift_ffn)


EPS_NORM = 1e-12

@jax.custom_vjp
def low(v):
    return lax.optimization_barrier(v.astype(jnp.bfloat16)).astype(jnp.float32)

@jax.custom_vjp
def low_back(v):
    return v

def low_keep(v):
    return (low(v), None)

def low_pass(kept, grad):
    return (grad,)

def back_keep(v):
    return (v, None)

def back_low(kept, grad):
    return (low(grad),)
low.defvjp(low_keep, low_pass)
low_back.defvjp(back_keep, back_low)

def layer_norm(residual, norm_gain, norm_shift):
    centre = residual - lax.optimization_barrier(jnp.mean(residual, axis=-1, keepdims=True))
    variance = lax.optimization_barrier(jnp.mean(centre * centre, axis=-1, keepdims=True))
    return centre * lax.rsqrt(variance + EPS_NORM) * norm_gain + norm_shift

def segment_of(seq_lengths, count_rows):
    seq_ends = jnp.cumsum(seq_lengths)
    positions = jnp.arange(count_rows, dtype=jnp.int32)
    return lax.optimization_barrier(jnp.sum((positions[:, None] >= seq_ends[None, :-1]).astype(jnp.int32), axis=1))

def bin_layer(params, bin_tokens, bin_lengths):
    w_query, w_key, w_value, b_query, b_value, w_out, b_out, gain_attn, shift_attn, w_inner, b_inner, w_outer, b_outer, gain_ffn, shift_ffn = params
    highest = lax.Precision.HIGHEST
    count_rows = bin_tokens.shape[0]
    segment = segment_of(bin_lengths, count_rows)
    allowed = segment[:, None] == segment[None, :]
    query = low(low_back(jnp.dot(bin_tokens, w_query, precision=highest) + b_query))
    keys = low(low_back(jnp.dot(bin_tokens, w_key, precision=highest)))
    values = low(low_back(jnp.dot(bin_tokens, w_value, precision=highest) + b_value))
    query_heads = query.reshape(count_rows, HEADS, HD)
    key_heads = keys.reshape(count_rows, HEADS, HD)
    value_heads = values.reshape(count_rows, HEADS, HD)
    scores = jnp.einsum('qhd,khd->hqk', query_heads, key_heads, precision=highest) * HD ** (-0.5)
    scores = low_back(scores)
    probs = jax.nn.softmax(jnp.where(allowed[None], scores, -1e+30), axis=-1)
    probs = low(probs)
    attn = jnp.einsum('hqk,khd->qhd', probs, value_heads, precision=highest).reshape(count_rows, D)
    attn = low(low_back(attn))
    branch = low_back(jnp.dot(attn, w_out, precision=highest) + b_out)
    hidden = layer_norm(bin_tokens + branch, gain_attn, shift_attn)
    inner = low_back(jnp.dot(low(hidden), w_inner, precision=highest) + b_inner)
    gelu_low = low(jax.nn.gelu(inner, approximate=False))
    ffn = low_back(jnp.dot(gelu_low, w_outer, precision=highest) + b_outer)
    return layer_norm(hidden + ffn, gain_ffn, shift_ffn)

def forward(params, packed, lengths):

    def bin_step(carry, item):
        return (carry, jax.checkpoint(bin_layer)(params, item[0], item[1]))
    unused, outputs = lax.scan(bin_step, None, (packed, lengths))
    return outputs

def reference(tokens, cotangent, block_route, lengths, w_query, w_key, w_value, b_query, b_value, w_out, b_out, gain_attn, shift_attn, w_inner, b_inner, w_outer, b_outer, gain_ffn, shift_ffn):
    bin_count = lengths.shape[0]
    shape_all = tokens.shape
    packed = jnp.zeros(shape_all, jnp.float32).at[block_route].set(tokens.astype(jnp.float32))
    packed = packed.reshape(bin_count, BIN, D)
    grad_packed = jnp.zeros(shape_all, jnp.float32).at[block_route].set(cotangent.astype(jnp.float32))
    grad_packed = grad_packed.reshape(bin_count, BIN, D)
    params = (w_query.astype(jnp.float32), w_key.astype(jnp.float32), w_value.astype(jnp.float32), b_query.astype(jnp.float32).reshape(D), b_value.astype(jnp.float32).reshape(D), w_out.astype(jnp.float32), b_out.astype(jnp.float32), gain_attn.astype(jnp.float32), shift_attn.astype(jnp.float32), w_inner.astype(jnp.float32), b_inner.astype(jnp.float32).reshape(FF), w_outer.astype(jnp.float32), b_outer.astype(jnp.float32), gain_ffn.astype(jnp.float32), shift_ffn.astype(jnp.float32))
    result, pullback = jax.vjp(lambda prm, inputs: forward(prm, inputs, lengths), params, packed)
    grads, grad_inputs = pullback(grad_packed)
    layer_out = result.reshape(shape_all)[block_route].astype(jnp.bfloat16)
    grad_tokens = grad_inputs.reshape(shape_all)[block_route].astype(jnp.bfloat16)
    return (layer_out, grad_tokens, grads[0], grads[1], grads[2], grads[3].reshape(N_TENSOR, D // N_TENSOR), grads[4].reshape(N_TENSOR, D // N_TENSOR), grads[5], grads[6], grads[7], grads[8], grads[9], grads[10].reshape(N_TENSOR, FF // N_TENSOR), grads[11], grads[12], grads[13], grads[14])
```

```python
from functools import partial
import math

import jax
import jax.numpy as jnp
from jax import lax
from jax.experimental import pallas as pl
from jax.experimental.pallas import tpu as pltpu
from jax.sharding import PartitionSpec as P

HEADS = 12
HD = 64


EPS_NORM = 1e-12


def layer_norm(residual, norm_gain, norm_shift):
    centre = residual - jnp.mean(residual, axis=-1, keepdims=True)
    spread = lax.rsqrt(jnp.mean(centre * centre, axis=-1, keepdims=True) + EPS_NORM)
    normed = centre * spread
    return (normed * norm_gain + norm_shift, normed, spread)


def norm_back(grad_out, normed, spread, norm_gain):
    scaled = grad_out * norm_gain
    inner_term = (
        scaled
        - jnp.mean(scaled, axis=-1, keepdims=True)
        - normed * jnp.mean(scaled * normed, axis=-1, keepdims=True)
    )
    return (inner_term * spread, jnp.sum(grad_out * normed, axis=0), jnp.sum(grad_out, axis=0))


def segment_of(seq_lengths, count_rows):
    seq_ends = jnp.cumsum(seq_lengths)
    positions = jnp.arange(count_rows, dtype=jnp.int32)
    return jnp.sum((positions[:, None] >= seq_ends[None, :-1]).astype(jnp.int32), axis=1)


def masked_scores(query_block, key_heads, segment, first_row, block_rows, score_scale):
    scores = (
        jnp.einsum("qhd,khd->hqk", query_block, key_heads, preferred_element_type=jnp.float32)
        * score_scale
    )
    allowed = segment[first_row : first_row + block_rows, None] == segment[None, :]
    return jnp.where(allowed[None], scores, -1e30)


def attend_forward(query_heads, key_heads, value_heads, segment, block_rows, score_scale):
    scores = masked_scores(query_heads, key_heads, segment, 0, block_rows, score_scale)
    row_peak = jnp.max(scores, axis=-1, keepdims=True)
    exp_scores = jnp.exp(scores - row_peak)
    row_total = jnp.sum(exp_scores, axis=-1, keepdims=True)
    prob_low = (exp_scores / row_total).astype(jnp.bfloat16)
    out_block = jnp.einsum(
        "hqk,khd->qhd", prob_low, value_heads, preferred_element_type=jnp.float32
    )
    out_rows = out_block.astype(jnp.bfloat16)
    lse_rows = row_peak + jnp.log(row_total)
    return (out_rows, lse_rows)


def attend_backward(
    query_heads, key_heads, value_heads, grad_heads, log_totals, segment, block_rows, score_scale
):
    scores = masked_scores(query_heads, key_heads, segment, 0, block_rows, score_scale)
    probs_full = jnp.exp(scores - log_totals)
    prob_low = probs_full.astype(jnp.bfloat16)
    grad_values = jnp.einsum(
        "hqk,qhd->khd", prob_low, grad_heads, preferred_element_type=jnp.float32
    )
    grad_probs = jnp.einsum(
        "qhd,khd->hqk", grad_heads, value_heads, preferred_element_type=jnp.float32
    )
    row_inner = jnp.sum(probs_full * grad_probs, axis=-1, keepdims=True)
    grad_scores = (probs_full * (grad_probs - row_inner)).astype(jnp.bfloat16)
    grad_query_rows = (
        jnp.einsum("hqk,khd->qhd", grad_scores, key_heads, preferred_element_type=jnp.float32)
        * score_scale
    )
    grad_keys = (
        jnp.einsum("hqk,qhd->khd", grad_scores, query_heads, preferred_element_type=jnp.float32)
        * score_scale
    )
    return (grad_query_rows, grad_keys, grad_values)


MESH = pl.DeviceIdType.MESH


def flip(place, bit):
    return place + bit * (1 - 2 * ((place // bit) % 2))


def bit_of(place, bit):
    return (place // bit) % 2


def orders_of(count):
    bits = [1 << i for i in range(count.bit_length() - 1)][::-1]
    return (tuple(bits), tuple(bits[:-2] + bits[-2:][::-1]))


def greet(dp_count, place, half):
    barrier = pltpu.get_barrier_semaphore()

    def hello(step, carry):
        peer = lax.rem(place + step, dp_count)
        pl.semaphore_signal(barrier, inc=1, device_id=(peer, half), device_id_type=MESH)
        return carry

    lax.fori_loop(1, dp_count, hello, 0)
    pl.semaphore_wait(barrier, dp_count - 1)


def exchange_start(dp_count, place, half, send_ref, recv_ref, send_sem, recv_sem):
    def push(step, carry):
        peer = lax.rem(place + step, dp_count)
        pltpu.make_async_remote_copy(
            src_ref=send_ref.at[peer],
            dst_ref=recv_ref.at[place],
            send_sem=send_sem.at[step],
            recv_sem=recv_sem.at[step],
            device_id=(peer, half),
            device_id_type=MESH,
        ).start()
        return carry

    lax.fori_loop(1, dp_count, push, 0)


def exchange_wait(dp_count, place, half, send_ref, recv_ref, send_sem, recv_sem):
    def settle(step, carry):
        source = lax.rem(place + dp_count - step, dp_count)
        pltpu.make_async_remote_copy(
            src_ref=send_ref.at[source],
            dst_ref=recv_ref.at[source],
            send_sem=send_sem.at[step],
            recv_sem=recv_sem.at[step],
            device_id=(source, half),
            device_id_type=MESH,
        ).wait()
        return carry

    lax.fori_loop(1, dp_count, settle, 0)


def copy_block(send_ref, recv_ref, place):
    recv_ref[place] = send_ref[place]


class Gather:
    def __init__(self, dp_count, place, half, order, ref, start, size, send_sem, recv_sem):
        self.place, self.half, self.order = place, half, order
        self.bits = [1 << i for i in range(dp_count.bit_length() - 1)][::-1]
        self.ref, self.cols = ref, pl.ds(start, size)
        self.send_sem, self.recv_sem = send_sem, recv_sem

    def copy(self, stage):
        done = self.order[:stage]
        index = tuple(
            slice(None) if bit in done else bit_of(self.place, bit) for bit in self.bits
        ) + (slice(None), self.cols)
        return pltpu.make_async_remote_copy(
            src_ref=self.ref.at[index],
            dst_ref=self.ref.at[index],
            send_sem=self.send_sem.at[stage],
            recv_sem=self.recv_sem.at[stage],
            device_id=(flip(self.place, self.order[stage]), self.half),
            device_id_type=MESH,
        )

    def start(self, stage):
        self.copy(stage).start()

    def wait_recv(self, stage):
        self.copy(stage).wait_recv()

    def wait_send(self, stage):
        self.copy(stage).wait_send()


class Scatter:
    def __init__(self, dp_count, place, half, order, ref, start, size, landing, send_sem, recv_sem):
        self.place, self.half = place, half
        self.order = order[::-1]
        self.bits = [1 << i for i in range(dp_count.bit_length() - 1)][::-1]
        self.ref, self.start_col, self.size = ref, start, size
        self.landing = landing
        self.send_sem, self.recv_sem = send_sem, recv_sem

    def view(self, stage, chosen):
        left = [bit for bit in self.bits if bit not in self.order[:stage]]
        own = bit_of(self.place, self.order[stage])
        index = tuple(
            (own if chosen == "own" else 1 - own) if bit == self.order[stage] else slice(None)
            for bit in left
        )
        if stage == 0:
            return self.ref.at[index + (slice(None), pl.ds(self.start_col, self.size))]
        return self.landing[stage - 1].at[index]

    def copy(self, stage):
        return pltpu.make_async_remote_copy(
            src_ref=self.view(stage, "other"),
            dst_ref=self.landing[stage],
            send_sem=self.send_sem.at[stage],
            recv_sem=self.recv_sem.at[stage],
            device_id=(flip(self.place, self.order[stage]), self.half),
            device_id_type=MESH,
        )

    def start(self, stage):
        self.copy(stage).start()

    def wait_recv(self, stage):
        self.copy(stage).wait_recv()

    def wait_send(self, stage):
        self.copy(stage).wait_send()

    def add(self, stage, out_ref=None):
        kept = self.view(stage, "own")
        land = self.landing[stage]
        lead = land.shape[:-2]
        count = math.prod(lead)

        def one(i, carry):
            index, rest = [], i
            for extent in lead[::-1]:
                index.append(lax.rem(rest, extent))
                rest = rest // extent
            index = tuple(index[::-1])
            total = kept[index].astype(jnp.float32) + land[index].astype(jnp.float32)
            land[index] = total.astype(land.dtype)
            return carry

        if out_ref is not None:
            out_ref[:, pl.ds(self.start_col, self.size)] = kept[...].astype(
                jnp.float32
            ) + land[...].astype(jnp.float32)
        elif count == 1:
            one(0, 0)
        else:
            lax.fori_loop(0, count, one, 0)


def bring_in(
    dp_count,
    plan,
    x_ref,
    dy_ref,
    w_ref,
    v_ref,
    xr_ref,
    dyr_ref,
    full_ref,
    vec_ref,
    vec_buf,
    vec_land,
    x_sems,
    dy_sems,
    w_sems,
    v_sems,
):
    place, half = lax.axis_index("dp"), lax.axis_index("tensor")
    stages = dp_count.bit_length() - 1
    orders = orders_of(dp_count)
    bits = orders[0]
    own = tuple(bit_of(place, bit) for bit in bits)
    full_ref[own] = w_ref[...]
    vec_buf[0] = v_ref[...]
    greet(dp_count, place, half)
    gathers = [
        Gather(
            dp_count, place, half, orders[which], full_ref, start, size, w_sems.at[0, i], w_sems.at[1, i]
        )
        for i, (group, which, start, size) in enumerate(plan)
    ]
    groups = max(group for group, _, _, _ in plan) + 1
    exchange_start(dp_count, place, half, x_ref, xr_ref, x_sems.at[0], x_sems.at[1])

    def vec_copy(stage):
        return pltpu.make_async_remote_copy(
            src_ref=vec_buf.at[stage],
            dst_ref=vec_land.at[stage],
            send_sem=v_sems.at[0, stage],
            recv_sem=v_sems.at[1, stage],
            device_id=(flip(place, bits[stage]), half),
            device_id_type=MESH,
        )

    for step in range(groups + stages - 1):
        for (group, _, _, _), gather in zip(plan, gathers):
            stage = step - group
            if 0 <= stage < stages:
                if stage > 0:
                    gather.wait_recv(stage - 1)
                gather.start(stage)
        if step < stages:
            vec_copy(step).start()
            vec_copy(step).wait()
            if step < stages - 1:
                vec_buf[step + 1] = vec_buf[step] + vec_land[step]
            else:
                vec_ref[...] = vec_buf[step] + vec_land[step]
        if step == stages - 1:
            exchange_start(dp_count, place, half, dy_ref, dyr_ref, dy_sems.at[0], dy_sems.at[1])
    copy_block(x_ref, xr_ref, place)
    copy_block(dy_ref, dyr_ref, place)
    for gather in gathers:
        gather.wait_recv(stages - 1)
    for gather in gathers:
        for stage in range(stages):
            gather.wait_send(stage)
    exchange_wait(dp_count, place, half, x_ref, xr_ref, x_sems.at[0], x_sems.at[1])
    exchange_wait(dp_count, place, half, dy_ref, dyr_ref, dy_sems.at[0], dy_sems.at[1])


def send_out(
    dp_count,
    plan,
    out_ref,
    gx_ref,
    g_ref,
    v_ref,
    back_ref,
    gback_ref,
    sum_ref,
    vec_ref,
    *scratch,
):
    stages = dp_count.bit_length() - 1
    landings, rest = scratch[: len(plan) * stages], scratch[len(plan) * stages :]
    vec_buf, vec_land, x_sems, dy_sems, w_sems, v_sems = rest
    place, half = lax.axis_index("dp"), lax.axis_index("tensor")
    orders = orders_of(dp_count)
    bits = orders[0]
    vec_buf[0] = v_ref[...]
    greet(dp_count, place, half)
    scatters = [
        Scatter(
            dp_count,
            place,
            half,
            orders[which],
            g_ref,
            start,
            size,
            landings[i * stages : (i + 1) * stages],
            w_sems.at[0, i],
            w_sems.at[1, i],
        )
        for i, (group, which, start, size) in enumerate(plan)
    ]
    groups = max(group for group, _, _, _ in plan) + 1
    exchange_start(dp_count, place, half, out_ref, back_ref, x_sems.at[0], x_sems.at[1])

    def vec_copy(stage):
        return pltpu.make_async_remote_copy(
            src_ref=vec_buf.at[stage],
            dst_ref=vec_land.at[stage],
            send_sem=v_sems.at[0, stage],
            recv_sem=v_sems.at[1, stage],
            device_id=(flip(place, bits[stage]), half),
            device_id_type=MESH,
        )

    for step in range(groups + stages):
        for (group, _, _, _), scatter in zip(plan, scatters):
            stage = step - group
            if 0 <= stage <= stages:
                if stage > 0:
                    scatter.wait_recv(stage - 1)
                    scatter.add(stage - 1, sum_ref if stage == stages else None)
                if stage < stages:
                    scatter.start(stage)
        if step < stages:
            vec_copy(step).start()
            vec_copy(step).wait()
            if step < stages - 1:
                vec_buf[step + 1] = vec_buf[step] + vec_land[step]
            else:
                vec_ref[...] = vec_buf[step] + vec_land[step]
        if step == stages - 1:
            exchange_start(dp_count, place, half, gx_ref, gback_ref, dy_sems.at[0], dy_sems.at[1])
    copy_block(out_ref, back_ref, place)
    copy_block(gx_ref, gback_ref, place)
    for scatter in scatters:
        for stage in range(stages):
            scatter.wait_send(stage)
    exchange_wait(dp_count, place, half, out_ref, back_ref, x_sems.at[0], x_sems.at[1])
    exchange_wait(dp_count, place, half, gx_ref, gback_ref, dy_sems.at[0], dy_sems.at[1])


def plan_of(columns, groups):
    size = columns // (2 * groups)
    return [
        (group, which, (2 * group + which) * size, size) for group in range(groups) for which in range(2)
    ]


def call_bring_in(dp_count, tokens_by, grads_by, shard, vectors):
    bits = (2,) * (dp_count.bit_length() - 1)
    stages = len(bits)
    plan = plan_of(shard.shape[1], 3)
    spec = pl.BlockSpec(memory_space=pltpu.VMEM)
    dma = pltpu.SemaphoreType.DMA
    return pl.pallas_call(
        partial(bring_in, dp_count, plan),
        out_shape=(
            jax.ShapeDtypeStruct(tokens_by.shape, tokens_by.dtype),
            jax.ShapeDtypeStruct(grads_by.shape, grads_by.dtype),
            jax.ShapeDtypeStruct(bits + shard.shape, shard.dtype),
            jax.ShapeDtypeStruct(vectors.shape, vectors.dtype),
        ),
        in_specs=[spec] * 4,
        out_specs=[spec] * 4,
        scratch_shapes=[
            pltpu.VMEM((stages,) + vectors.shape, vectors.dtype),
            pltpu.VMEM((stages,) + vectors.shape, vectors.dtype),
            dma((2, dp_count)),
            dma((2, dp_count)),
            dma((2, len(plan), stages)),
            dma((2, stages)),
        ],
        compiler_params=pltpu.CompilerParams(
            collective_id=0, has_side_effects=True, vmem_limit_bytes=40 << 20
        ),
        name="bring_in",
    )(tokens_by, grads_by, shard, vectors)


def call_send_out(dp_count, out_by, gx_by, grads, vectors):
    bits = (2,) * (dp_count.bit_length() - 1)
    stages = len(bits)
    plan = plan_of(grads.shape[-1], 3)
    rows = grads.shape[-2]
    spec = pl.BlockSpec(memory_space=pltpu.VMEM)
    dma = pltpu.SemaphoreType.DMA
    landings = [
        pltpu.VMEM((2,) * (stages - 1 - stage) + (rows, size), grads.dtype)
        for _, _, _, size in plan
        for stage in range(stages)
    ]
    return pl.pallas_call(
        partial(send_out, dp_count, plan),
        out_shape=(
            jax.ShapeDtypeStruct(out_by.shape, out_by.dtype),
            jax.ShapeDtypeStruct(gx_by.shape, gx_by.dtype),
            jax.ShapeDtypeStruct((rows, grads.shape[-1]), jnp.float32),
            jax.ShapeDtypeStruct(vectors.shape, vectors.dtype),
        ),
        in_specs=[spec] * 4,
        out_specs=[spec] * 4,
        scratch_shapes=landings
        + [
            pltpu.VMEM((stages,) + vectors.shape, vectors.dtype),
            pltpu.VMEM((stages,) + vectors.shape, vectors.dtype),
            dma((2, dp_count)),
            dma((2, dp_count)),
            dma((2, len(plan), stages)),
            dma((2, stages)),
        ],
        compiler_params=pltpu.CompilerParams(
            collective_id=1, has_side_effects=True, vmem_limit_bytes=40 << 20
        ),
        name="send_out",
    )(out_by, gx_by, grads, vectors)


def segment_at(seq_lengths, places, half_rows):
    seq_ends = jnp.cumsum(seq_lengths)
    within = jnp.arange(2 * half_rows, dtype=jnp.int32)
    positions = (places[:, None] * (2 * half_rows) + within[None, :]).reshape(-1)
    return jnp.sum((positions[:, None] >= seq_ends[None, :-1]).astype(jnp.int32), axis=1)


def shards_fast(
    tokens,
    cotangent,
    block_route,
    lengths,
    w_query,
    w_key,
    w_value,
    b_query,
    b_value,
    w_out,
    b_out,
    gain_attn,
    shift_attn,
    w_inner,
    b_inner,
    w_outer,
    b_outer,
    gain_ffn,
    shift_ffn,
):
    dp_count = lax.axis_size("dp")
    micro_count = lengths.shape[0]
    half_rows = tokens.shape[1]
    model_width = tokens.shape[2]
    half_width = w_query.shape[1]
    ff_half = w_inner.shape[1]
    local_heads = HEADS // lax.axis_size("tensor")
    score_scale = HD ** (-0.5)
    place = lax.axis_index("dp")
    blocks = tokens.reshape(micro_count, dp_count, half_rows, model_width)
    upstream = cotangent.reshape(micro_count, dp_count, half_rows, model_width)
    target = block_route.reshape(micro_count, dp_count)
    dest_dev = target // (micro_count * dp_count)
    inverse = jnp.argmax(
        dest_dev[:, None, :] == jnp.arange(dp_count, dtype=jnp.int32)[None, :, None], axis=2
    )
    by_dest = jnp.take_along_axis(blocks, inverse[:, :, None, None], axis=1).swapaxes(0, 1)
    grad_dest = jnp.take_along_axis(upstream, inverse[:, :, None, None], axis=1).swapaxes(0, 1)
    shard = jnp.concatenate([w_query, w_key, w_value, w_out.T, w_inner, w_outer.T], axis=1)
    own_width = model_width // dp_count
    six = jnp.stack([b_out, gain_attn, shift_attn, b_outer, gain_ffn, shift_ffn]).astype(jnp.float32)
    vectors = jnp.zeros((16, model_width), jnp.float32)
    vectors = lax.dynamic_update_slice(vectors, six, (jnp.int32(0), place * own_width))
    own_inner = b_inner.shape[1]
    bias_row = lax.dynamic_update_slice(
        jnp.zeros((1, ff_half), jnp.float32), b_inner.astype(jnp.float32), (jnp.int32(0), place * own_inner)
    ).reshape(2, model_width)
    vectors = lax.dynamic_update_slice(vectors, bias_row, (jnp.int32(6), jnp.int32(0)))
    vectors = lax.dynamic_update_slice(
        vectors,
        block_route.astype(jnp.float32)[None],
        (jnp.int32(8), place * (micro_count * dp_count)),
    )
    xr, dyr, full, vec = call_bring_in(dp_count, by_dest, grad_dest, shard, vectors)
    route = vec[8].astype(jnp.int32).reshape(dp_count, micro_count, dp_count)
    mine = (route // (micro_count * dp_count)) == place
    arrived_place = jnp.sum(jnp.where(mine, route % dp_count, 0), axis=2).T
    full = full.reshape(model_width, -1)
    full_query, full_key, full_value, full_out, full_inner, full_outer = jnp.split(
        full, [half_width, 2 * half_width, 3 * half_width, 4 * half_width, 4 * half_width + ff_half], axis=1
    )
    full_out, full_outer = full_out.T, full_outer.T
    bias_out, full_gain_attn, full_shift_attn, bias_outer, full_gain_ffn, full_shift_ffn = vec[:6]
    bias_inner = vec[6:8].reshape(1, ff_half)
    bin_tokens = xr.swapaxes(0, 1)
    bin_grads = dyr.swapaxes(0, 1)
    acc_query = jnp.zeros((model_width, half_width), jnp.float32)
    acc_key = acc_value = acc_query
    acc_out = jnp.zeros((half_width, model_width), jnp.float32)
    acc_inner = jnp.zeros((model_width, ff_half), jnp.float32)
    acc_outer = jnp.zeros((ff_half, model_width), jnp.float32)
    acc_bias_query = jnp.zeros((1, half_width), jnp.float32)
    acc_bias_value = acc_bias_query
    acc_bias_inner = jnp.zeros((1, ff_half), jnp.float32)
    acc_vectors = jnp.zeros((6, model_width), jnp.float32)
    out_bins = []
    grad_bins = []
    for micro_step in range(micro_count):
        own_rows = bin_tokens[micro_step]
        whole_bin = lax.all_gather(own_rows, "tensor", axis=1, tiled=True).reshape(-1, model_width)
        bin_rows = whole_bin.shape[0]
        block_rows = math.gcd(bin_rows, 512)
        segment = segment_at(lengths[micro_step], arrived_place[micro_step], half_rows)
        query = (
            jnp.dot(whole_bin, full_query, preferred_element_type=jnp.float32) + b_query[0]
        ).astype(jnp.bfloat16)
        keys = jnp.dot(whole_bin, full_key, preferred_element_type=jnp.float32).astype(jnp.bfloat16)
        values = (
            jnp.dot(whole_bin, full_value, preferred_element_type=jnp.float32) + b_value[0]
        ).astype(jnp.bfloat16)
        query_heads = query.reshape(bin_rows, local_heads, HD)
        key_heads = keys.reshape(bin_rows, local_heads, HD)
        value_heads = values.reshape(bin_rows, local_heads, HD)
        attn_heads, log_totals = attend_forward(
            query_heads, key_heads, value_heads, segment, block_rows, score_scale
        )
        attn = attn_heads.reshape(bin_rows, local_heads * HD)
        attn_partial = jnp.dot(attn, full_out, preferred_element_type=jnp.float32).reshape(
            dp_count, -1, model_width
        )
        branch = lax.psum_scatter(attn_partial, "tensor", scatter_dimension=1, tiled=True).reshape(
            -1, model_width
        )
        mid = own_rows.reshape(-1, model_width).astype(jnp.float32) + branch + bias_out
        hidden, normed_attn, spread_attn = layer_norm(mid, full_gain_attn, full_shift_attn)
        hidden_low = hidden.astype(jnp.bfloat16).reshape(dp_count, half_rows, model_width)
        hidden_whole = lax.all_gather(hidden_low, "tensor", axis=1, tiled=True).reshape(
            -1, model_width
        )
        inner = (
            jnp.dot(hidden_whole, full_inner, preferred_element_type=jnp.float32) + bias_inner[0]
        )
        gelu_value, gelu_pull = jax.vjp(partial(jax.nn.gelu, approximate=False), inner)
        gelu_low = gelu_value.astype(jnp.bfloat16)
        ffn_partial = jnp.dot(gelu_low, full_outer, preferred_element_type=jnp.float32).reshape(
            dp_count, -1, model_width
        )
        ffn = lax.psum_scatter(ffn_partial, "tensor", scatter_dimension=1, tiled=True).reshape(
            -1, model_width
        )
        top = hidden + ffn + bias_outer
        result, normed_ffn, spread_ffn = layer_norm(top, full_gain_ffn, full_shift_ffn)
        out_bins.append(result.astype(jnp.bfloat16).reshape(dp_count, half_rows, model_width))
        back_query, back_key, back_value, back_out, back_inner, back_outer = full_query, full_key, full_value, full_out, full_inner, full_outer
        back_gain_attn, back_gain_ffn = full_gain_attn, full_gain_ffn
        grad_result = bin_grads[micro_step].reshape(-1, model_width).astype(jnp.float32)
        grad_top, grad_gain_ffn, grad_shift_ffn = norm_back(
            grad_result, normed_ffn, spread_ffn, back_gain_ffn
        )
        grad_ffn_low = grad_top.astype(jnp.bfloat16)
        grad_bias_outer = jnp.sum(grad_ffn_low.astype(jnp.float32), axis=0)
        grad_ffn_whole = lax.all_gather(
            grad_ffn_low.reshape(dp_count, half_rows, model_width), "tensor", axis=1, tiled=True
        ).reshape(-1, model_width)
        acc_outer = acc_outer + jnp.einsum(
            "nf,nd->fd", gelu_low, grad_ffn_whole, preferred_element_type=jnp.float32
        )
        grad_gelu = jnp.einsum(
            "nd,fd->nf", grad_ffn_whole, back_outer, preferred_element_type=jnp.float32
        )
        grad_inner_low = gelu_pull(grad_gelu)[0].astype(jnp.bfloat16)
        acc_bias_inner = acc_bias_inner + jnp.sum(grad_inner_low.astype(jnp.float32), axis=0)[None]
        acc_inner = acc_inner + jnp.einsum(
            "nd,nf->df", hidden_whole, grad_inner_low, preferred_element_type=jnp.float32
        )
        hidden_partial = jnp.einsum(
            "nf,df->nd", grad_inner_low, back_inner, preferred_element_type=jnp.float32
        ).reshape(dp_count, -1, model_width)
        grad_hidden = grad_top + lax.psum_scatter(
            hidden_partial, "tensor", scatter_dimension=1, tiled=True
        ).reshape(-1, model_width)
        grad_mid, grad_gain_attn, grad_shift_attn = norm_back(
            grad_hidden, normed_attn, spread_attn, back_gain_attn
        )
        grad_branch_low = grad_mid.astype(jnp.bfloat16)
        grad_bias_out = jnp.sum(grad_branch_low.astype(jnp.float32), axis=0)
        grad_branch_whole = lax.all_gather(
            grad_branch_low.reshape(dp_count, half_rows, model_width), "tensor", axis=1, tiled=True
        ).reshape(-1, model_width)
        acc_out = acc_out + jnp.einsum(
            "nh,nd->hd", attn, grad_branch_whole, preferred_element_type=jnp.float32
        )
        grad_attn_low = jnp.einsum(
            "nd,hd->nh", grad_branch_whole, back_out, preferred_element_type=jnp.float32
        ).astype(jnp.bfloat16)
        grad_heads = grad_attn_low.reshape(bin_rows, local_heads, HD)
        grad_query, grad_keys, grad_values = attend_backward(
            query_heads,
            key_heads,
            value_heads,
            grad_heads,
            log_totals,
            segment,
            block_rows,
            score_scale,
        )
        grad_query_low = grad_query.reshape(bin_rows, -1).astype(jnp.bfloat16)
        grad_key_low = grad_keys.reshape(bin_rows, -1).astype(jnp.bfloat16)
        grad_value_low = grad_values.reshape(bin_rows, -1).astype(jnp.bfloat16)
        acc_bias_query = acc_bias_query + jnp.sum(grad_query_low.astype(jnp.float32), axis=0)[None]
        acc_bias_value = acc_bias_value + jnp.sum(grad_value_low.astype(jnp.float32), axis=0)[None]
        acc_query = acc_query + jnp.einsum(
            "nd,nh->dh", whole_bin, grad_query_low, preferred_element_type=jnp.float32
        )
        acc_key = acc_key + jnp.einsum(
            "nd,nh->dh", whole_bin, grad_key_low, preferred_element_type=jnp.float32
        )
        acc_value = acc_value + jnp.einsum(
            "nd,nh->dh", whole_bin, grad_value_low, preferred_element_type=jnp.float32
        )
        input_partial = (
            jnp.einsum("nh,dh->nd", grad_query_low, back_query, preferred_element_type=jnp.float32)
            + jnp.einsum("nh,dh->nd", grad_key_low, back_key, preferred_element_type=jnp.float32)
            + jnp.einsum(
                "nh,dh->nd", grad_value_low, back_value, preferred_element_type=jnp.float32
            )
        )
        grad_input = grad_mid + lax.psum_scatter(
            input_partial.reshape(dp_count, -1, model_width).astype(jnp.bfloat16),
            "tensor",
            scatter_dimension=1,
            tiled=True,
        ).astype(jnp.float32).reshape(-1, model_width)
        grad_bins.append(grad_input.astype(jnp.bfloat16).reshape(dp_count, half_rows, model_width))
        acc_vectors = acc_vectors + jnp.stack(
            [
                grad_bias_out,
                grad_gain_attn,
                grad_shift_attn,
                grad_bias_outer,
                grad_gain_ffn,
                grad_shift_ffn,
            ]
        )
    out_by = jnp.stack(out_bins, axis=1)
    gx_by = jnp.stack(grad_bins, axis=1)
    grads = jnp.concatenate(
        [acc_query, acc_key, acc_value, acc_out.T, acc_inner, acc_outer.T], axis=1
    ).astype(jnp.bfloat16)
    bits = (2,) * (dp_count.bit_length() - 1)
    small = jnp.concatenate(
        [
            acc_vectors,
            acc_bias_inner.reshape(2, model_width),
            jnp.concatenate([acc_bias_query, acc_bias_value], axis=1),
            jnp.zeros((7, model_width), jnp.float32),
        ],
        axis=0,
    )
    back, gback, sums, total = call_send_out(
        dp_count, out_by, gx_by, grads.reshape(bits + (own_width, grads.shape[1])), small
    )
    vec_own = lax.dynamic_slice_in_dim(
        lax.psum(total[:6], "tensor"), place * own_width, own_width, 1
    )
    sum_bias_inner = lax.dynamic_slice_in_dim(
        total[6:8].reshape(1, ff_half), place * own_inner, own_inner, 1
    )
    bias_qv = total[8:9]
    layer_out = jnp.take_along_axis(
        back.swapaxes(0, 1), dest_dev[:, :, None, None], axis=1
    ).reshape(tokens.shape)
    grad_tokens = jnp.take_along_axis(
        gback.swapaxes(0, 1), dest_dev[:, :, None, None], axis=1
    ).reshape(tokens.shape)
    sum_query, sum_key, sum_value, sum_out, sum_inner, sum_outer = jnp.split(
        sums, [half_width, 2 * half_width, 3 * half_width, 4 * half_width, 4 * half_width + ff_half], axis=1
    )
    return (
        layer_out,
        grad_tokens,
        sum_query,
        sum_key,
        sum_value,
        bias_qv[:, :half_width],
        bias_qv[:, half_width:],
        sum_out.T,
        vec_own[0],
        vec_own[1],
        vec_own[2],
        sum_inner,
        sum_bias_inner,
        sum_outer.T,
        vec_own[3],
        vec_own[4],
        vec_own[5],
    )


def shards(
    tokens,
    cotangent,
    block_route,
    lengths,
    w_query,
    w_key,
    w_value,
    b_query,
    b_value,
    w_out,
    b_out,
    gain_attn,
    shift_attn,
    w_inner,
    b_inner,
    w_outer,
    b_outer,
    gain_ffn,
    shift_ffn,
):
    dp_count = lax.axis_size("dp")
    micro_count = lengths.shape[0]
    half_rows = tokens.shape[1]
    model_width = tokens.shape[2]
    local_heads = HEADS // lax.axis_size("tensor")
    score_scale = HD ** (-0.5)
    blocks = tokens.reshape(micro_count, dp_count, half_rows, model_width)
    upstream = cotangent.reshape(micro_count, dp_count, half_rows, model_width)
    target = block_route.reshape(micro_count, dp_count)
    dest_dev = target // (micro_count * dp_count)
    bin_place = target % dp_count
    micro_ids = jnp.broadcast_to(
        jnp.arange(micro_count, dtype=jnp.int32)[:, None], (micro_count, dp_count)
    )
    slot_ids = jnp.broadcast_to(
        jnp.arange(dp_count, dtype=jnp.int32)[None, :], (micro_count, dp_count)
    )
    inverse = jnp.zeros((micro_count, dp_count), jnp.int32).at[micro_ids, dest_dev].set(slot_ids)
    by_dest = jnp.take_along_axis(blocks, inverse[:, :, None, None], axis=1)
    grad_dest = jnp.take_along_axis(upstream, inverse[:, :, None, None], axis=1)
    place_dest = jnp.take_along_axis(bin_place, inverse, axis=1)
    arrived, arrived_grad, arrived_place = (
        lax.all_to_all(by_dest, "dp", split_axis=1, concat_axis=1, tiled=True),
        lax.all_to_all(grad_dest, "dp", split_axis=1, concat_axis=1, tiled=True),
        lax.all_to_all(place_dest, "dp", split_axis=1, concat_axis=1, tiled=True),
    )
    anchor = (
        jnp.zeros((micro_count, dp_count), jnp.int32).at[micro_ids, arrived_place].set(slot_ids)
    )
    bin_tokens = jnp.take_along_axis(arrived, anchor[:, :, None, None], axis=1)
    bin_grads = jnp.take_along_axis(arrived_grad, anchor[:, :, None, None], axis=1)
    acc_query = jnp.zeros((model_width, w_query.shape[1]), jnp.float32)
    acc_key = jnp.zeros((model_width, w_key.shape[1]), jnp.float32)
    acc_value = jnp.zeros((model_width, w_value.shape[1]), jnp.float32)
    acc_out = jnp.zeros((w_out.shape[0], model_width), jnp.float32)
    acc_inner = jnp.zeros((model_width, w_inner.shape[1]), jnp.float32)
    acc_outer = jnp.zeros((w_outer.shape[0], model_width), jnp.float32)
    acc_bias_query = jnp.zeros((1, w_query.shape[1]), jnp.float32)
    acc_bias_value = jnp.zeros((1, w_value.shape[1]), jnp.float32)
    acc_bias_inner = jnp.zeros((1, w_inner.shape[1]), jnp.float32)
    acc_vectors = jnp.zeros((6, model_width), jnp.float32)
    out_bins = []
    grad_bins = []
    for micro_step in range(micro_count):
        gathered = (
            lax.all_gather(w_query, "dp", axis=0, tiled=True),
            lax.all_gather(w_key, "dp", axis=0, tiled=True),
            lax.all_gather(w_value, "dp", axis=0, tiled=True),
            lax.all_gather(w_out, "dp", axis=1, tiled=True),
            lax.all_gather(w_inner, "dp", axis=0, tiled=True),
            lax.all_gather(w_outer, "dp", axis=1, tiled=True),
            lax.all_gather(b_inner, "dp", axis=1, tiled=True),
            lax.all_gather(b_out, "dp", axis=0, tiled=True),
            lax.all_gather(gain_attn, "dp", axis=0, tiled=True),
            lax.all_gather(shift_attn, "dp", axis=0, tiled=True),
            lax.all_gather(b_outer, "dp", axis=0, tiled=True),
            lax.all_gather(gain_ffn, "dp", axis=0, tiled=True),
            lax.all_gather(shift_ffn, "dp", axis=0, tiled=True),
        )
        (
            full_query,
            full_key,
            full_value,
            full_out,
            full_inner,
            full_outer,
            bias_inner,
            bias_out,
            full_gain_attn,
            full_shift_attn,
            bias_outer,
            full_gain_ffn,
            full_shift_ffn,
        ) = gathered
        own_rows = bin_tokens[micro_step]
        whole_bin = lax.all_gather(own_rows, "tensor", axis=1, tiled=True).reshape(-1, model_width)
        bin_rows = whole_bin.shape[0]
        block_rows = math.gcd(bin_rows, 512)
        segment = segment_of(lengths[micro_step], bin_rows)
        query = (
            jnp.dot(whole_bin, full_query, preferred_element_type=jnp.float32) + b_query[0]
        ).astype(jnp.bfloat16)
        keys = jnp.dot(whole_bin, full_key, preferred_element_type=jnp.float32).astype(jnp.bfloat16)
        values = (
            jnp.dot(whole_bin, full_value, preferred_element_type=jnp.float32) + b_value[0]
        ).astype(jnp.bfloat16)
        query_heads = query.reshape(bin_rows, local_heads, HD)
        key_heads = keys.reshape(bin_rows, local_heads, HD)
        value_heads = values.reshape(bin_rows, local_heads, HD)
        attn_heads, log_totals = attend_forward(
            query_heads, key_heads, value_heads, segment, block_rows, score_scale
        )
        attn = attn_heads.reshape(bin_rows, local_heads * HD)
        attn_partial = jnp.dot(attn, full_out, preferred_element_type=jnp.float32).reshape(
            dp_count, -1, model_width
        )
        branch = lax.psum_scatter(attn_partial, "tensor", scatter_dimension=1, tiled=True).reshape(
            -1, model_width
        )
        mid = own_rows.reshape(-1, model_width).astype(jnp.float32) + branch + bias_out
        hidden, normed_attn, spread_attn = layer_norm(mid, full_gain_attn, full_shift_attn)
        hidden_low = hidden.astype(jnp.bfloat16).reshape(dp_count, half_rows, model_width)
        hidden_whole = lax.all_gather(hidden_low, "tensor", axis=1, tiled=True).reshape(
            -1, model_width
        )
        inner = (
            jnp.dot(hidden_whole, full_inner, preferred_element_type=jnp.float32) + bias_inner[0]
        )
        gelu_value, gelu_pull = jax.vjp(partial(jax.nn.gelu, approximate=False), inner)
        gelu_low = gelu_value.astype(jnp.bfloat16)
        ffn_partial = jnp.dot(gelu_low, full_outer, preferred_element_type=jnp.float32).reshape(
            dp_count, -1, model_width
        )
        ffn = lax.psum_scatter(ffn_partial, "tensor", scatter_dimension=1, tiled=True).reshape(
            -1, model_width
        )
        top = hidden + ffn + bias_outer
        result, normed_ffn, spread_ffn = layer_norm(top, full_gain_ffn, full_shift_ffn)
        out_bins.append(result.astype(jnp.bfloat16).reshape(dp_count, half_rows, model_width))
        back_full = (
            lax.all_gather(w_query, "dp", axis=0, tiled=True),
            lax.all_gather(w_key, "dp", axis=0, tiled=True),
            lax.all_gather(w_value, "dp", axis=0, tiled=True),
            lax.all_gather(w_out, "dp", axis=1, tiled=True),
            lax.all_gather(w_inner, "dp", axis=0, tiled=True),
            lax.all_gather(w_outer, "dp", axis=1, tiled=True),
            lax.all_gather(gain_attn, "dp", axis=0, tiled=True),
            lax.all_gather(gain_ffn, "dp", axis=0, tiled=True),
        )
        (
            back_query,
            back_key,
            back_value,
            back_out,
            back_inner,
            back_outer,
            back_gain_attn,
            back_gain_ffn,
        ) = back_full
        grad_result = bin_grads[micro_step].reshape(-1, model_width).astype(jnp.float32)
        grad_top, grad_gain_ffn, grad_shift_ffn = norm_back(
            grad_result, normed_ffn, spread_ffn, back_gain_ffn
        )
        grad_ffn_low = grad_top.astype(jnp.bfloat16)
        grad_bias_outer = jnp.sum(grad_ffn_low.astype(jnp.float32), axis=0)
        grad_ffn_whole = lax.all_gather(
            grad_ffn_low.reshape(dp_count, half_rows, model_width), "tensor", axis=1, tiled=True
        ).reshape(-1, model_width)
        acc_outer = acc_outer + jnp.einsum(
            "nf,nd->fd", gelu_low, grad_ffn_whole, preferred_element_type=jnp.float32
        )
        grad_gelu = jnp.einsum(
            "nd,fd->nf", grad_ffn_whole, back_outer, preferred_element_type=jnp.float32
        )
        grad_inner_low = gelu_pull(grad_gelu)[0].astype(jnp.bfloat16)
        acc_bias_inner = acc_bias_inner + jnp.sum(grad_inner_low.astype(jnp.float32), axis=0)[None]
        acc_inner = acc_inner + jnp.einsum(
            "nd,nf->df", hidden_whole, grad_inner_low, preferred_element_type=jnp.float32
        )
        hidden_partial = jnp.einsum(
            "nf,df->nd", grad_inner_low, back_inner, preferred_element_type=jnp.float32
        ).reshape(dp_count, -1, model_width)
        grad_hidden = grad_top + lax.psum_scatter(
            hidden_partial, "tensor", scatter_dimension=1, tiled=True
        ).reshape(-1, model_width)
        grad_mid, grad_gain_attn, grad_shift_attn = norm_back(
            grad_hidden, normed_attn, spread_attn, back_gain_attn
        )
        grad_branch_low = grad_mid.astype(jnp.bfloat16)
        grad_bias_out = jnp.sum(grad_branch_low.astype(jnp.float32), axis=0)
        grad_branch_whole = lax.all_gather(
            grad_branch_low.reshape(dp_count, half_rows, model_width), "tensor", axis=1, tiled=True
        ).reshape(-1, model_width)
        acc_out = acc_out + jnp.einsum(
            "nh,nd->hd", attn, grad_branch_whole, preferred_element_type=jnp.float32
        )
        grad_attn_low = jnp.einsum(
            "nd,hd->nh", grad_branch_whole, back_out, preferred_element_type=jnp.float32
        ).astype(jnp.bfloat16)
        grad_heads = grad_attn_low.reshape(bin_rows, local_heads, HD)
        grad_query, grad_keys, grad_values = attend_backward(
            query_heads,
            key_heads,
            value_heads,
            grad_heads,
            log_totals,
            segment,
            block_rows,
            score_scale,
        )
        grad_query_low = grad_query.reshape(bin_rows, -1).astype(jnp.bfloat16)
        grad_key_low = grad_keys.reshape(bin_rows, -1).astype(jnp.bfloat16)
        grad_value_low = grad_values.reshape(bin_rows, -1).astype(jnp.bfloat16)
        acc_bias_query = acc_bias_query + jnp.sum(grad_query_low.astype(jnp.float32), axis=0)[None]
        acc_bias_value = acc_bias_value + jnp.sum(grad_value_low.astype(jnp.float32), axis=0)[None]
        acc_query = acc_query + jnp.einsum(
            "nd,nh->dh", whole_bin, grad_query_low, preferred_element_type=jnp.float32
        )
        acc_key = acc_key + jnp.einsum(
            "nd,nh->dh", whole_bin, grad_key_low, preferred_element_type=jnp.float32
        )
        acc_value = acc_value + jnp.einsum(
            "nd,nh->dh", whole_bin, grad_value_low, preferred_element_type=jnp.float32
        )
        input_partial = (
            jnp.einsum("nh,dh->nd", grad_query_low, back_query, preferred_element_type=jnp.float32)
            + jnp.einsum("nh,dh->nd", grad_key_low, back_key, preferred_element_type=jnp.float32)
            + jnp.einsum(
                "nh,dh->nd", grad_value_low, back_value, preferred_element_type=jnp.float32
            )
        )
        grad_input = grad_mid + lax.psum_scatter(
            input_partial.reshape(dp_count, -1, model_width).astype(jnp.bfloat16),
            "tensor",
            scatter_dimension=1,
            tiled=True,
        ).astype(jnp.float32).reshape(-1, model_width)
        grad_bins.append(grad_input.astype(jnp.bfloat16).reshape(dp_count, half_rows, model_width))
        acc_vectors = acc_vectors + jnp.stack(
            [
                grad_bias_out,
                grad_gain_attn,
                grad_shift_attn,
                grad_bias_outer,
                grad_gain_ffn,
                grad_shift_ffn,
            ]
        )
    out_stack = jnp.stack(out_bins)
    grad_stack = jnp.stack(grad_bins)
    send_out = jnp.take_along_axis(out_stack, arrived_place[:, :, None, None], axis=1)
    send_grad = jnp.take_along_axis(grad_stack, arrived_place[:, :, None, None], axis=1)
    back_out_rows, back_grad_rows = (
        lax.all_to_all(send_out, "dp", split_axis=1, concat_axis=1, tiled=True),
        lax.all_to_all(send_grad, "dp", split_axis=1, concat_axis=1, tiled=True),
    )
    layer_out = jnp.take_along_axis(back_out_rows, dest_dev[:, :, None, None], axis=1).reshape(
        tokens.shape
    )
    grad_tokens = jnp.take_along_axis(back_grad_rows, dest_dev[:, :, None, None], axis=1).reshape(
        tokens.shape
    )
    sum_query, sum_key, sum_value, sum_out, sum_inner, sum_outer, sum_bias_inner = (
        lax.psum_scatter(acc_query, "dp", scatter_dimension=0, tiled=True),
        lax.psum_scatter(acc_key, "dp", scatter_dimension=0, tiled=True),
        lax.psum_scatter(acc_value, "dp", scatter_dimension=0, tiled=True),
        lax.psum_scatter(acc_out, "dp", scatter_dimension=1, tiled=True),
        lax.psum_scatter(acc_inner, "dp", scatter_dimension=0, tiled=True),
        lax.psum_scatter(acc_outer, "dp", scatter_dimension=1, tiled=True),
        lax.psum_scatter(acc_bias_inner, "dp", scatter_dimension=1, tiled=True),
    )
    half_width = w_query.shape[1]
    tensor_pos = lax.axis_index("tensor")
    bias_pair = lax.dynamic_update_slice(
        jnp.zeros((2, model_width), jnp.float32),
        jnp.concatenate([acc_bias_query, acc_bias_value], axis=0),
        (jnp.int32(0), tensor_pos * half_width),
    )
    vectors, bias_total = lax.psum((acc_vectors, bias_pair), ("dp", "tensor"))
    own_width = model_width // dp_count
    vec_own = lax.dynamic_slice_in_dim(vectors, lax.axis_index("dp") * own_width, own_width, 1)
    bias_own = lax.dynamic_slice_in_dim(bias_total, tensor_pos * half_width, half_width, 1)
    return (
        layer_out,
        grad_tokens,
        sum_query,
        sum_key,
        sum_value,
        bias_own[0:1],
        bias_own[1:2],
        sum_out,
        vec_own[0],
        vec_own[1],
        vec_own[2],
        sum_inner,
        sum_bias_inner,
        sum_outer,
        vec_own[3],
        vec_own[4],
        vec_own[5],
    )


def solution(mesh):
    placed = (
        P("dp", "tensor", None),
        P("dp", "tensor", None),
        P("dp"),
        P("dp", None),
        P("dp", "tensor"),
        P("dp", "tensor"),
        P("dp", "tensor"),
        P("tensor", None),
        P("tensor", None),
        P("tensor", "dp"),
        P("dp"),
        P("dp"),
        P("dp"),
        P("dp", "tensor"),
        P("tensor", "dp"),
        P("tensor", "dp"),
        P("dp"),
        P("dp"),
        P("dp"),
    )
    dp_count = mesh.shape["dp"]

    def body(*args):
        tokens, w_query, b_inner = args[0], args[4], args[14]
        fits = (
            dp_count & (dp_count - 1) == 0
            and w_query.shape[0] % 16 == 0
            and tokens.shape[1] % 8 == 0
            and mesh.shape["tensor"] == 2
        )
        return (shards_fast if fits else shards)(*args)

    return jax.shard_map(
        body,
        mesh=mesh,
        in_specs=placed,
        out_specs=(
            P("dp", "tensor", None),
            P("dp", "tensor", None),
            P("dp", "tensor"),
            P("dp", "tensor"),
            P("dp", "tensor"),
            P("tensor", None),
            P("tensor", None),
            P("tensor", "dp"),
            P("dp"),
            P("dp"),
            P("dp"),
            P("dp", "tensor"),
            P("tensor", "dp"),
            P("tensor", "dp"),
            P("dp"),
            P("dp"),
            P("dp"),
        ),
        check_vma=False,
    )
```

```python
from functools import partial
import math

import jax
import jax.numpy as jnp
from jax import lax
from jax.experimental import pallas as pl
from jax.experimental.pallas import tpu as pltpu
from jax.sharding import PartitionSpec as P

HEADS = 12
HD = 64


EPS_NORM = 1e-12


def layer_norm(residual, norm_gain, norm_shift):
    centre = residual - jnp.mean(residual, axis=-1, keepdims=True)
    spread = lax.rsqrt(jnp.mean(centre * centre, axis=-1, keepdims=True) + EPS_NORM)
    normed = centre * spread
    return (normed * norm_gain + norm_shift, normed, spread)


def norm_back(grad_out, normed, spread, norm_gain):
    scaled = grad_out * norm_gain
    inner_term = (
        scaled
        - jnp.mean(scaled, axis=-1, keepdims=True)
        - normed * jnp.mean(scaled * normed, axis=-1, keepdims=True)
    )
    return (inner_term * spread, jnp.sum(grad_out * normed, axis=0), jnp.sum(grad_out, axis=0))


def segment_of(seq_lengths, count_rows):
    seq_ends = jnp.cumsum(seq_lengths)
    positions = jnp.arange(count_rows, dtype=jnp.int32)
    return jnp.sum((positions[:, None] >= seq_ends[None, :-1]).astype(jnp.int32), axis=1)


def masked_scores(query_block, key_heads, segment, first_row, block_rows, score_scale):
    scores = (
        jnp.einsum("qhd,khd->hqk", query_block, key_heads, preferred_element_type=jnp.float32)
        * score_scale
    )
    allowed = segment[first_row : first_row + block_rows, None] == segment[None, :]
    return jnp.where(allowed[None], scores, -1e30)


def attend_forward(query_heads, key_heads, value_heads, segment, block_rows, score_scale):
    scores = masked_scores(query_heads, key_heads, segment, 0, block_rows, score_scale)
    row_peak = jnp.max(scores, axis=-1, keepdims=True)
    exp_scores = jnp.exp(scores - row_peak)
    row_total = jnp.sum(exp_scores, axis=-1, keepdims=True)
    prob_low = (exp_scores / row_total).astype(jnp.bfloat16)
    out_block = jnp.einsum(
        "hqk,khd->qhd", prob_low, value_heads, preferred_element_type=jnp.float32
    )
    out_rows = out_block.astype(jnp.bfloat16)
    lse_rows = row_peak + jnp.log(row_total)
    return (out_rows, lse_rows)


def attend_backward(
    query_heads, key_heads, value_heads, grad_heads, log_totals, segment, block_rows, score_scale
):
    scores = masked_scores(query_heads, key_heads, segment, 0, block_rows, score_scale)
    probs_full = jnp.exp(scores - log_totals)
    prob_low = probs_full.astype(jnp.bfloat16)
    grad_values = jnp.einsum(
        "hqk,qhd->khd", prob_low, grad_heads, preferred_element_type=jnp.float32
    )
    grad_probs = jnp.einsum(
        "qhd,khd->hqk", grad_heads, value_heads, preferred_element_type=jnp.float32
    )
    row_inner = jnp.sum(probs_full * grad_probs, axis=-1, keepdims=True)
    grad_scores = (probs_full * (grad_probs - row_inner)).astype(jnp.bfloat16)
    grad_query_rows = (
        jnp.einsum("hqk,khd->qhd", grad_scores, key_heads, preferred_element_type=jnp.float32)
        * score_scale
    )
    grad_keys = (
        jnp.einsum("hqk,qhd->khd", grad_scores, query_heads, preferred_element_type=jnp.float32)
        * score_scale
    )
    return (grad_query_rows, grad_keys, grad_values)


MESH = pl.DeviceIdType.MESH
LANES = 128
NT = (((1,), (1,)), ((), ()))
NN = (((1,), (0,)), ((), ()))
F32 = jnp.float32
LOW = jnp.bfloat16
VMEM_BYTES = 63 << 20


def flip(place, bit):
    return place + bit * (1 - 2 * ((place // bit) % 2))


def bit_of(place, bit):
    return (place // bit) % 2


def bits_of(count):
    return tuple(1 << i for i in range(count.bit_length() - 1))[::-1]


def orders_of(count):
    bits = bits_of(count)
    return (bits, bits[:-2] + bits[-2:][::-1])


def mm(left, right, dims=NN):
    return lax.dot_general(left, right, dims, preferred_element_type=F32)


class Gather:
    def __init__(self, dp_count, place, half, order, ref, start, size, send_sem, recv_sem):
        self.place, self.half, self.order = place, half, order
        self.bits = bits_of(dp_count)
        self.ref, self.cols = ref, pl.ds(start, size)
        self.send_sem, self.recv_sem = send_sem, recv_sem

    def copy(self, stage):
        done = self.order[:stage]
        index = tuple(
            slice(None) if bit in done else bit_of(self.place, bit) for bit in self.bits
        ) + (slice(None), self.cols)
        return pltpu.make_async_remote_copy(
            src_ref=self.ref.at[index],
            dst_ref=self.ref.at[index],
            send_sem=self.send_sem.at[stage],
            recv_sem=self.recv_sem.at[stage],
            device_id=(flip(self.place, self.order[stage]), self.half),
            device_id_type=MESH,
        )


class Scatter:
    def __init__(self, dp_count, place, half, order, ref, start, size, landing, send_sem, recv_sem):
        self.place, self.half = place, half
        self.order = order[::-1]
        self.bits = bits_of(dp_count)
        self.ref, self.cols = ref, pl.ds(start, size)
        self.landing = landing
        self.send_sem, self.recv_sem = send_sem, recv_sem

    def view(self, stage, chosen):
        left = [bit for bit in self.bits if bit not in self.order[:stage]]
        own = bit_of(self.place, self.order[stage])
        index = tuple(
            (own if chosen == "own" else 1 - own) if bit == self.order[stage] else slice(None)
            for bit in left
        )
        if stage == 0:
            return self.ref.at[index + (slice(None), self.cols)]
        return self.landing[stage - 1].at[index]

    def copy(self, stage):
        return pltpu.make_async_remote_copy(
            src_ref=self.view(stage, "other"),
            dst_ref=self.landing[stage],
            send_sem=self.send_sem.at[stage],
            recv_sem=self.recv_sem.at[stage],
            device_id=(flip(self.place, self.order[stage]), self.half),
            device_id_type=MESH,
        )

    def add(self, stage):
        kept = self.view(stage, "own")
        land = self.landing[stage]
        lead = land.shape[:-2]
        count = math.prod(lead)

        def one(i, carry):
            index, rest = [], i
            for extent in lead[::-1]:
                index.append(lax.rem(rest, extent))
                rest = rest // extent
            index = tuple(index[::-1])
            land[index] = (kept[index].astype(F32) + land[index].astype(F32)).astype(land.dtype)
            return carry

        if count == 1:
            one(0, 0)
        else:
            lax.fori_loop(0, count, one, 0)

    def finish(self, stage, out_ref, out_cols):
        kept = self.view(stage, "own")
        out_ref[:, out_cols] = kept[...].astype(F32) + self.landing[stage][...].astype(F32)


def layer(sizes, gather_plan, scatter_plan, *refs):
    dp_count, micro, rows, width, heads_wide, ff = sizes
    (
        tokens_ref,
        cot_ref,
        route_ref,
        inverse_ref,
        lengths_ref,
        wq_ref,
        wk_ref,
        wv_ref,
        wo_ref,
        wi_ref,
        wu_ref,
        small_ref,
        bq_ref,
        bv_ref,
        bi_ref,
        layer_out_ref,
        grad_tokens_ref,
        sum_ref,
        vec_out_ref,
        full,
        grads,
        x_send,
        dy_send,
        x_land,
        dy_land,
        out_send,
        gx_send,
        out_land,
        gx_land,
        xs,
        hs,
        gs,
        gb,
        flipped,
        xs_flipped,
        hs_flipped,
        qkv,
        dqkv,
        attn,
        gattn,
        probs,
        bias,
        gelu_low,
        dgelu,
        ginner,
        normed,
        spread,
        grad_keep,
        own_part,
        part_send,
        part_land,
        last_send,
        last_land,
        vec_buf,
        vec_land,
        vec,
        vec_pair,
        vecg_buf,
        vecg_land,
        vec_acc,
        *rest,
    ) = refs
    stages = dp_count.bit_length() - 1
    landings = [rest[i * stages : (i + 1) * stages] for i in range(len(scatter_plan))]
    (
        x_sems,
        dy_sems,
        out_sems,
        gx_sems,
        gather_sems,
        scatter_sems,
        vec_sems,
        vecg_sems,
        pair_sems,
    ) = rest[len(scatter_plan) * stages :]
    place, half = lax.axis_index("dp"), lax.axis_index("tensor")
    other = 1 - half
    bits = bits_of(dp_count)
    orders = orders_of(dp_count)
    bin_half = dp_count * rows
    tall = micro * bin_half
    blocks = micro * dp_count
    own_width = width // dp_count
    block_len = 2 * rows
    pairs = heads_wide // LANES
    key_col, value_col, out_col = heads_wide, 2 * heads_wide, 3 * heads_wide
    inner_col, outer_col = 4 * heads_wide, 4 * heads_wide + ff
    tile = heads_wide

    def weights(start, size):
        return full[(slice(None),) * stages + (slice(None), pl.ds(start, size))].reshape(width, size)

    def pair_copy(src, dst, which):
        return pltpu.make_async_remote_copy(
            src_ref=src,
            dst_ref=dst,
            send_sem=pair_sems.at[0, which],
            recv_sem=pair_sems.at[1, which],
            device_id=(place, other),
            device_id_type=MESH,
        )

    def push(send_ref, recv_ref, sems):
        def one(step, carry):
            peer = lax.rem(place + step, dp_count)
            pltpu.make_async_remote_copy(
                src_ref=send_ref.at[peer],
                dst_ref=recv_ref.at[place],
                send_sem=sems.at[0, step],
                recv_sem=sems.at[1, step],
                device_id=(peer, half),
                device_id_type=MESH,
            ).start()
            return carry

        lax.fori_loop(1, dp_count, one, 0)

    def settle(send_ref, recv_ref, sems):
        recv_ref[place] = send_ref[place]

        def one(step, carry):
            source = lax.rem(place + dp_count - step, dp_count)
            pltpu.make_async_remote_copy(
                src_ref=send_ref.at[source],
                dst_ref=recv_ref.at[source],
                send_sem=sems.at[0, step],
                recv_sem=sems.at[1, step],
                device_id=(source, half),
                device_id_type=MESH,
            ).wait()
            return carry

        lax.fori_loop(1, dp_count, one, 0)

    def arrange(src_ref, dst_ref):
        def one(i, carry):
            m, peer = i // dp_count, lax.rem(i, dp_count)
            dst_ref[peer, m] = src_ref[m * dp_count + inverse_ref[m, peer]]
            return carry

        lax.fori_loop(0, blocks, one, 0)

    own = tuple(bit_of(place, bit) for bit in bits)
    eye = (
        lax.broadcasted_iota(jnp.int32, (own_width, own_width), 0)
        == lax.broadcasted_iota(jnp.int32, (own_width, own_width), 1)
    ).astype(LOW)
    full[own + (slice(None), pl.ds(0, heads_wide))] = wq_ref[...]
    full[own + (slice(None), pl.ds(key_col, heads_wide))] = wk_ref[...]
    full[own + (slice(None), pl.ds(value_col, heads_wide))] = wv_ref[...]
    full[own + (slice(None), pl.ds(out_col, heads_wide))] = mm(eye, wo_ref[...], NT).astype(LOW)
    full[own + (slice(None), pl.ds(inner_col, ff))] = wi_ref[...]
    full[own + (slice(None), pl.ds(outer_col, ff))] = mm(eye, wu_ref[...], NT).astype(LOW)

    def spread_out(piece, total):
        size = piece.shape[1]
        target = lax.broadcasted_iota(jnp.int32, (size, total), 1)
        at = lax.broadcasted_iota(jnp.int32, (size, total), 0) + place * size
        return lax.dot_general(
            piece,
            (target == at).astype(F32),
            NN,
            precision=lax.Precision.HIGHEST,
            preferred_element_type=F32,
        )

    vec_buf[0, 0:8, :] = spread_out(small_ref[...], width)
    long_row = spread_out(jnp.broadcast_to(bi_ref[...].astype(F32), (8, bi_ref.shape[1])), ff)
    vec_buf[0, 8:16, :] = jnp.zeros((8, width), F32)
    for i in range(ff // width):
        vec_buf[0, 8 + i : 9 + i, :] = long_row[0:1, i * width : (i + 1) * width]
    arrange(tokens_ref, x_send)

    barrier = pltpu.get_barrier_semaphore()

    def hello(step, carry):
        peer = lax.rem(place + step, dp_count)
        pl.semaphore_signal(barrier, inc=1, device_id=(peer, half), device_id_type=MESH)
        return carry

    lax.fori_loop(1, dp_count, hello, 0)
    pl.semaphore_signal(barrier, inc=1, device_id=(place, other), device_id_type=MESH)
    pl.semaphore_wait(barrier, dp_count)

    gathers = [
        Gather(
            dp_count,
            place,
            half,
            orders[which],
            full,
            start,
            size,
            gather_sems.at[0, i],
            gather_sems.at[1, i],
        )
        for i, (group, which, start, size) in enumerate(gather_plan)
    ]

    def advance(step):
        for (group, _, _, _), gather in zip(gather_plan, gathers):
            stage = step - group
            if 0 <= stage < stages:
                if stage > 0:
                    gather.copy(stage - 1).wait_recv()
                gather.copy(stage).start()

    def need(wanted):
        for (group, _, _, _), gather in zip(gather_plan, gathers):
            if group == wanted:
                gather.copy(stages - 1).wait_recv()

    def swing(buf, land, sems, stage, last_ref):
        copy = pltpu.make_async_remote_copy(
            src_ref=buf.at[stage],
            dst_ref=land.at[stage],
            send_sem=sems.at[0, stage],
            recv_sem=sems.at[1, stage],
            device_id=(flip(place, bits[stage]), half),
            device_id_type=MESH,
        )

        def fold():
            copy.wait()
            total = buf[stage] + land[stage]
            if stage < stages - 1:
                buf[stage + 1] = total
            else:
                last_ref[...] = total

        return copy.start, fold

    push(x_send, x_land, x_sems)
    begin, fold = swing(vec_buf, vec_land, vec_sems, 0, vec)
    begin()
    advance(0)
    arrange(cot_ref, dy_send)
    for stage in range(1, stages):
        fold()
        begin, fold = swing(vec_buf, vec_land, vec_sems, stage, vec)
        begin()
        advance(stage)
    push(dy_send, dy_land, dy_sems)
    fold()

    route = vec[6:7, :]
    target = jnp.floor((route + 0.5) * (1.0 / blocks))
    in_bin = route - dp_count * jnp.floor((route + 0.5) * (1.0 / dp_count))
    placed = jnp.where(target == place.astype(F32), in_bin, 0.0)
    placed_rows = jnp.broadcast_to(placed, (8, blocks * dp_count))

    def mask_bin(m, carry):
        shape = (2 * bin_half, blocks * dp_count)
        row = lax.broadcasted_iota(jnp.int32, shape, 0)
        lane = lax.broadcasted_iota(jnp.int32, shape, 1)
        source = lax.rem(row, bin_half) // rows
        chosen = (lane // dp_count) == source * micro + m
        tall_place = jnp.sum(jnp.where(chosen, placed, 0.0), axis=1, keepdims=True)
        wide_place = mm(placed_rows, chosen.astype(F32), NT)[0:1, :]
        ends, end = [], 0
        for i in range(lengths_ref.shape[1] - 1):
            end = end + lengths_ref[m, i]
            ends.append(end.astype(F32))

        def sequence(at, index):
            within = (lax.rem(index, rows) + (index // bin_half) * rows).astype(F32)
            position = at * block_len + within
            return sum((position >= end).astype(F32) for end in ends)

        down = sequence(
            tall_place, lax.broadcasted_iota(jnp.int32, (2 * bin_half, 1), 0)
        )
        across = sequence(
            wide_place, lax.broadcasted_iota(jnp.int32, (1, 2 * bin_half), 1)
        )
        bias[m] = jnp.where(down == across, 0.0, -1e30)
        return carry

    lax.fori_loop(0, micro, mask_bin, 0)

    settle(x_send, x_land, x_sems)

    def order_rows(m, carry):
        block = x_land[:, m].astype(F32).reshape(bin_half, width)
        xs[half, pl.ds(pl.multiple_of(m * bin_half, bin_half), bin_half), :] = block.astype(LOW)
        return carry

    lax.fori_loop(0, micro, order_rows, 0)
    swap_x = pair_copy(xs.at[half], xs.at[half], 0)
    swap_x.start()
    advance(stages)
    swap_x.wait()
    need(0)

    def project(i, carry):
        h = lax.rem(half + i, 2)
        own_rows = xs[h]
        qkv[h, :, pl.ds(0, heads_wide)] = (
            (mm(own_rows, weights(0, heads_wide)) + bq_ref[...].astype(F32)).astype(LOW)
            * LOW(HD ** (-0.5))
        )
        qkv[h, :, pl.ds(key_col, heads_wide)] = mm(own_rows, weights(key_col, heads_wide)).astype(LOW)
        qkv[h, :, pl.ds(value_col, heads_wide)] = (
            mm(own_rows, weights(value_col, heads_wide)) + bv_ref[...].astype(F32)
        ).astype(LOW)
        return carry

    lax.fori_loop(0, 2, project, 0)
    advance(stages + 1)

    low_lane = lax.broadcasted_iota(jnp.int32, (2 * bin_half, LANES), 1) < HD
    nothing = jnp.zeros((2 * bin_half, LANES), LOW)

    def bin_of(ref, m, start):
        at = pl.ds(pl.multiple_of(m * bin_half, bin_half), bin_half)
        return jnp.concatenate([ref[0, at, pl.ds(start, LANES)], ref[1, at, pl.ds(start, LANES)]], axis=0)

    def put_bin(ref, m, start, value):
        at = pl.ds(pl.multiple_of(m * bin_half, bin_half), bin_half)
        ref[0, at, pl.ds(start, LANES)] = value[:bin_half].astype(ref.dtype)
        ref[1, at, pl.ds(start, LANES)] = value[bin_half:].astype(ref.dtype)

    def split_heads(value):
        return (jnp.where(low_lane, value, nothing), jnp.where(low_lane, nothing, value))

    def attend(m):
        for j in range(pairs):
            query = bin_of(qkv, m, j * LANES)
            key = bin_of(qkv, m, key_col + j * LANES)
            value = bin_of(qkv, m, value_col + j * LANES)
            total = None
            for e, (query_e, value_e) in enumerate(zip(split_heads(query), split_heads(value))):
                score = mm(query_e, key, NT) + bias[m]
                power = jnp.exp(score - jnp.max(score, axis=1, keepdims=True))
                prob = power * (1.0 / jnp.sum(power, axis=1, keepdims=True))
                probs[m, 2 * j + e] = prob.astype(probs.dtype)
                part = mm(prob.astype(LOW), value_e)
                total = part if total is None else total + part
            put_bin(attn, m, j * LANES, total)

    for m in range(micro):
        attend(m)
        advance(stages + 2 + m)
    for step in range(stages + 2 + micro, stages + max(g for g, _, _, _ in gather_plan)):
        advance(step)

    def two_halves(left_ref, columns, start, send_ref, which, land_ref):
        away = mm(left_ref[other], weights(start, columns), NT)
        send_ref[...] = away.astype(send_ref.dtype)
        copy = pair_copy(send_ref, land_ref, which)
        copy.start()
        own_part[...] = mm(left_ref[half], weights(start, columns), NT)
        return copy

    need(1)
    copy = two_halves(attn, heads_wide, out_col, part_send, 1, part_land.at[0])
    chunk = 4 * rows
    per_bin = bin_half // chunk
    chunks = tall // chunk
    ones = jnp.ones((8, tall), LOW)

    def mean_of(v):
        return jnp.sum(v, axis=1, keepdims=True) * (1.0 / width)

    copy.wait()

    def norm_attn(i, carry):
        at = pl.ds(pl.multiple_of(i * chunk, chunk), chunk)
        mid = xs[half, at, :].astype(F32) + (own_part[at, :] + part_land[0, at, :]) + vec[0:1, :]
        centre = mid - mean_of(mid)
        inverse_s = lax.rsqrt(mean_of(centre * centre) + EPS_NORM)
        unit = centre * inverse_s
        normed[at, :] = unit
        spread[at, :] = jnp.broadcast_to(inverse_s, (chunk, LANES))
        hs[half, at, :] = (unit * vec[1:2, :] + vec[2:3, :]).astype(LOW)
        return carry

    lax.fori_loop(0, chunks, norm_attn, 0)
    swap_h = pair_copy(hs.at[half], hs.at[half], 2)
    swap_h.start()
    need(2)

    def widen(h):
        for i in range(ff // tile):
            start = i * tile
            row = 8 + start // width
            inner = mm(hs[h], weights(inner_col + start, tile)) + vec[
                row : row + 1, start % width : start % width + tile
            ]
            cdf = 0.5 * (1.0 + lax.erf(inner * (0.5**0.5)))
            density = jnp.exp(-0.5 * inner * inner) * ((2.0 * math.pi) ** -0.5)
            gelu_low[h, :, start : start + tile] = (inner * cdf).astype(LOW)
            dgelu[h, :, start : start + tile] = (cdf + inner * density).astype(dgelu.dtype)

    def widen_step(i, carry):
        @pl.when(i == 1)
        def _():
            swap_h.wait()

        widen(lax.rem(half + i, 2))
        return carry

    lax.fori_loop(0, 2, widen_step, 0)
    xs_flipped[...] = xs[...].reshape(2 * tall, width).T
    hs_flipped[...] = hs[...].reshape(2 * tall, width).T
    for group in range(3, max(g for g, _, _, _ in gather_plan) + 1):
        need(group)
    copy = two_halves(gelu_low, ff, outer_col, part_send, 3, part_land.at[1])
    settle(dy_send, dy_land, dy_sems)
    for i in range(3):
        vec_acc[i] = jnp.zeros((8, width), F32)
    copy.wait()

    def fold_rows(v):
        return jnp.sum(v.reshape(chunk // 8, 8, width), axis=0)

    def norm_ffn(i, carry):
        at = pl.ds(pl.multiple_of(i * chunk, chunk), chunk)
        m, quarter = i // per_bin, lax.rem(i, per_bin)
        sources = pl.ds(quarter * (chunk // rows), chunk // rows)
        hidden = normed[at, :] * vec[1:2, :] + vec[2:3, :]
        top = hidden + (own_part[at, :] + part_land[1, at, :]) + vec[3:4, :]
        centre = top - mean_of(top)
        inverse_s = lax.rsqrt(mean_of(centre * centre) + EPS_NORM)
        unit = centre * inverse_s
        result = unit * vec[4:5, :] + vec[5:6, :]
        out_send[sources, m] = result.reshape(chunk // rows, rows, width).astype(LOW)
        dy = dy_land[sources, m].astype(F32).reshape(chunk, width)
        vec_acc[0] = vec_acc[0] + fold_rows(dy * unit)
        vec_acc[1] = vec_acc[1] + fold_rows(dy)
        scaled = dy * vec[4:5, :]
        grad_top = (scaled - mean_of(scaled) - unit * mean_of(scaled * unit)) * inverse_s
        grad_keep[at, :] = grad_top
        gs[half, at, :] = grad_top.astype(LOW)
        return carry

    lax.fori_loop(0, chunks, norm_ffn, 0)
    swap_g = pair_copy(gs.at[half], gs.at[half], 4)
    swap_g.start()
    push(out_send, out_land, out_sems)
    vecg_buf[0, 4:5, :] = jnp.sum(vec_acc[0], axis=0, keepdims=True)
    vecg_buf[0, 5:6, :] = jnp.sum(vec_acc[1], axis=0, keepdims=True)
    vecg_buf[0, 3:4, :] = mm(ones, gs[half])[0:1, :]

    def narrow(h):
        for i in range(ff // tile):
            start = i * tile
            grad = mm(gs[h], weights(outer_col + start, tile)) * dgelu[h, :, start : start + tile].astype(F32)
            ginner[h, :, start : start + tile] = grad.astype(LOW)

    def narrow_step(i, carry):
        @pl.when(i == 1)
        def _():
            swap_g.wait()

        narrow(lax.rem(half + i, 2))
        return carry

    lax.fori_loop(0, 2, narrow_step, 0)

    scatters = [
        Scatter(
            dp_count,
            place,
            half,
            orders[which],
            grads,
            start,
            size,
            landings[i],
            scatter_sems.at[0, i],
            scatter_sems.at[1, i],
        )
        for i, (group, which, start, size) in enumerate(scatter_plan)
    ]
    members = lambda wanted: [
        (plan, scatter) for plan, scatter in zip(scatter_plan, scatters) if plan[0] == wanted
    ]

    def reduce_start(group):
        for _, scatter in members(group):
            scatter.copy(0).start()

    def reduce_step(group, stage):
        for _, scatter in members(group):
            scatter.copy(stage).wait_recv()
            if stage < stages - 1:
                scatter.add(stage)
                scatter.copy(stage + 1).start()
            else:
                scatter.finish(stage, sum_ref, scatter.cols)

    def grad_columns(left_t, right_ref, start, columns, grads_start):
        for i in range(columns // tile):
            piece = mm(left_t, right_ref[:, :, start + i * tile : start + (i + 1) * tile].reshape(2 * tall, tile))
            grads[(slice(None),) * (stages + 1) + (pl.ds(grads_start + i * tile, tile),)] = piece.astype(
                LOW
            ).reshape(bits_shape + (own_width, tile))

    bits_shape = (2,) * stages
    copy = two_halves(ginner, ff, inner_col, part_send, 5, part_land.at[2])
    flipped[...] = gs[...].reshape(2 * tall, width).T
    grad_columns(flipped[...], gelu_low, 0, ff, outer_col)
    reduce_start(0)
    for i in range(ff // width):
        columns = slice(i * width, (i + 1) * width)
        vecg_buf[0, 6 + i : 7 + i, :] = (mm(ones, ginner[0, :, columns]) + mm(ones, ginner[1, :, columns]))[0:1, :]
    copy.wait()
    for i in range(3):
        vec_acc[i] = jnp.zeros((8, width), F32)

    def norm_back(i, carry):
        at = pl.ds(pl.multiple_of(i * chunk, chunk), chunk)
        grad_hidden = grad_keep[at, :] + (own_part[at, :] + part_land[2, at, :])
        unit = normed[at, :]
        vec_acc[0] = vec_acc[0] + fold_rows(grad_hidden * unit)
        vec_acc[1] = vec_acc[1] + fold_rows(grad_hidden)
        scaled = grad_hidden * vec[1:2, :]
        grad_mid = (scaled - mean_of(scaled) - unit * mean_of(scaled * unit)) * spread[at, 0:1]
        grad_keep[at, :] = grad_mid
        gb[half, at, :] = grad_mid.astype(LOW)
        return carry

    lax.fori_loop(0, chunks, norm_back, 0)
    swap_b = pair_copy(gb.at[half], gb.at[half], 6)
    swap_b.start()
    vecg_buf[0, 1:2, :] = jnp.sum(vec_acc[0], axis=0, keepdims=True)
    vecg_buf[0, 2:3, :] = jnp.sum(vec_acc[1], axis=0, keepdims=True)
    vecg_buf[0, 0:1, :] = mm(ones, gb[half])[0:1, :]
    grad_columns(hs_flipped[...], ginner, 0, ff, inner_col)
    swap_b.wait()
    flipped[...] = gb[...].reshape(2 * tall, width).T
    grad_columns(flipped[...], attn, 0, heads_wide, out_col)
    reduce_start(1)

    def to_heads(h, carry):
        gattn[h] = mm(gb[h], weights(out_col, heads_wide)).astype(LOW)
        return carry

    lax.fori_loop(0, 2, to_heads, 0)

    def attend_back(m):
        for j in range(pairs):
            query = bin_of(qkv, m, j * LANES)
            key = bin_of(qkv, m, key_col + j * LANES)
            value = bin_of(qkv, m, value_col + j * LANES)
            grad = bin_of(gattn, m, j * LANES)
            keys, queries, upstream = split_heads(key), split_heads(query), split_heads(grad)
            d_query = d_key = d_value = None
            for e in range(2):
                prob = probs[m, 2 * j + e].astype(F32)
                d_prob = mm(upstream[e], value, NT)
                inner = jnp.sum(prob * d_prob, axis=1, keepdims=True)
                d_score = (prob * (d_prob - inner)).astype(LOW)
                part_q = mm(d_score, keys[e])
                part_k = mm(d_score.T, queries[e])
                part_v = mm(prob.astype(LOW).T, upstream[e])
                d_query = part_q if d_query is None else d_query + part_q
                d_key = part_k if d_key is None else d_key + part_k
                d_value = part_v if d_value is None else d_value + part_v
            put_bin(dqkv, m, j * LANES, d_query * (HD ** (-0.5)))
            put_bin(dqkv, m, key_col + j * LANES, d_key)
            put_bin(dqkv, m, value_col + j * LANES, d_value)

    attend_back(0)
    reduce_step(0, 0)
    for m in range(1, micro):
        attend_back(m)
    reduce_step(0, 1)

    away = mm(dqkv[other], weights(0, 3 * heads_wide), NT)
    last_send[...] = away.astype(LOW)
    copy = pair_copy(last_send, last_land, 7)
    copy.start()
    grad_columns(xs_flipped[...], dqkv, 0, 3 * heads_wide, 0)
    reduce_start(2)
    own_part[...] = mm(dqkv[half], weights(0, 3 * heads_wide), NT)
    copy.wait()

    def leave(i, carry):
        at = pl.ds(pl.multiple_of(i * chunk, chunk), chunk)
        m, quarter = i // per_bin, lax.rem(i, per_bin)
        sources = pl.ds(quarter * (chunk // rows), chunk // rows)
        grad_x = grad_keep[at, :] + (own_part[at, :] + last_land[at, :].astype(F32))
        gx_send[sources, m] = grad_x.reshape(chunk // rows, rows, width).astype(LOW)
        return carry

    lax.fori_loop(0, chunks, leave, 0)
    push(gx_send, gx_land, gx_sems)
    for i, start in enumerate((0, value_col)):
        columns = slice(start, start + heads_wide)
        vecg_buf[0, 8:9, i * heads_wide : (i + 1) * heads_wide] = (
            mm(ones, dqkv[0, :, columns]) + mm(ones, dqkv[1, :, columns])
        )[0:1, :]
    vecg_buf[0, 9:16, :] = jnp.zeros((7, width), F32)

    swap_v = pair_copy(vecg_buf.at[0], vec_pair, 8)
    swap_v.start()
    swap_v.wait()
    vecg_buf[0, 0:6, :] = vecg_buf[0, 0:6, :] + vec_pair[0:6, :]
    begin, fold = swing(vecg_buf, vecg_land, vecg_sems, 0, vec_out_ref)
    begin()
    reduce_step(1, 0)
    reduce_step(0, 2)
    fold()
    begin, fold = swing(vecg_buf, vecg_land, vecg_sems, 1, vec_out_ref)
    begin()
    reduce_step(1, 1)
    reduce_step(0, 3)
    fold()
    for stage in range(2, stages):
        begin, fold = swing(vecg_buf, vecg_land, vecg_sems, stage, vec_out_ref)
        begin()
        fold()
    reduce_step(2, 0)
    reduce_step(1, 2)
    reduce_step(2, 1)
    reduce_step(1, 3)
    settle(out_send, out_land, out_sems)

    def hand_back(land_ref, result_ref):
        def one(i, carry):
            result_ref[i] = land_ref[route_ref[i] // blocks, i // dp_count]
            return carry

        lax.fori_loop(0, blocks, one, 0)

    hand_back(out_land, layer_out_ref)
    reduce_step(2, 2)
    settle(gx_send, gx_land, gx_sems)
    hand_back(gx_land, grad_tokens_ref)
    reduce_step(2, 3)
    for gather in gathers:
        for stage in range(stages):
            gather.copy(stage).wait_send()
    for scatter in scatters:
        for stage in range(stages):
            scatter.copy(stage).wait_send()


def plan_of(cuts):
    plan = []
    for group, (start, stop) in enumerate(cuts):
        middle = start + (stop - start + LANES) // (2 * LANES) * LANES
        plan.append((group, 0, start, middle - start))
        plan.append((group, 1, middle, stop - middle))
    return plan


def shards_fast(
    tokens,
    cotangent,
    block_route,
    lengths,
    w_query,
    w_key,
    w_value,
    b_query,
    b_value,
    w_out,
    b_out,
    gain_attn,
    shift_attn,
    w_inner,
    b_inner,
    w_outer,
    b_outer,
    gain_ffn,
    shift_ffn,
):
    dp_count = lax.axis_size("dp")
    micro, rows, width = lengths.shape[0], tokens.shape[1], tokens.shape[2]
    heads_wide, ff = w_query.shape[1], w_inner.shape[1]
    place = lax.axis_index("dp")
    blocks = micro * dp_count
    own_width = width // dp_count
    columns = 4 * heads_wide + 2 * ff
    stages = dp_count.bit_length() - 1
    bits = (2,) * stages
    target = block_route.reshape(micro, dp_count) // blocks
    inverse = jnp.argmax(
        target[:, None, :] == jnp.arange(dp_count, dtype=jnp.int32)[None, :, None], axis=2
    ).astype(jnp.int32)
    nothing = jnp.zeros((1, own_width), F32)
    small = jnp.concatenate(
        [v.astype(F32)[None] for v in (b_out, gain_attn, shift_attn, b_outer, gain_ffn, shift_ffn, block_route)]
        + [nothing],
        axis=0,
    )
    inner_col, outer_col = 4 * heads_wide, 4 * heads_wide + ff
    third = inner_col + ff // 2
    gather_plan = plan_of(
        [
            (0, 3 * heads_wide),
            (3 * heads_wide, third),
            (third, outer_col),
            (outer_col, outer_col + ff // 2),
            (outer_col + ff // 2, columns),
        ]
    )
    scatter_plan = plan_of([(outer_col, columns), (3 * heads_wide, outer_col), (0, 3 * heads_wide)])
    bin_half = dp_count * rows
    tall = micro * bin_half
    vmem, smem = pl.BlockSpec(memory_space=pltpu.VMEM), pl.BlockSpec(memory_space=pltpu.SMEM)
    dma = pltpu.SemaphoreType.DMA
    swap_shape = (dp_count, micro, rows, width)
    scratch = [
        pltpu.VMEM(bits + (own_width, columns), LOW),
        pltpu.VMEM(bits + (own_width, columns), LOW),
    ]
    scratch += [pltpu.VMEM(swap_shape, LOW) for _ in range(8)]
    scratch += [pltpu.VMEM((2, tall, width), LOW) for _ in range(4)]
    scratch += [pltpu.VMEM((width, 2 * tall), LOW) for _ in range(3)]
    scratch += [pltpu.VMEM((2, tall, 3 * heads_wide), LOW) for _ in range(2)]
    scratch += [pltpu.VMEM((2, tall, heads_wide), LOW) for _ in range(2)]
    scratch += [
        pltpu.VMEM((micro, heads_wide // HD, 2 * bin_half, 2 * bin_half), LOW),
        pltpu.VMEM((micro, 2 * bin_half, 2 * bin_half), F32),
    ]
    scratch += [pltpu.VMEM((2, tall, ff), LOW) for _ in range(3)]
    scratch += [
        pltpu.VMEM((tall, width), F32),
        pltpu.VMEM((tall, LANES), F32),
        pltpu.VMEM((tall, width), F32),
        pltpu.VMEM((tall, width), F32),
        pltpu.VMEM((tall, width), F32),
        pltpu.VMEM((3, tall, width), F32),
        pltpu.VMEM((tall, width), LOW),
        pltpu.VMEM((tall, width), LOW),
        pltpu.VMEM((stages, 16, width), F32),
        pltpu.VMEM((stages, 16, width), F32),
        pltpu.VMEM((16, width), F32),
        pltpu.VMEM((16, width), F32),
        pltpu.VMEM((stages, 16, width), F32),
        pltpu.VMEM((stages, 16, width), F32),
        pltpu.VMEM((3, 8, width), F32),
    ]
    scratch += [
        pltpu.VMEM((2,) * (stages - 1 - stage) + (own_width, size), LOW)
        for _, _, _, size in scatter_plan
        for stage in range(stages)
    ]
    scratch += [dma((2, dp_count)) for _ in range(4)]
    scratch += [
        dma((2, len(gather_plan), stages)),
        dma((2, len(scatter_plan), stages)),
        dma((2, stages)),
        dma((2, stages)),
        dma((2, 9)),
    ]
    sizes = (dp_count, micro, rows, width, heads_wide, ff)
    layer_out, grad_tokens, sums, total = pl.pallas_call(
        partial(layer, sizes, gather_plan, scatter_plan),
        out_shape=(
            jax.ShapeDtypeStruct(tokens.shape, tokens.dtype),
            jax.ShapeDtypeStruct(tokens.shape, tokens.dtype),
            jax.ShapeDtypeStruct((own_width, columns), F32),
            jax.ShapeDtypeStruct((16, width), F32),
        ),
        in_specs=[vmem] * 2 + [smem] * 3 + [vmem] * 10,
        out_specs=[vmem] * 4,
        scratch_shapes=scratch,
        compiler_params=pltpu.CompilerParams(
            collective_id=0, has_side_effects=True, vmem_limit_bytes=VMEM_BYTES
        ),
        name="layer",
    )(
        tokens,
        cotangent,
        block_route,
        inverse,
        lengths,
        w_query,
        w_key,
        w_value,
        w_out,
        w_inner,
        w_outer,
        small,
        b_query,
        b_value,
        b_inner,
    )
    own_inner = b_inner.shape[1]
    vec_own = lax.dynamic_slice_in_dim(total[:6], place * own_width, own_width, 1)
    sum_bias_inner = lax.dynamic_slice_in_dim(
        total[6:8].reshape(1, ff), place * own_inner, own_inner, 1
    )
    return (
        layer_out,
        grad_tokens,
        sums[:, :heads_wide],
        sums[:, heads_wide : 2 * heads_wide],
        sums[:, 2 * heads_wide : 3 * heads_wide],
        total[8:9, :heads_wide],
        total[8:9, heads_wide:],
        sums[:, 3 * heads_wide : 4 * heads_wide].T,
        vec_own[0],
        vec_own[1],
        vec_own[2],
        sums[:, inner_col:outer_col],
        sum_bias_inner,
        sums[:, outer_col:].T,
        vec_own[3],
        vec_own[4],
        vec_own[5],
    )


def shards(
    tokens,
    cotangent,
    block_route,
    lengths,
    w_query,
    w_key,
    w_value,
    b_query,
    b_value,
    w_out,
    b_out,
    gain_attn,
    shift_attn,
    w_inner,
    b_inner,
    w_outer,
    b_outer,
    gain_ffn,
    shift_ffn,
):
    dp_count = lax.axis_size("dp")
    micro_count = lengths.shape[0]
    half_rows = tokens.shape[1]
    model_width = tokens.shape[2]
    local_heads = HEADS // lax.axis_size("tensor")
    score_scale = HD ** (-0.5)
    blocks = tokens.reshape(micro_count, dp_count, half_rows, model_width)
    upstream = cotangent.reshape(micro_count, dp_count, half_rows, model_width)
    target = block_route.reshape(micro_count, dp_count)
    dest_dev = target // (micro_count * dp_count)
    bin_place = target % dp_count
    micro_ids = jnp.broadcast_to(
        jnp.arange(micro_count, dtype=jnp.int32)[:, None], (micro_count, dp_count)
    )
    slot_ids = jnp.broadcast_to(
        jnp.arange(dp_count, dtype=jnp.int32)[None, :], (micro_count, dp_count)
    )
    inverse = jnp.zeros((micro_count, dp_count), jnp.int32).at[micro_ids, dest_dev].set(slot_ids)
    by_dest = jnp.take_along_axis(blocks, inverse[:, :, None, None], axis=1)
    grad_dest = jnp.take_along_axis(upstream, inverse[:, :, None, None], axis=1)
    place_dest = jnp.take_along_axis(bin_place, inverse, axis=1)
    arrived, arrived_grad, arrived_place = (
        lax.all_to_all(by_dest, "dp", split_axis=1, concat_axis=1, tiled=True),
        lax.all_to_all(grad_dest, "dp", split_axis=1, concat_axis=1, tiled=True),
        lax.all_to_all(place_dest, "dp", split_axis=1, concat_axis=1, tiled=True),
    )
    anchor = (
        jnp.zeros((micro_count, dp_count), jnp.int32).at[micro_ids, arrived_place].set(slot_ids)
    )
    bin_tokens = jnp.take_along_axis(arrived, anchor[:, :, None, None], axis=1)
    bin_grads = jnp.take_along_axis(arrived_grad, anchor[:, :, None, None], axis=1)
    acc_query = jnp.zeros((model_width, w_query.shape[1]), jnp.float32)
    acc_key = jnp.zeros((model_width, w_key.shape[1]), jnp.float32)
    acc_value = jnp.zeros((model_width, w_value.shape[1]), jnp.float32)
    acc_out = jnp.zeros((w_out.shape[0], model_width), jnp.float32)
    acc_inner = jnp.zeros((model_width, w_inner.shape[1]), jnp.float32)
    acc_outer = jnp.zeros((w_outer.shape[0], model_width), jnp.float32)
    acc_bias_query = jnp.zeros((1, w_query.shape[1]), jnp.float32)
    acc_bias_value = jnp.zeros((1, w_value.shape[1]), jnp.float32)
    acc_bias_inner = jnp.zeros((1, w_inner.shape[1]), jnp.float32)
    acc_vectors = jnp.zeros((6, model_width), jnp.float32)
    out_bins = []
    grad_bins = []
    for micro_step in range(micro_count):
        gathered = (
            lax.all_gather(w_query, "dp", axis=0, tiled=True),
            lax.all_gather(w_key, "dp", axis=0, tiled=True),
            lax.all_gather(w_value, "dp", axis=0, tiled=True),
            lax.all_gather(w_out, "dp", axis=1, tiled=True),
            lax.all_gather(w_inner, "dp", axis=0, tiled=True),
            lax.all_gather(w_outer, "dp", axis=1, tiled=True),
            lax.all_gather(b_inner, "dp", axis=1, tiled=True),
            lax.all_gather(b_out, "dp", axis=0, tiled=True),
            lax.all_gather(gain_attn, "dp", axis=0, tiled=True),
            lax.all_gather(shift_attn, "dp", axis=0, tiled=True),
            lax.all_gather(b_outer, "dp", axis=0, tiled=True),
            lax.all_gather(gain_ffn, "dp", axis=0, tiled=True),
            lax.all_gather(shift_ffn, "dp", axis=0, tiled=True),
        )
        (
            full_query,
            full_key,
            full_value,
            full_out,
            full_inner,
            full_outer,
            bias_inner,
            bias_out,
            full_gain_attn,
            full_shift_attn,
            bias_outer,
            full_gain_ffn,
            full_shift_ffn,
        ) = gathered
        own_rows = bin_tokens[micro_step]
        whole_bin = lax.all_gather(own_rows, "tensor", axis=1, tiled=True).reshape(-1, model_width)
        bin_rows = whole_bin.shape[0]
        block_rows = math.gcd(bin_rows, 512)
        segment = segment_of(lengths[micro_step], bin_rows)
        query = (
            jnp.dot(whole_bin, full_query, preferred_element_type=jnp.float32) + b_query[0]
        ).astype(jnp.bfloat16)
        keys = jnp.dot(whole_bin, full_key, preferred_element_type=jnp.float32).astype(jnp.bfloat16)
        values = (
            jnp.dot(whole_bin, full_value, preferred_element_type=jnp.float32) + b_value[0]
        ).astype(jnp.bfloat16)
        query_heads = query.reshape(bin_rows, local_heads, HD)
        key_heads = keys.reshape(bin_rows, local_heads, HD)
        value_heads = values.reshape(bin_rows, local_heads, HD)
        attn_heads, log_totals = attend_forward(
            query_heads, key_heads, value_heads, segment, block_rows, score_scale
        )
        attn = attn_heads.reshape(bin_rows, local_heads * HD)
        attn_partial = jnp.dot(attn, full_out, preferred_element_type=jnp.float32).reshape(
            dp_count, -1, model_width
        )
        branch = lax.psum_scatter(attn_partial, "tensor", scatter_dimension=1, tiled=True).reshape(
            -1, model_width
        )
        mid = own_rows.reshape(-1, model_width).astype(jnp.float32) + branch + bias_out
        hidden, normed_attn, spread_attn = layer_norm(mid, full_gain_attn, full_shift_attn)
        hidden_low = hidden.astype(jnp.bfloat16).reshape(dp_count, half_rows, model_width)
        hidden_whole = lax.all_gather(hidden_low, "tensor", axis=1, tiled=True).reshape(
            -1, model_width
        )
        inner = (
            jnp.dot(hidden_whole, full_inner, preferred_element_type=jnp.float32) + bias_inner[0]
        )
        gelu_value, gelu_pull = jax.vjp(partial(jax.nn.gelu, approximate=False), inner)
        gelu_low = gelu_value.astype(jnp.bfloat16)
        ffn_partial = jnp.dot(gelu_low, full_outer, preferred_element_type=jnp.float32).reshape(
            dp_count, -1, model_width
        )
        ffn = lax.psum_scatter(ffn_partial, "tensor", scatter_dimension=1, tiled=True).reshape(
            -1, model_width
        )
        top = hidden + ffn + bias_outer
        result, normed_ffn, spread_ffn = layer_norm(top, full_gain_ffn, full_shift_ffn)
        out_bins.append(result.astype(jnp.bfloat16).reshape(dp_count, half_rows, model_width))
        back_full = (
            lax.all_gather(w_query, "dp", axis=0, tiled=True),
            lax.all_gather(w_key, "dp", axis=0, tiled=True),
            lax.all_gather(w_value, "dp", axis=0, tiled=True),
            lax.all_gather(w_out, "dp", axis=1, tiled=True),
            lax.all_gather(w_inner, "dp", axis=0, tiled=True),
            lax.all_gather(w_outer, "dp", axis=1, tiled=True),
            lax.all_gather(gain_attn, "dp", axis=0, tiled=True),
            lax.all_gather(gain_ffn, "dp", axis=0, tiled=True),
        )
        (
            back_query,
            back_key,
            back_value,
            back_out,
            back_inner,
            back_outer,
            back_gain_attn,
            back_gain_ffn,
        ) = back_full
        grad_result = bin_grads[micro_step].reshape(-1, model_width).astype(jnp.float32)
        grad_top, grad_gain_ffn, grad_shift_ffn = norm_back(
            grad_result, normed_ffn, spread_ffn, back_gain_ffn
        )
        grad_ffn_low = grad_top.astype(jnp.bfloat16)
        grad_bias_outer = jnp.sum(grad_ffn_low.astype(jnp.float32), axis=0)
        grad_ffn_whole = lax.all_gather(
            grad_ffn_low.reshape(dp_count, half_rows, model_width), "tensor", axis=1, tiled=True
        ).reshape(-1, model_width)
        acc_outer = acc_outer + jnp.einsum(
            "nf,nd->fd", gelu_low, grad_ffn_whole, preferred_element_type=jnp.float32
        )
        grad_gelu = jnp.einsum(
            "nd,fd->nf", grad_ffn_whole, back_outer, preferred_element_type=jnp.float32
        )
        grad_inner_low = gelu_pull(grad_gelu)[0].astype(jnp.bfloat16)
        acc_bias_inner = acc_bias_inner + jnp.sum(grad_inner_low.astype(jnp.float32), axis=0)[None]
        acc_inner = acc_inner + jnp.einsum(
            "nd,nf->df", hidden_whole, grad_inner_low, preferred_element_type=jnp.float32
        )
        hidden_partial = jnp.einsum(
            "nf,df->nd", grad_inner_low, back_inner, preferred_element_type=jnp.float32
        ).reshape(dp_count, -1, model_width)
        grad_hidden = grad_top + lax.psum_scatter(
            hidden_partial, "tensor", scatter_dimension=1, tiled=True
        ).reshape(-1, model_width)
        grad_mid, grad_gain_attn, grad_shift_attn = norm_back(
            grad_hidden, normed_attn, spread_attn, back_gain_attn
        )
        grad_branch_low = grad_mid.astype(jnp.bfloat16)
        grad_bias_out = jnp.sum(grad_branch_low.astype(jnp.float32), axis=0)
        grad_branch_whole = lax.all_gather(
            grad_branch_low.reshape(dp_count, half_rows, model_width), "tensor", axis=1, tiled=True
        ).reshape(-1, model_width)
        acc_out = acc_out + jnp.einsum(
            "nh,nd->hd", attn, grad_branch_whole, preferred_element_type=jnp.float32
        )
        grad_attn_low = jnp.einsum(
            "nd,hd->nh", grad_branch_whole, back_out, preferred_element_type=jnp.float32
        ).astype(jnp.bfloat16)
        grad_heads = grad_attn_low.reshape(bin_rows, local_heads, HD)
        grad_query, grad_keys, grad_values = attend_backward(
            query_heads,
            key_heads,
            value_heads,
            grad_heads,
            log_totals,
            segment,
            block_rows,
            score_scale,
        )
        grad_query_low = grad_query.reshape(bin_rows, -1).astype(jnp.bfloat16)
        grad_key_low = grad_keys.reshape(bin_rows, -1).astype(jnp.bfloat16)
        grad_value_low = grad_values.reshape(bin_rows, -1).astype(jnp.bfloat16)
        acc_bias_query = acc_bias_query + jnp.sum(grad_query_low.astype(jnp.float32), axis=0)[None]
        acc_bias_value = acc_bias_value + jnp.sum(grad_value_low.astype(jnp.float32), axis=0)[None]
        acc_query = acc_query + jnp.einsum(
            "nd,nh->dh", whole_bin, grad_query_low, preferred_element_type=jnp.float32
        )
        acc_key = acc_key + jnp.einsum(
            "nd,nh->dh", whole_bin, grad_key_low, preferred_element_type=jnp.float32
        )
        acc_value = acc_value + jnp.einsum(
            "nd,nh->dh", whole_bin, grad_value_low, preferred_element_type=jnp.float32
        )
        input_partial = (
            jnp.einsum("nh,dh->nd", grad_query_low, back_query, preferred_element_type=jnp.float32)
            + jnp.einsum("nh,dh->nd", grad_key_low, back_key, preferred_element_type=jnp.float32)
            + jnp.einsum(
                "nh,dh->nd", grad_value_low, back_value, preferred_element_type=jnp.float32
            )
        )
        grad_input = grad_mid + lax.psum_scatter(
            input_partial.reshape(dp_count, -1, model_width).astype(jnp.bfloat16),
            "tensor",
            scatter_dimension=1,
            tiled=True,
        ).astype(jnp.float32).reshape(-1, model_width)
        grad_bins.append(grad_input.astype(jnp.bfloat16).reshape(dp_count, half_rows, model_width))
        acc_vectors = acc_vectors + jnp.stack(
            [
                grad_bias_out,
                grad_gain_attn,
                grad_shift_attn,
                grad_bias_outer,
                grad_gain_ffn,
                grad_shift_ffn,
            ]
        )
    out_stack = jnp.stack(out_bins)
    grad_stack = jnp.stack(grad_bins)
    send_out = jnp.take_along_axis(out_stack, arrived_place[:, :, None, None], axis=1)
    send_grad = jnp.take_along_axis(grad_stack, arrived_place[:, :, None, None], axis=1)
    back_out_rows, back_grad_rows = (
        lax.all_to_all(send_out, "dp", split_axis=1, concat_axis=1, tiled=True),
        lax.all_to_all(send_grad, "dp", split_axis=1, concat_axis=1, tiled=True),
    )
    layer_out = jnp.take_along_axis(back_out_rows, dest_dev[:, :, None, None], axis=1).reshape(
        tokens.shape
    )
    grad_tokens = jnp.take_along_axis(back_grad_rows, dest_dev[:, :, None, None], axis=1).reshape(
        tokens.shape
    )
    sum_query, sum_key, sum_value, sum_out, sum_inner, sum_outer, sum_bias_inner = (
        lax.psum_scatter(acc_query, "dp", scatter_dimension=0, tiled=True),
        lax.psum_scatter(acc_key, "dp", scatter_dimension=0, tiled=True),
        lax.psum_scatter(acc_value, "dp", scatter_dimension=0, tiled=True),
        lax.psum_scatter(acc_out, "dp", scatter_dimension=1, tiled=True),
        lax.psum_scatter(acc_inner, "dp", scatter_dimension=0, tiled=True),
        lax.psum_scatter(acc_outer, "dp", scatter_dimension=1, tiled=True),
        lax.psum_scatter(acc_bias_inner, "dp", scatter_dimension=1, tiled=True),
    )
    half_width = w_query.shape[1]
    tensor_pos = lax.axis_index("tensor")
    bias_pair = lax.dynamic_update_slice(
        jnp.zeros((2, model_width), jnp.float32),
        jnp.concatenate([acc_bias_query, acc_bias_value], axis=0),
        (jnp.int32(0), tensor_pos * half_width),
    )
    vectors, bias_total = lax.psum((acc_vectors, bias_pair), ("dp", "tensor"))
    own_width = model_width // dp_count
    vec_own = lax.dynamic_slice_in_dim(vectors, lax.axis_index("dp") * own_width, own_width, 1)
    bias_own = lax.dynamic_slice_in_dim(bias_total, tensor_pos * half_width, half_width, 1)
    return (
        layer_out,
        grad_tokens,
        sum_query,
        sum_key,
        sum_value,
        bias_own[0:1],
        bias_own[1:2],
        sum_out,
        vec_own[0],
        vec_own[1],
        vec_own[2],
        sum_inner,
        sum_bias_inner,
        sum_outer,
        vec_own[3],
        vec_own[4],
        vec_own[5],
    )


def solution(mesh):
    placed = (
        P("dp", "tensor", None),
        P("dp", "tensor", None),
        P("dp"),
        P("dp", None),
        P("dp", "tensor"),
        P("dp", "tensor"),
        P("dp", "tensor"),
        P("tensor", None),
        P("tensor", None),
        P("tensor", "dp"),
        P("dp"),
        P("dp"),
        P("dp"),
        P("dp", "tensor"),
        P("tensor", "dp"),
        P("tensor", "dp"),
        P("dp"),
        P("dp"),
        P("dp"),
    )
    dp_count = mesh.shape["dp"]

    def body(*args):
        tokens, w_query, b_inner = args[0], args[4], args[14]
        fits = (
            dp_count & (dp_count - 1) == 0
            and w_query.shape[0] % 16 == 0
            and tokens.shape[1] % 8 == 0
            and mesh.shape["tensor"] == 2
        )
        return (shards_fast if fits else shards)(*args)

    return jax.shard_map(
        body,
        mesh=mesh,
        in_specs=placed,
        out_specs=(
            P("dp", "tensor", None),
            P("dp", "tensor", None),
            P("dp", "tensor"),
            P("dp", "tensor"),
            P("dp", "tensor"),
            P("tensor", None),
            P("tensor", None),
            P("tensor", "dp"),
            P("dp"),
            P("dp"),
            P("dp"),
            P("dp", "tensor"),
            P("tensor", "dp"),
            P("tensor", "dp"),
            P("dp"),
            P("dp"),
            P("dp"),
        ),
        check_vma=False,
    )
```

```python
from functools import partial
import math

import jax
import jax.numpy as jnp
from jax import lax
from jax.experimental import pallas as pl
from jax.experimental.pallas import tpu as pltpu
from jax.sharding import PartitionSpec as P

HEADS = 12
HD = 64


EPS_NORM = 1e-12


def layer_norm(residual, norm_gain, norm_shift):
    centre = residual - jnp.mean(residual, axis=-1, keepdims=True)
    spread = lax.rsqrt(jnp.mean(centre * centre, axis=-1, keepdims=True) + EPS_NORM)
    normed = centre * spread
    return (normed * norm_gain + norm_shift, normed, spread)


def norm_back(grad_out, normed, spread, norm_gain):
    scaled = grad_out * norm_gain
    inner_term = (
        scaled
        - jnp.mean(scaled, axis=-1, keepdims=True)
        - normed * jnp.mean(scaled * normed, axis=-1, keepdims=True)
    )
    return (inner_term * spread, jnp.sum(grad_out * normed, axis=0), jnp.sum(grad_out, axis=0))


def segment_of(seq_lengths, count_rows):
    seq_ends = jnp.cumsum(seq_lengths)
    positions = jnp.arange(count_rows, dtype=jnp.int32)
    return jnp.sum((positions[:, None] >= seq_ends[None, :-1]).astype(jnp.int32), axis=1)


def masked_scores(query_block, key_heads, segment, first_row, block_rows, score_scale):
    scores = (
        jnp.einsum("qhd,khd->hqk", query_block, key_heads, preferred_element_type=jnp.float32)
        * score_scale
    )
    allowed = segment[first_row : first_row + block_rows, None] == segment[None, :]
    return jnp.where(allowed[None], scores, -1e30)


def attend_forward(query_heads, key_heads, value_heads, segment, block_rows, score_scale):
    scores = masked_scores(query_heads, key_heads, segment, 0, block_rows, score_scale)
    row_peak = jnp.max(scores, axis=-1, keepdims=True)
    exp_scores = jnp.exp(scores - row_peak)
    row_total = jnp.sum(exp_scores, axis=-1, keepdims=True)
    prob_low = (exp_scores / row_total).astype(jnp.bfloat16)
    out_block = jnp.einsum(
        "hqk,khd->qhd", prob_low, value_heads, preferred_element_type=jnp.float32
    )
    out_rows = out_block.astype(jnp.bfloat16)
    lse_rows = row_peak + jnp.log(row_total)
    return (out_rows, lse_rows)


def attend_backward(
    query_heads, key_heads, value_heads, grad_heads, log_totals, segment, block_rows, score_scale
):
    scores = masked_scores(query_heads, key_heads, segment, 0, block_rows, score_scale)
    probs_full = jnp.exp(scores - log_totals)
    prob_low = probs_full.astype(jnp.bfloat16)
    grad_values = jnp.einsum(
        "hqk,qhd->khd", prob_low, grad_heads, preferred_element_type=jnp.float32
    )
    grad_probs = jnp.einsum(
        "qhd,khd->hqk", grad_heads, value_heads, preferred_element_type=jnp.float32
    )
    row_inner = jnp.sum(probs_full * grad_probs, axis=-1, keepdims=True)
    grad_scores = (probs_full * (grad_probs - row_inner)).astype(jnp.bfloat16)
    grad_query_rows = (
        jnp.einsum("hqk,khd->qhd", grad_scores, key_heads, preferred_element_type=jnp.float32)
        * score_scale
    )
    grad_keys = (
        jnp.einsum("hqk,qhd->khd", grad_scores, query_heads, preferred_element_type=jnp.float32)
        * score_scale
    )
    return (grad_query_rows, grad_keys, grad_values)


MESH = pl.DeviceIdType.MESH
LANES = 128
NT = (((1,), (1,)), ((), ()))
NN = (((1,), (0,)), ((), ()))
F32 = jnp.float32
LOW = jnp.bfloat16
VMEM_BYTES = 63 << 20


def flip(place, bit):
    return place + bit * (1 - 2 * ((place // bit) % 2))


def bit_of(place, bit):
    return (place // bit) % 2


def bits_of(count):
    return tuple(1 << i for i in range(count.bit_length() - 1))[::-1]


def orders_of(count):
    bits = bits_of(count)
    return (bits, bits[:-2] + bits[-2:][::-1])


def mm(left, right, dims=NN):
    return lax.dot_general(left, right, dims, preferred_element_type=F32)


class Gather:
    def __init__(self, dp_count, place, half, order, ref, start, size, send_sem, recv_sem):
        self.place, self.half, self.order = place, half, order
        self.bits = bits_of(dp_count)
        self.ref, self.cols = ref, pl.ds(start, size)
        self.send_sem, self.recv_sem = send_sem, recv_sem

    def copy(self, stage):
        done = self.order[:stage]
        index = tuple(
            slice(None) if bit in done else bit_of(self.place, bit) for bit in self.bits
        ) + (slice(None), self.cols)
        return pltpu.make_async_remote_copy(
            src_ref=self.ref.at[index],
            dst_ref=self.ref.at[index],
            send_sem=self.send_sem.at[stage],
            recv_sem=self.recv_sem.at[stage],
            device_id=(flip(self.place, self.order[stage]), self.half),
            device_id_type=MESH,
        )


class Scatter:
    def __init__(self, dp_count, place, half, order, ref, start, size, landing, send_sem, recv_sem):
        self.place, self.half = place, half
        self.order = order
        self.bits = bits_of(dp_count)
        self.ref, self.cols = ref, pl.ds(start, size)
        self.landing = landing
        self.send_sem, self.recv_sem = send_sem, recv_sem

    def view(self, stage, chosen):
        left = [bit for bit in self.bits if bit not in self.order[:stage]]
        own = bit_of(self.place, self.order[stage])
        index = tuple(
            (own if chosen == "own" else 1 - own) if bit == self.order[stage] else slice(None)
            for bit in left
        )
        if stage == 0:
            return self.ref.at[index + (slice(None), self.cols)]
        return self.landing[stage - 1].at[index]

    def copy(self, stage):
        return pltpu.make_async_remote_copy(
            src_ref=self.view(stage, "other"),
            dst_ref=self.landing[stage],
            send_sem=self.send_sem.at[stage],
            recv_sem=self.recv_sem.at[stage],
            device_id=(flip(self.place, self.order[stage]), self.half),
            device_id_type=MESH,
        )

    def add(self, stage):
        kept = self.view(stage, "own")
        land = self.landing[stage]
        lead = land.shape[:-2]
        count = math.prod(lead)

        def one(i, carry):
            index, rest = [], i
            for extent in lead[::-1]:
                index.append(lax.rem(rest, extent))
                rest = rest // extent
            index = tuple(index[::-1])
            land[index] = (kept[index].astype(F32) + land[index].astype(F32)).astype(land.dtype)
            return carry

        if count == 1:
            one(0, 0)
        else:
            lax.fori_loop(0, count, one, 0)

    def finish(self, stage, outs):
        kept = self.view(stage, "own")
        sums, refs, copy_out = outs
        sums[:, self.cols] = kept[...].astype(F32) + self.landing[stage][...].astype(F32)
        first, begin = self.cols.start, 0
        for ref in refs:
            low = max(first, begin)
            high = min(first + self.cols.size, begin + ref.shape[1])
            if low < high:
                copy_out(sums.at[:, pl.ds(low, high - low)], ref.at[:, pl.ds(low - begin, high - low)])
            begin += ref.shape[1]


def layer(sizes, gather_plan, scatter_plan, *refs):
    dp_count, micro, rows, width, heads_wide, ff = sizes
    (
        tokens_ref,
        cot_ref,
        route_ref,
        lengths_ref,
        wq_ref,
        wk_ref,
        wv_ref,
        wo_ref,
        wi_ref,
        wu_ref,
        *small_refs,
        bq_ref,
        bv_ref,
        bi_ref,
        layer_out_hbm,
        grad_tokens_hbm,
        gq_hbm,
        gk_hbm,
        gv_hbm,
        go_hbm,
        gi_hbm,
        gu_hbm,
    ) = refs[:28]
    vec_out_ref = refs[28]
    (
        inverse_ref,
        target_ref,
        tokens_in,
        cot_in,
        layer_out_ref,
        grad_tokens_ref,
        sums,
        full,
        grads,
        x_send,
        dy_send,
        x_land,
        dy_land,
        out_send,
        gx_send,
        out_land,
        gx_land,
        xs,
        hs,
        gs,
        gb,
        flipped,
        xs_flipped,
        hs_flipped,
        qkv,
        dqkv,
        attn,
        gattn,
        probs,
        bias,
        gelu_low,
        dgelu,
        ginner,
        normed,
        spread,
        spread_ffn,
        grad_keep,
        own_part,
        part_send,
        part_land,
        last_send,
        last_land,
        piece,
        pieces,
        vec,
        vec_pair,
        vecg_buf,
        vecg_land,
        vec_acc,
        *rest,
    ) = refs[29:]
    stages = dp_count.bit_length() - 1
    landings = [rest[i * stages : (i + 1) * stages] for i in range(len(scatter_plan))]
    (
        x_sems,
        dy_sems,
        out_sems,
        gx_sems,
        gather_sems,
        scatter_sems,
        vec_sems,
        vecg_sems,
        pair_sems,
        in_sems,
        out_copy_sems,
    ) = rest[len(scatter_plan) * stages :]
    place, half = lax.axis_index("dp"), lax.axis_index("tensor")
    other = 1 - half
    bits = bits_of(dp_count)
    orders = orders_of(dp_count)
    bin_half = dp_count * rows
    tall = micro * bin_half
    blocks = micro * dp_count
    own_width = width // dp_count
    block_len = 2 * rows
    pairs = heads_wide // LANES
    key_col, value_col, out_col = heads_wide, 2 * heads_wide, 3 * heads_wide
    inner_col, outer_col = 4 * heads_wide, 4 * heads_wide + ff
    tile = heads_wide

    def weights(start, size):
        return full[(slice(None),) * stages + (slice(None), pl.ds(start, size))].reshape(width, size)

    def pair_copy(src, dst, which):
        return pltpu.make_async_remote_copy(
            src_ref=src,
            dst_ref=dst,
            send_sem=pair_sems.at[0, which],
            recv_sem=pair_sems.at[1, which],
            device_id=(place, other),
            device_id_type=MESH,
        )

    group = dp_count // 2
    base, within_group = place - lax.rem(place, group), lax.rem(place, group)
    far_base = lax.rem(base + group, dp_count)

    def message(step, sign, send_ref, recv_ref, sems, near):
        index = step if near else group + step
        peer = (base if near else far_base) + lax.rem(within_group + group + sign * step, group)
        return pltpu.make_async_remote_copy(
            src_ref=send_ref.at[peer],
            dst_ref=recv_ref.at[place if sign > 0 else peer],
            send_sem=sems.at[0, index],
            recv_sem=sems.at[1, index],
            device_id=(peer, half),
            device_id_type=MESH,
        )

    def push(send_ref, recv_ref, sems, near):
        def one(step, carry):
            message(step, 1, send_ref, recv_ref, sems, near).start()
            return carry

        lax.fori_loop(1 if near else 0, group, one, 0)

    def settle(send_ref, recv_ref, sems):
        recv_ref[place] = send_ref[place]
        for near in (True, False):

            def one(step, carry):
                message(step, -1, send_ref, recv_ref, sems, near).wait()
                return carry

            lax.fori_loop(1 if near else 0, group, one, 0)

    def arrange(src_ref, dst_ref):
        def one(i, carry):
            m, peer = i // dp_count, lax.rem(i, dp_count)
            dst_ref[peer, m] = src_ref[m * dp_count + inverse_ref[m, peer]]
            return carry

        lax.fori_loop(0, blocks, one, 0)

    barrier = pltpu.get_barrier_semaphore()

    def hello(step, carry):
        peer = lax.rem(place + step, dp_count)
        pl.semaphore_signal(barrier, inc=1, device_id=(peer, half), device_id_type=MESH)
        return carry

    lax.fori_loop(1, dp_count, hello, 0)
    pl.semaphore_signal(barrier, inc=1, device_id=(place, other), device_id_type=MESH)

    own = tuple(bit_of(place, bit) for bit in bits)
    fetches = [
        pltpu.make_async_copy(src, dst, in_sems.at[i])
        for i, (src, dst) in enumerate(
            [
                (ref, full.at[own + (slice(None), pl.ds(start, size))])
                for ref, start, size in (
                    (wq_ref, 0, heads_wide),
                    (wk_ref, key_col, heads_wide),
                    (wv_ref, value_col, heads_wide),
                    (wo_ref, out_col, heads_wide),
                    (wi_ref, inner_col, ff),
                    (wu_ref, outer_col, ff),
                )
            ]
            + [(tokens_ref, tokens_in), (cot_ref, cot_in)]
        )
    ]
    for fetch in fetches:
        fetch.start()
    leaving = []

    def copy_out(src, dst):
        copy = pltpu.make_async_copy(src, dst, out_copy_sems.at[len(leaving)])
        copy.start()
        leaving.append(copy)

    outs = (sums, (gq_hbm, gk_hbm, gv_hbm, go_hbm, gi_hbm, gu_hbm), copy_out)

    piece[...] = jnp.zeros((16, LANES), F32)
    for i, ref in enumerate(small_refs):
        piece[i : i + 1, 0:own_width] = ref[...].astype(F32).reshape(1, own_width)
    piece[8:16, 0 : bi_ref.shape[1]] = jnp.broadcast_to(bi_ref[...].astype(F32), (8, bi_ref.shape[1]))
    route = piece[6:7, 0:own_width]
    piece[7:8, 0:own_width] = route - dp_count * jnp.floor((route + 0.5) * (1.0 / dp_count))
    piece[6:7, 0:own_width] = jnp.floor((route + 0.5) * (1.0 / blocks))
    def find_target(i, carry):
        target_ref[i] = lax.div(route_ref[i], blocks)
        return carry


    def invert(i, carry):
        m, peer = lax.div(i, dp_count), lax.rem(i, dp_count)
        slot = jnp.int32(0)
        for k in range(dp_count):
            slot = jnp.where(target_ref[m * dp_count + k] == peer, k, slot)
        inverse_ref[m, peer] = slot
        return carry

    for fetch in fetches[:6]:
        fetch.wait()
    pl.semaphore_wait(barrier, dp_count)

    gathers = [
        Gather(
            dp_count,
            place,
            half,
            order,
            full,
            start,
            size,
            gather_sems.at[0, i],
            gather_sems.at[1, i],
        )
        for i, (group, order, start, size) in enumerate(gather_plan)
    ]
    gone = {}

    def advance(*groups):
        for wanted in groups:
            stage = gone.get(wanted, 0)
            gone[wanted] = stage + 1
            for (group, _, _, _), gather in zip(gather_plan, gathers):
                if group == wanted:
                    with jax.named_scope(f"gather_{wanted}_{stage}"):
                        if stage > 0:
                            gather.copy(stage - 1).wait_recv()
                        if stage < stages:
                            gather.copy(stage).start()

    def swing(buf, land, sems, stage, last_ref):
        copy = pltpu.make_async_remote_copy(
            src_ref=buf.at[stage],
            dst_ref=land.at[stage],
            send_sem=sems.at[0, stage],
            recv_sem=sems.at[1, stage],
            device_id=(flip(place, bits[stage]), half),
            device_id_type=MESH,
        )

        def fold():
            copy.wait()
            total = buf[stage] + land[stage]
            if stage < stages - 1:
                buf[stage + 1] = total
            else:
                last_ref[...] = total

        return copy.start, fold

    def push_piece(step, carry):
        peer = lax.rem(place + step, dp_count)
        pltpu.make_async_remote_copy(
            src_ref=piece,
            dst_ref=pieces.at[place],
            send_sem=vec_sems.at[0, step],
            recv_sem=vec_sems.at[1, step],
            device_id=(peer, half),
            device_id_type=MESH,
        ).start()
        return carry

    def wait_piece(step, carry):
        source = lax.rem(place + dp_count - step, dp_count)
        pltpu.make_async_remote_copy(
            src_ref=piece,
            dst_ref=pieces.at[source],
            send_sem=vec_sems.at[0, step],
            recv_sem=vec_sems.at[1, step],
            device_id=(source, half),
            device_id_type=MESH,
        ).wait()
        return carry

    advance(0, 4)
    lax.fori_loop(1, dp_count, push_piece, 0)
    advance(1)
    lax.fori_loop(0, blocks, find_target, 0)
    lax.fori_loop(0, blocks, invert, 0)
    fetches[6].wait()
    arrange(tokens_in, x_send)
    push(x_send, x_land, x_sems, True)
    advance(4)
    fetches[7].wait()
    arrange(cot_in, dy_send)
    advance(0)
    push(x_send, x_land, x_sems, False)
    pieces[place] = piece[...]
    lax.fori_loop(1, dp_count, wait_piece, 0)

    def lay(source, total):
        block = pieces[source]

        def laid(block, size, extent):
            target = lax.broadcasted_iota(jnp.int32, (LANES, extent), 1)
            at = lax.broadcasted_iota(jnp.int32, (LANES, extent), 0)
            hit = (target == at + source * size) & (at < size)
            return mm(block.astype(LOW), hit.astype(F32).astype(LOW))

        return (
            total[0] + laid(block[0:8], own_width, width),
            total[1] + laid(block[8:16], bi_ref.shape[1], ff),
        )

    short, long = lax.fori_loop(
        0, dp_count, lay, (jnp.zeros((8, width), F32), jnp.zeros((8, ff), F32))
    )
    vec[0:8, :] = short
    for i in range(ff // width):
        vec[8 + i : 9 + i, :] = long[0:1, i * width : (i + 1) * width]

    placed = jnp.where(vec[6:7, :] == place.astype(F32), vec[7:8, :], 0.0)
    placed_rows = jnp.broadcast_to(placed, (8, blocks * dp_count))

    def mask_bin(m, carry):
        shape = (2 * bin_half, blocks * dp_count)
        row = lax.broadcasted_iota(jnp.int32, shape, 0)
        lane = lax.broadcasted_iota(jnp.int32, shape, 1)
        source = lax.rem(row, bin_half) // rows
        chosen = (lane // dp_count) == source * micro + m
        tall_place = jnp.sum(jnp.where(chosen, placed, 0.0), axis=1, keepdims=True)
        wide_place = mm(placed_rows, chosen.astype(F32), NT)[0:1, :]
        ends, end = [], 0
        for i in range(lengths_ref.shape[1] - 1):
            end = end + lengths_ref[m, i]
            ends.append(end.astype(F32))

        def sequence(at, index):
            within = (lax.rem(index, rows) + (index // bin_half) * rows).astype(F32)
            position = at * block_len + within
            return sum((position >= end).astype(F32) for end in ends)

        down = sequence(
            tall_place, lax.broadcasted_iota(jnp.int32, (2 * bin_half, 1), 0)
        )
        across = sequence(
            wide_place, lax.broadcasted_iota(jnp.int32, (1, 2 * bin_half), 1)
        )
        bias[m] = jnp.where(down == across, 0.0, -1e30)
        return carry

    lax.fori_loop(0, micro, mask_bin, 0)

    advance(0, 1)
    advance(2)
    advance(0, 1)
    advance(3)
    advance(1)
    advance(0)
    advance(2)
    settle(x_send, x_land, x_sems)

    def order_rows(m, carry):
        block = x_land[:, m].astype(F32).reshape(bin_half, width)
        xs[half, pl.ds(pl.multiple_of(m * bin_half, bin_half), bin_half), :] = block.astype(LOW)
        return carry

    lax.fori_loop(0, micro, order_rows, 0)
    swap_x = pair_copy(xs.at[half], xs.at[half], 0)
    swap_x.start()
    advance(3, 4)
    swap_x.wait()

    def project(i, carry):
        h = lax.rem(half + i, 2)
        own_rows = xs[h]
        qkv[h, :, pl.ds(0, heads_wide)] = (
            (mm(own_rows, weights(0, heads_wide)) + bq_ref[...].astype(F32)).astype(LOW)
            * LOW(HD ** (-0.5))
        )
        qkv[h, :, pl.ds(key_col, heads_wide)] = mm(own_rows, weights(key_col, heads_wide)).astype(LOW)
        qkv[h, :, pl.ds(value_col, heads_wide)] = (
            mm(own_rows, weights(value_col, heads_wide)) + bv_ref[...].astype(F32)
        ).astype(LOW)
        return carry

    lax.fori_loop(0, 2, project, 0)

    low_lane = lax.broadcasted_iota(jnp.int32, (2 * bin_half, LANES), 1) < HD
    nothing = jnp.zeros((2 * bin_half, LANES), LOW)

    def bin_of(ref, m, start):
        at = pl.ds(pl.multiple_of(m * bin_half, bin_half), bin_half)
        return jnp.concatenate([ref[0, at, pl.ds(start, LANES)], ref[1, at, pl.ds(start, LANES)]], axis=0)

    def put_bin(ref, m, start, value):
        at = pl.ds(pl.multiple_of(m * bin_half, bin_half), bin_half)
        ref[0, at, pl.ds(start, LANES)] = value[:bin_half].astype(ref.dtype)
        ref[1, at, pl.ds(start, LANES)] = value[bin_half:].astype(ref.dtype)

    def split_heads(value):
        return (jnp.where(low_lane, value, nothing), jnp.where(low_lane, nothing, value))

    def attend(m):
        for j in range(pairs):
            query = bin_of(qkv, m, j * LANES)
            key = bin_of(qkv, m, key_col + j * LANES)
            value = bin_of(qkv, m, value_col + j * LANES)
            total = None
            for e, (query_e, value_e) in enumerate(zip(split_heads(query), split_heads(value))):
                score = mm(query_e, key, NT) + bias[m]
                power = jnp.exp(score - jnp.max(score, axis=1, keepdims=True))
                prob = power * (1.0 / jnp.sum(power, axis=1, keepdims=True))
                probs[m, 2 * j + e] = prob.astype(probs.dtype)
                part = mm(prob.astype(LOW), value_e)
                total = part if total is None else total + part
            put_bin(attn, m, j * LANES, total)

    for m in range(micro):
        attend(m)
        if m == 0:
            advance(2, 1)
        if m == 1:
            advance(3)
        if m == 2:
            advance(4, 2)
            push(dy_send, dy_land, dy_sems, False)
    def two_halves(left_ref, columns, start, send_ref, which, land_ref):
        away = mm(left_ref[other], weights(start, columns), NT)
        send_ref[...] = away.astype(send_ref.dtype)
        copy = pair_copy(send_ref, land_ref, which)
        copy.start()
        own_part[...] = mm(left_ref[half], weights(start, columns), NT)
        return copy


    copy = two_halves(attn, heads_wide, out_col, part_send, 1, part_land.at[0])
    chunk = 4 * rows
    per_bin = bin_half // chunk
    chunks = tall // chunk
    ones = jnp.ones((8, tall), LOW)

    def mean_of(v):
        return jnp.sum(v, axis=1, keepdims=True) * (1.0 / width)

    copy.wait()

    def norm_attn(i, carry):
        at = pl.ds(pl.multiple_of(i * chunk, chunk), chunk)
        mid = xs[half, at, :].astype(F32) + (own_part[at, :] + part_land[0, at, :]) + vec[0:1, :]
        centre = mid - mean_of(mid)
        inverse_s = lax.rsqrt(mean_of(centre * centre) + EPS_NORM)
        unit = centre * inverse_s
        normed[at, :] = unit
        spread[at, :] = jnp.broadcast_to(inverse_s, (chunk, LANES))
        hs[half, at, :] = (unit * vec[1:2, :] + vec[2:3, :]).astype(LOW)
        return carry

    lax.fori_loop(0, chunks, norm_attn, 0)
    swap_h = pair_copy(hs.at[half], hs.at[half], 2)
    swap_h.start()
    advance(2, 3)
    push(dy_send, dy_land, dy_sems, True)

    def widen(h):
        for i in range(ff // tile):
            start = i * tile
            row = 8 + start // width
            inner = mm(hs[h], weights(inner_col + start, tile)) + vec[
                row : row + 1, start % width : start % width + tile
            ]
            cdf = 0.5 * (1.0 + lax.erf(inner * (0.5**0.5)))
            density = jnp.exp(-0.5 * inner * inner) * ((2.0 * math.pi) ** -0.5)
            gelu_low[h, :, start : start + tile] = (inner * cdf).astype(LOW)
            dgelu[h, :, start : start + tile] = (cdf + inner * density).astype(dgelu.dtype)

    def widen_step(i, carry):
        @pl.when(i == 1)
        def _():
            swap_h.wait()

        widen(lax.rem(half + i, 2))
        return carry

    lax.fori_loop(0, 2, widen_step, 0)
    xs_flipped[...] = xs[...].reshape(2 * tall, width).T
    hs_flipped[...] = hs[...].reshape(2 * tall, width).T
    advance(3, 4)
    copy = two_halves(gelu_low, ff, outer_col, part_send, 3, part_land.at[1])
    copy.wait()

    def fold_rows(v):
        return jnp.sum(v.reshape(chunk // 8, 8, width), axis=0)

    def norm_ffn(i, carry):
        at = pl.ds(pl.multiple_of(i * chunk, chunk), chunk)
        m, quarter = i // per_bin, lax.rem(i, per_bin)
        sources = pl.ds(quarter * (chunk // rows), chunk // rows)
        hidden = normed[at, :] * vec[1:2, :] + vec[2:3, :]
        top = hidden + (own_part[at, :] + part_land[1, at, :]) + vec[3:4, :]
        centre = top - mean_of(top)
        inverse_s = lax.rsqrt(mean_of(centre * centre) + EPS_NORM)
        unit = centre * inverse_s
        own_part[at, :] = unit
        spread_ffn[at, :] = jnp.broadcast_to(inverse_s, (chunk, LANES))
        result = unit * vec[4:5, :] + vec[5:6, :]
        out_send[sources, m] = result.reshape(chunk // rows, rows, width).astype(LOW)
        return carry

    lax.fori_loop(0, chunks, norm_ffn, 0)
    push(out_send, out_land, out_sems, False)
    push(out_send, out_land, out_sems, True)
    settle(dy_send, dy_land, dy_sems)
    for i in range(3):
        vec_acc[i] = jnp.zeros((8, width), F32)

    def norm_ffn_back(i, carry):
        at = pl.ds(pl.multiple_of(i * chunk, chunk), chunk)
        m, quarter = i // per_bin, lax.rem(i, per_bin)
        sources = pl.ds(quarter * (chunk // rows), chunk // rows)
        unit = own_part[at, :]
        dy = dy_land[sources, m].astype(F32).reshape(chunk, width)
        vec_acc[0] = vec_acc[0] + fold_rows(dy * unit)
        vec_acc[1] = vec_acc[1] + fold_rows(dy)
        scaled = dy * vec[4:5, :]
        grad_top = (scaled - mean_of(scaled) - unit * mean_of(scaled * unit)) * spread_ffn[at, 0:1]
        grad_keep[at, :] = grad_top
        gs[half, at, :] = grad_top.astype(LOW)
        return carry

    lax.fori_loop(0, chunks, norm_ffn_back, 0)
    swap_g = pair_copy(gs.at[half], gs.at[half], 4)
    swap_g.start()
    vecg_buf[0, 4:5, :] = jnp.sum(vec_acc[0], axis=0, keepdims=True)
    vecg_buf[0, 5:6, :] = jnp.sum(vec_acc[1], axis=0, keepdims=True)
    vecg_buf[0, 3:4, :] = mm(ones, gs[half])[0:1, :]

    def narrow(h):
        for i in range(ff // tile):
            start = i * tile
            grad = mm(gs[h], weights(outer_col + start, tile)) * dgelu[h, :, start : start + tile].astype(F32)
            ginner[h, :, start : start + tile] = grad.astype(LOW)

    narrow(half)
    swap_g.wait()

    scatters = [
        Scatter(
            dp_count,
            place,
            half,
            order,
            grads,
            start,
            size,
            landings[i],
            scatter_sems.at[0, i],
            scatter_sems.at[1, i],
        )
        for i, (group, order, start, size) in enumerate(scatter_plan)
    ]
    sent = {}

    def reduce(*groups):
        for wanted in groups:
            stage = sent.get(wanted, 0)
            sent[wanted] = stage + 1
            for (group, _, _, _), scatter in zip(scatter_plan, scatters):
                if group == wanted:
                    with jax.named_scope(f"reduce_{wanted}_{stage}"):
                        if stage > 0:
                            scatter.copy(stage - 1).wait_recv()
                            if stage < stages:
                                scatter.add(stage - 1)
                            else:
                                scatter.finish(stage - 1, outs)
                        if stage < stages:
                            scatter.copy(stage).start()

    def grad_columns(left_t, right_ref, start, columns, grads_start):
        for i in range(columns // tile):
            piece = mm(left_t, right_ref[:, :, start + i * tile : start + (i + 1) * tile].reshape(2 * tall, tile))
            grads[(slice(None),) * (stages + 1) + (pl.ds(grads_start + i * tile, tile),)] = piece.astype(
                LOW
            ).reshape(bits_shape + (own_width, tile))

    bits_shape = (2,) * stages
    flipped[...] = gs[...].reshape(2 * tall, width).T
    grad_columns(flipped[...], gelu_low, 0, ff // 2, outer_col)
    reduce(0)
    grad_columns(flipped[...], gelu_low, ff // 2, ff // 2, outer_col + ff // 2)
    reduce(1)
    narrow(other)
    copy = two_halves(ginner, ff, inner_col, part_send, 5, part_land.at[2])
    for i in range(ff // width):
        columns = slice(i * width, (i + 1) * width)
        vecg_buf[0, 6 + i : 7 + i, :] = (mm(ones, ginner[0, :, columns]) + mm(ones, ginner[1, :, columns]))[0:1, :]
    copy.wait()
    for i in range(3):
        vec_acc[i] = jnp.zeros((8, width), F32)

    def norm_back(i, carry):
        at = pl.ds(pl.multiple_of(i * chunk, chunk), chunk)
        grad_hidden = grad_keep[at, :] + (own_part[at, :] + part_land[2, at, :])
        unit = normed[at, :]
        vec_acc[0] = vec_acc[0] + fold_rows(grad_hidden * unit)
        vec_acc[1] = vec_acc[1] + fold_rows(grad_hidden)
        scaled = grad_hidden * vec[1:2, :]
        grad_mid = (scaled - mean_of(scaled) - unit * mean_of(scaled * unit)) * spread[at, 0:1]
        grad_keep[at, :] = grad_mid
        gb[half, at, :] = grad_mid.astype(LOW)
        return carry

    lax.fori_loop(0, chunks, norm_back, 0)
    swap_b = pair_copy(gb.at[half], gb.at[half], 6)
    swap_b.start()
    vecg_buf[0, 1:2, :] = jnp.sum(vec_acc[0], axis=0, keepdims=True)
    vecg_buf[0, 2:3, :] = jnp.sum(vec_acc[1], axis=0, keepdims=True)
    vecg_buf[0, 0:1, :] = mm(ones, gb[half])[0:1, :]
    grad_columns(hs_flipped[...], ginner, 0, ff, inner_col)
    swap_b.wait()
    flipped[...] = gb[...].reshape(2 * tall, width).T
    grad_columns(flipped[...], attn, 0, heads_wide, out_col)
    reduce(2)

    def to_heads(h, carry):
        gattn[h] = mm(gb[h], weights(out_col, heads_wide)).astype(LOW)
        return carry

    lax.fori_loop(0, 2, to_heads, 0)

    def attend_back(m):
        for j in range(pairs):
            query = bin_of(qkv, m, j * LANES)
            key = bin_of(qkv, m, key_col + j * LANES)
            value = bin_of(qkv, m, value_col + j * LANES)
            grad = bin_of(gattn, m, j * LANES)
            keys, queries, upstream = split_heads(key), split_heads(query), split_heads(grad)
            d_query = d_key = d_value = None
            for e in range(2):
                prob = probs[m, 2 * j + e].astype(F32)
                d_prob = mm(upstream[e], value, NT)
                inner = jnp.sum(prob * d_prob, axis=1, keepdims=True)
                d_score = (prob * (d_prob - inner)).astype(LOW)
                part_q = mm(d_score, keys[e])
                part_k = mm(d_score.T, queries[e])
                part_v = mm(prob.astype(LOW).T, upstream[e])
                d_query = part_q if d_query is None else d_query + part_q
                d_key = part_k if d_key is None else d_key + part_k
                d_value = part_v if d_value is None else d_value + part_v
            put_bin(dqkv, m, j * LANES, d_query * (HD ** (-0.5)))
            put_bin(dqkv, m, key_col + j * LANES, d_key)
            put_bin(dqkv, m, value_col + j * LANES, d_value)

    for m in range(micro):
        attend_back(m)
        if m == 1:
            reduce(0, 1)

    away = mm(dqkv[other], weights(0, 3 * heads_wide), NT)
    last_send[...] = away.astype(LOW)
    copy = pair_copy(last_send, last_land, 7)
    copy.start()
    grad_columns(xs_flipped[...], dqkv, 0, 3 * heads_wide, 0)
    reduce(3)
    own_part[...] = mm(dqkv[half], weights(0, 3 * heads_wide), NT)
    copy.wait()

    def leave(i, carry):
        at = pl.ds(pl.multiple_of(i * chunk, chunk), chunk)
        m, quarter = i // per_bin, lax.rem(i, per_bin)
        sources = pl.ds(quarter * (chunk // rows), chunk // rows)
        grad_x = grad_keep[at, :] + (own_part[at, :] + last_land[at, :].astype(F32))
        gx_send[sources, m] = grad_x.reshape(chunk // rows, rows, width).astype(LOW)
        return carry

    lax.fori_loop(0, chunks, leave, 0)
    push(gx_send, gx_land, gx_sems, False)
    push(gx_send, gx_land, gx_sems, True)
    reduce(0, 1)
    for i, start in enumerate((0, value_col)):
        columns = slice(start, start + heads_wide)
        vecg_buf[0, 8:9, i * heads_wide : (i + 1) * heads_wide] = (
            mm(ones, dqkv[0, :, columns]) + mm(ones, dqkv[1, :, columns])
        )[0:1, :]
    vecg_buf[0, 9:16, :] = jnp.zeros((7, width), F32)

    swap_v = pair_copy(vecg_buf.at[0], vec_pair, 8)
    swap_v.start()
    swap_v.wait()
    vecg_buf[0, 0:6, :] = vecg_buf[0, 0:6, :] + vec_pair[0:6, :]

    def hand_back(land_ref, result_ref, hbm_ref):
        def one(i, carry):
            result_ref[i] = land_ref[target_ref[i], i // dp_count]
            return carry

        lax.fori_loop(0, blocks, one, 0)
        copy_out(result_ref, hbm_ref)

    begin, fold = swing(vecg_buf, vecg_land, vecg_sems, 0, vec_out_ref)
    begin()
    reduce(2)
    fold()
    begin, fold = swing(vecg_buf, vecg_land, vecg_sems, 1, vec_out_ref)
    begin()
    settle(out_send, out_land, out_sems)
    hand_back(out_land, layer_out_ref, layer_out_hbm)
    reduce(1, 0)
    reduce(2)
    fold()
    begin, fold = swing(vecg_buf, vecg_land, vecg_sems, 2, vec_out_ref)
    begin()
    reduce(1, 0)
    reduce(3)
    fold()
    begin, fold = swing(vecg_buf, vecg_land, vecg_sems, 3, vec_out_ref)
    begin()
    reduce(2)
    reduce(3)
    reduce(2)
    fold()
    reduce(3)
    settle(gx_send, gx_land, gx_sems)
    hand_back(gx_land, grad_tokens_ref, grad_tokens_hbm)
    reduce(3)
    for copy in leaving:
        copy.wait()
    assert all(n == stages + 1 for n in (*gone.values(), *sent.values()))
    for gather in gathers:
        for stage in range(stages):
            gather.copy(stage).wait_send()
    for scatter in scatters:
        for stage in range(stages):
            scatter.copy(stage).wait_send()


def finish(*refs):
    sources, total_ref, targets = refs[:8], refs[8], refs[9:17]
    own_ref, inner_ref, query_ref, value_ref, *held, sems = refs[17:]
    loads = [pltpu.make_async_copy(src, hold, sems.at[0, i]) for i, (src, hold) in enumerate(zip(sources, held))]
    stores = [pltpu.make_async_copy(hold, dst, sems.at[1, i]) for i, (hold, dst) in enumerate(zip(held, targets))]
    for load in loads:
        load.start()
    for load, store in zip(loads, stores):
        load.wait()
        store.start()
    place = lax.axis_index("dp")

    def cut(row, size):
        extent = row.shape[1]
        source = lax.broadcasted_iota(jnp.int32, (extent, size), 0)
        at = lax.broadcasted_iota(jnp.int32, (extent, size), 1) + place * size
        return lax.dot_general(
            row,
            (source == at).astype(F32),
            NN,
            precision=lax.Precision.HIGHEST,
            preferred_element_type=F32,
        )

    own_ref[...] = cut(total_ref[0:8, :], own_ref.shape[1])
    width, heads_wide = total_ref.shape[1], query_ref.shape[1]
    rows = inner_ref.shape[1] * lax.axis_size("dp") // width
    long = jnp.concatenate([total_ref[6 + i : 7 + i, :] for i in range(rows)], axis=1)
    inner_ref[...] = cut(jnp.broadcast_to(long, (8, long.shape[1])), inner_ref.shape[1])[0:1, :]
    query_ref[...] = total_ref[8:9, :heads_wide]
    value_ref[...] = total_ref[8:9, heads_wide:]
    for store in stores:
        store.wait()


def plans(dp_count, heads_wide, ff):
    bits = bits_of(dp_count)
    far, near = bits[:-2], bits[-2:]
    far_first = (far + near, far + near[::-1])
    near_first = (near[::-1] + far, near + far)
    inner_col, outer_col = 4 * heads_wide, 4 * heads_wide + ff

    def plan_of(cuts):
        plan = []
        for group, (orders, start, stop) in enumerate(cuts):
            middle = start + (stop - start + LANES) // (2 * LANES) * LANES
            plan.append((group, orders[0], start, middle - start))
            plan.append((group, orders[1], middle, stop - middle))
        return plan

    gather = plan_of(
        [
            (far_first, 0, 3 * heads_wide),
            (far_first, 3 * heads_wide, inner_col + ff // 2),
            (far_first, inner_col + ff // 2, outer_col),
            (far_first, outer_col, outer_col + ff // 2),
            (near_first, outer_col + ff // 2, outer_col + ff),
        ]
    )
    back = lambda orders: (orders[0][::-1], orders[1][::-1])
    scatter = plan_of(
        [
            (back(far_first), outer_col, outer_col + ff // 2),
            (back(near_first), outer_col + ff // 2, outer_col + ff),
            (back(far_first), 3 * heads_wide, outer_col),
            (back(far_first), 0, 3 * heads_wide),
        ]
    )
    return gather, scatter


def shards_fast(
    tokens,
    cotangent,
    block_route,
    lengths,
    w_query,
    w_key,
    w_value,
    b_query,
    b_value,
    w_out,
    b_out,
    gain_attn,
    shift_attn,
    w_inner,
    b_inner,
    w_outer,
    b_outer,
    gain_ffn,
    shift_ffn,
):
    dp_count = lax.axis_size("dp")
    micro, rows, width = lengths.shape[0], tokens.shape[1], tokens.shape[2]
    heads_wide, ff = w_query.shape[1], w_inner.shape[1]
    place = lax.axis_index("dp")
    blocks = micro * dp_count
    own_width = width // dp_count
    columns = 4 * heads_wide + 2 * ff
    stages = dp_count.bit_length() - 1
    bits = (2,) * stages
    inner_col, outer_col = 4 * heads_wide, 4 * heads_wide + ff
    gather_plan, scatter_plan = plans(dp_count, heads_wide, ff)
    bin_half = dp_count * rows
    tall = micro * bin_half
    vmem, smem = pl.BlockSpec(memory_space=pltpu.VMEM), pl.BlockSpec(memory_space=pltpu.SMEM)
    dma = pltpu.SemaphoreType.DMA
    swap_shape = (dp_count, micro, rows, width)
    scratch = [
        pltpu.SMEM((micro, dp_count), jnp.int32),
        pltpu.SMEM((blocks,), jnp.int32),
        pltpu.VMEM(tokens.shape, LOW),
        pltpu.VMEM(tokens.shape, LOW),
        pltpu.VMEM(tokens.shape, LOW),
        pltpu.VMEM(tokens.shape, LOW),
        pltpu.VMEM((own_width, columns), F32),
        pltpu.VMEM(bits + (own_width, columns), LOW),
        pltpu.VMEM(bits + (own_width, columns), LOW),
    ]
    scratch += [pltpu.VMEM(swap_shape, LOW) for _ in range(8)]
    scratch += [pltpu.VMEM((2, tall, width), LOW) for _ in range(4)]
    scratch += [pltpu.VMEM((width, 2 * tall), LOW) for _ in range(3)]
    scratch += [pltpu.VMEM((2, tall, 3 * heads_wide), LOW) for _ in range(2)]
    scratch += [pltpu.VMEM((2, tall, heads_wide), LOW) for _ in range(2)]
    scratch += [
        pltpu.VMEM((micro, heads_wide // HD, 2 * bin_half, 2 * bin_half), LOW),
        pltpu.VMEM((micro, 2 * bin_half, 2 * bin_half), F32),
    ]
    scratch += [pltpu.VMEM((2, tall, ff), LOW) for _ in range(3)]
    scratch += [
        pltpu.VMEM((tall, width), F32),
        pltpu.VMEM((tall, LANES), F32),
        pltpu.VMEM((tall, LANES), F32),
        pltpu.VMEM((tall, width), F32),
        pltpu.VMEM((tall, width), F32),
        pltpu.VMEM((tall, width), F32),
        pltpu.VMEM((3, tall, width), F32),
        pltpu.VMEM((tall, width), LOW),
        pltpu.VMEM((tall, width), LOW),
        pltpu.VMEM((16, LANES), F32),
        pltpu.VMEM((dp_count, 16, LANES), F32),
        pltpu.VMEM((16, width), F32),
        pltpu.VMEM((16, width), F32),
        pltpu.VMEM((stages, 16, width), F32),
        pltpu.VMEM((stages, 16, width), F32),
        pltpu.VMEM((3, 8, width), F32),
    ]
    scratch += [
        pltpu.VMEM((2,) * (stages - 1 - stage) + (own_width, size), LOW)
        for _, _, _, size in scatter_plan
        for stage in range(stages)
    ]
    scratch += [dma((2, dp_count)) for _ in range(4)]
    scratch += [
        dma((2, len(gather_plan), stages)),
        dma((2, len(scatter_plan), stages)),
        dma((2, dp_count)),
        dma((2, stages)),
        dma((2, 9)),
        dma((8,)),
        dma((32,)),
    ]
    sizes = (dp_count, micro, rows, width, heads_wide, ff)
    hbm = pl.BlockSpec(memory_space=pl.ANY)
    grad_shapes = [jax.ShapeDtypeStruct((own_width, size), F32) for size in (heads_wide,) * 4 + (ff,) * 2]
    made = (
        jax.ShapeDtypeStruct(tokens.shape, tokens.dtype),
        jax.ShapeDtypeStruct(tokens.shape, tokens.dtype),
        *grad_shapes,
    )
    *big, total = pl.pallas_call(
        partial(layer, sizes, gather_plan, scatter_plan),
        out_shape=(*made, jax.ShapeDtypeStruct((16, width), F32)),
        in_specs=[hbm] * 2 + [smem] * 2 + [hbm] * 6 + [vmem] * 10,
        out_specs=[hbm] * 8 + [vmem],
        scratch_shapes=scratch,
        compiler_params=pltpu.CompilerParams(
            collective_id=0, has_side_effects=True, vmem_limit_bytes=VMEM_BYTES
        ),
        name="layer",
    )(
        tokens,
        cotangent,
        block_route,
        lengths,
        w_query,
        w_key,
        w_value,
        w_out.T,
        w_inner,
        w_outer.T,
        b_out,
        gain_attn,
        shift_attn,
        b_outer,
        gain_ffn,
        shift_ffn,
        block_route,
        b_query,
        b_value,
        b_inner,
    )
    own_inner = b_inner.shape[1]
    *big, own, bias_inner, bias_query, bias_value = pl.pallas_call(
        finish,
        out_shape=(
            *made,
            jax.ShapeDtypeStruct((8, own_width), F32),
            jax.ShapeDtypeStruct((1, own_inner), F32),
            jax.ShapeDtypeStruct((1, heads_wide), F32),
            jax.ShapeDtypeStruct((1, heads_wide), F32),
        ),
        in_specs=[hbm] * 8 + [vmem],
        out_specs=[hbm] * 8 + [vmem] * 4,
        scratch_shapes=[pltpu.VMEM(result.shape, result.dtype) for result in made] + [dma((2, 8))],
        name="finish",
    )(*big, total)
    layer_out, grad_tokens, gq, gk, gv, go, gi, gu = big
    return (
        layer_out,
        grad_tokens,
        gq,
        gk,
        gv,
        bias_query,
        bias_value,
        go.T,
        own[0],
        own[1],
        own[2],
        gi,
        bias_inner,
        gu.T,
        own[3],
        own[4],
        own[5],
    )


def shards(
    tokens,
    cotangent,
    block_route,
    lengths,
    w_query,
    w_key,
    w_value,
    b_query,
    b_value,
    w_out,
    b_out,
    gain_attn,
    shift_attn,
    w_inner,
    b_inner,
    w_outer,
    b_outer,
    gain_ffn,
    shift_ffn,
):
    dp_count = lax.axis_size("dp")
    micro_count = lengths.shape[0]
    half_rows = tokens.shape[1]
    model_width = tokens.shape[2]
    local_heads = HEADS // lax.axis_size("tensor")
    score_scale = HD ** (-0.5)
    blocks = tokens.reshape(micro_count, dp_count, half_rows, model_width)
    upstream = cotangent.reshape(micro_count, dp_count, half_rows, model_width)
    target = block_route.reshape(micro_count, dp_count)
    dest_dev = target // (micro_count * dp_count)
    bin_place = target % dp_count
    micro_ids = jnp.broadcast_to(
        jnp.arange(micro_count, dtype=jnp.int32)[:, None], (micro_count, dp_count)
    )
    slot_ids = jnp.broadcast_to(
        jnp.arange(dp_count, dtype=jnp.int32)[None, :], (micro_count, dp_count)
    )
    inverse = jnp.zeros((micro_count, dp_count), jnp.int32).at[micro_ids, dest_dev].set(slot_ids)
    by_dest = jnp.take_along_axis(blocks, inverse[:, :, None, None], axis=1)
    grad_dest = jnp.take_along_axis(upstream, inverse[:, :, None, None], axis=1)
    place_dest = jnp.take_along_axis(bin_place, inverse, axis=1)
    arrived, arrived_grad, arrived_place = (
        lax.all_to_all(by_dest, "dp", split_axis=1, concat_axis=1, tiled=True),
        lax.all_to_all(grad_dest, "dp", split_axis=1, concat_axis=1, tiled=True),
        lax.all_to_all(place_dest, "dp", split_axis=1, concat_axis=1, tiled=True),
    )
    anchor = (
        jnp.zeros((micro_count, dp_count), jnp.int32).at[micro_ids, arrived_place].set(slot_ids)
    )
    bin_tokens = jnp.take_along_axis(arrived, anchor[:, :, None, None], axis=1)
    bin_grads = jnp.take_along_axis(arrived_grad, anchor[:, :, None, None], axis=1)
    acc_query = jnp.zeros((model_width, w_query.shape[1]), jnp.float32)
    acc_key = jnp.zeros((model_width, w_key.shape[1]), jnp.float32)
    acc_value = jnp.zeros((model_width, w_value.shape[1]), jnp.float32)
    acc_out = jnp.zeros((w_out.shape[0], model_width), jnp.float32)
    acc_inner = jnp.zeros((model_width, w_inner.shape[1]), jnp.float32)
    acc_outer = jnp.zeros((w_outer.shape[0], model_width), jnp.float32)
    acc_bias_query = jnp.zeros((1, w_query.shape[1]), jnp.float32)
    acc_bias_value = jnp.zeros((1, w_value.shape[1]), jnp.float32)
    acc_bias_inner = jnp.zeros((1, w_inner.shape[1]), jnp.float32)
    acc_vectors = jnp.zeros((6, model_width), jnp.float32)
    out_bins = []
    grad_bins = []
    for micro_step in range(micro_count):
        gathered = (
            lax.all_gather(w_query, "dp", axis=0, tiled=True),
            lax.all_gather(w_key, "dp", axis=0, tiled=True),
            lax.all_gather(w_value, "dp", axis=0, tiled=True),
            lax.all_gather(w_out, "dp", axis=1, tiled=True),
            lax.all_gather(w_inner, "dp", axis=0, tiled=True),
            lax.all_gather(w_outer, "dp", axis=1, tiled=True),
            lax.all_gather(b_inner, "dp", axis=1, tiled=True),
            lax.all_gather(b_out, "dp", axis=0, tiled=True),
            lax.all_gather(gain_attn, "dp", axis=0, tiled=True),
            lax.all_gather(shift_attn, "dp", axis=0, tiled=True),
            lax.all_gather(b_outer, "dp", axis=0, tiled=True),
            lax.all_gather(gain_ffn, "dp", axis=0, tiled=True),
            lax.all_gather(shift_ffn, "dp", axis=0, tiled=True),
        )
        (
            full_query,
            full_key,
            full_value,
            full_out,
            full_inner,
            full_outer,
            bias_inner,
            bias_out,
            full_gain_attn,
            full_shift_attn,
            bias_outer,
            full_gain_ffn,
            full_shift_ffn,
        ) = gathered
        own_rows = bin_tokens[micro_step]
        whole_bin = lax.all_gather(own_rows, "tensor", axis=1, tiled=True).reshape(-1, model_width)
        bin_rows = whole_bin.shape[0]
        block_rows = math.gcd(bin_rows, 512)
        segment = segment_of(lengths[micro_step], bin_rows)
        query = (
            jnp.dot(whole_bin, full_query, preferred_element_type=jnp.float32) + b_query[0]
        ).astype(jnp.bfloat16)
        keys = jnp.dot(whole_bin, full_key, preferred_element_type=jnp.float32).astype(jnp.bfloat16)
        values = (
            jnp.dot(whole_bin, full_value, preferred_element_type=jnp.float32) + b_value[0]
        ).astype(jnp.bfloat16)
        query_heads = query.reshape(bin_rows, local_heads, HD)
        key_heads = keys.reshape(bin_rows, local_heads, HD)
        value_heads = values.reshape(bin_rows, local_heads, HD)
        attn_heads, log_totals = attend_forward(
            query_heads, key_heads, value_heads, segment, block_rows, score_scale
        )
        attn = attn_heads.reshape(bin_rows, local_heads * HD)
        attn_partial = jnp.dot(attn, full_out, preferred_element_type=jnp.float32).reshape(
            dp_count, -1, model_width
        )
        branch = lax.psum_scatter(attn_partial, "tensor", scatter_dimension=1, tiled=True).reshape(
            -1, model_width
        )
        mid = own_rows.reshape(-1, model_width).astype(jnp.float32) + branch + bias_out
        hidden, normed_attn, spread_attn = layer_norm(mid, full_gain_attn, full_shift_attn)
        hidden_low = hidden.astype(jnp.bfloat16).reshape(dp_count, half_rows, model_width)
        hidden_whole = lax.all_gather(hidden_low, "tensor", axis=1, tiled=True).reshape(
            -1, model_width
        )
        inner = (
            jnp.dot(hidden_whole, full_inner, preferred_element_type=jnp.float32) + bias_inner[0]
        )
        gelu_value, gelu_pull = jax.vjp(partial(jax.nn.gelu, approximate=False), inner)
        gelu_low = gelu_value.astype(jnp.bfloat16)
        ffn_partial = jnp.dot(gelu_low, full_outer, preferred_element_type=jnp.float32).reshape(
            dp_count, -1, model_width
        )
        ffn = lax.psum_scatter(ffn_partial, "tensor", scatter_dimension=1, tiled=True).reshape(
            -1, model_width
        )
        top = hidden + ffn + bias_outer
        result, normed_ffn, spread_ffn = layer_norm(top, full_gain_ffn, full_shift_ffn)
        out_bins.append(result.astype(jnp.bfloat16).reshape(dp_count, half_rows, model_width))
        back_full = (
            lax.all_gather(w_query, "dp", axis=0, tiled=True),
            lax.all_gather(w_key, "dp", axis=0, tiled=True),
            lax.all_gather(w_value, "dp", axis=0, tiled=True),
            lax.all_gather(w_out, "dp", axis=1, tiled=True),
            lax.all_gather(w_inner, "dp", axis=0, tiled=True),
            lax.all_gather(w_outer, "dp", axis=1, tiled=True),
            lax.all_gather(gain_attn, "dp", axis=0, tiled=True),
            lax.all_gather(gain_ffn, "dp", axis=0, tiled=True),
        )
        (
            back_query,
            back_key,
            back_value,
            back_out,
            back_inner,
            back_outer,
            back_gain_attn,
            back_gain_ffn,
        ) = back_full
        grad_result = bin_grads[micro_step].reshape(-1, model_width).astype(jnp.float32)
        grad_top, grad_gain_ffn, grad_shift_ffn = norm_back(
            grad_result, normed_ffn, spread_ffn, back_gain_ffn
        )
        grad_ffn_low = grad_top.astype(jnp.bfloat16)
        grad_bias_outer = jnp.sum(grad_ffn_low.astype(jnp.float32), axis=0)
        grad_ffn_whole = lax.all_gather(
            grad_ffn_low.reshape(dp_count, half_rows, model_width), "tensor", axis=1, tiled=True
        ).reshape(-1, model_width)
        acc_outer = acc_outer + jnp.einsum(
            "nf,nd->fd", gelu_low, grad_ffn_whole, preferred_element_type=jnp.float32
        )
        grad_gelu = jnp.einsum(
            "nd,fd->nf", grad_ffn_whole, back_outer, preferred_element_type=jnp.float32
        )
        grad_inner_low = gelu_pull(grad_gelu)[0].astype(jnp.bfloat16)
        acc_bias_inner = acc_bias_inner + jnp.sum(grad_inner_low.astype(jnp.float32), axis=0)[None]
        acc_inner = acc_inner + jnp.einsum(
            "nd,nf->df", hidden_whole, grad_inner_low, preferred_element_type=jnp.float32
        )
        hidden_partial = jnp.einsum(
            "nf,df->nd", grad_inner_low, back_inner, preferred_element_type=jnp.float32
        ).reshape(dp_count, -1, model_width)
        grad_hidden = grad_top + lax.psum_scatter(
            hidden_partial, "tensor", scatter_dimension=1, tiled=True
        ).reshape(-1, model_width)
        grad_mid, grad_gain_attn, grad_shift_attn = norm_back(
            grad_hidden, normed_attn, spread_attn, back_gain_attn
        )
        grad_branch_low = grad_mid.astype(jnp.bfloat16)
        grad_bias_out = jnp.sum(grad_branch_low.astype(jnp.float32), axis=0)
        grad_branch_whole = lax.all_gather(
            grad_branch_low.reshape(dp_count, half_rows, model_width), "tensor", axis=1, tiled=True
        ).reshape(-1, model_width)
        acc_out = acc_out + jnp.einsum(
            "nh,nd->hd", attn, grad_branch_whole, preferred_element_type=jnp.float32
        )
        grad_attn_low = jnp.einsum(
            "nd,hd->nh", grad_branch_whole, back_out, preferred_element_type=jnp.float32
        ).astype(jnp.bfloat16)
        grad_heads = grad_attn_low.reshape(bin_rows, local_heads, HD)
        grad_query, grad_keys, grad_values = attend_backward(
            query_heads,
            key_heads,
            value_heads,
            grad_heads,
            log_totals,
            segment,
            block_rows,
            score_scale,
        )
        grad_query_low = grad_query.reshape(bin_rows, -1).astype(jnp.bfloat16)
        grad_key_low = grad_keys.reshape(bin_rows, -1).astype(jnp.bfloat16)
        grad_value_low = grad_values.reshape(bin_rows, -1).astype(jnp.bfloat16)
        acc_bias_query = acc_bias_query + jnp.sum(grad_query_low.astype(jnp.float32), axis=0)[None]
        acc_bias_value = acc_bias_value + jnp.sum(grad_value_low.astype(jnp.float32), axis=0)[None]
        acc_query = acc_query + jnp.einsum(
            "nd,nh->dh", whole_bin, grad_query_low, preferred_element_type=jnp.float32
        )
        acc_key = acc_key + jnp.einsum(
            "nd,nh->dh", whole_bin, grad_key_low, preferred_element_type=jnp.float32
        )
        acc_value = acc_value + jnp.einsum(
            "nd,nh->dh", whole_bin, grad_value_low, preferred_element_type=jnp.float32
        )
        input_partial = (
            jnp.einsum("nh,dh->nd", grad_query_low, back_query, preferred_element_type=jnp.float32)
            + jnp.einsum("nh,dh->nd", grad_key_low, back_key, preferred_element_type=jnp.float32)
            + jnp.einsum(
                "nh,dh->nd", grad_value_low, back_value, preferred_element_type=jnp.float32
            )
        )
        grad_input = grad_mid + lax.psum_scatter(
            input_partial.reshape(dp_count, -1, model_width).astype(jnp.bfloat16),
            "tensor",
            scatter_dimension=1,
            tiled=True,
        ).astype(jnp.float32).reshape(-1, model_width)
        grad_bins.append(grad_input.astype(jnp.bfloat16).reshape(dp_count, half_rows, model_width))
        acc_vectors = acc_vectors + jnp.stack(
            [
                grad_bias_out,
                grad_gain_attn,
                grad_shift_attn,
                grad_bias_outer,
                grad_gain_ffn,
                grad_shift_ffn,
            ]
        )
    out_stack = jnp.stack(out_bins)
    grad_stack = jnp.stack(grad_bins)
    send_out = jnp.take_along_axis(out_stack, arrived_place[:, :, None, None], axis=1)
    send_grad = jnp.take_along_axis(grad_stack, arrived_place[:, :, None, None], axis=1)
    back_out_rows, back_grad_rows = (
        lax.all_to_all(send_out, "dp", split_axis=1, concat_axis=1, tiled=True),
        lax.all_to_all(send_grad, "dp", split_axis=1, concat_axis=1, tiled=True),
    )
    layer_out = jnp.take_along_axis(back_out_rows, dest_dev[:, :, None, None], axis=1).reshape(
        tokens.shape
    )
    grad_tokens = jnp.take_along_axis(back_grad_rows, dest_dev[:, :, None, None], axis=1).reshape(
        tokens.shape
    )
    sum_query, sum_key, sum_value, sum_out, sum_inner, sum_outer, sum_bias_inner = (
        lax.psum_scatter(acc_query, "dp", scatter_dimension=0, tiled=True),
        lax.psum_scatter(acc_key, "dp", scatter_dimension=0, tiled=True),
        lax.psum_scatter(acc_value, "dp", scatter_dimension=0, tiled=True),
        lax.psum_scatter(acc_out, "dp", scatter_dimension=1, tiled=True),
        lax.psum_scatter(acc_inner, "dp", scatter_dimension=0, tiled=True),
        lax.psum_scatter(acc_outer, "dp", scatter_dimension=1, tiled=True),
        lax.psum_scatter(acc_bias_inner, "dp", scatter_dimension=1, tiled=True),
    )
    half_width = w_query.shape[1]
    tensor_pos = lax.axis_index("tensor")
    bias_pair = lax.dynamic_update_slice(
        jnp.zeros((2, model_width), jnp.float32),
        jnp.concatenate([acc_bias_query, acc_bias_value], axis=0),
        (jnp.int32(0), tensor_pos * half_width),
    )
    vectors, bias_total = lax.psum((acc_vectors, bias_pair), ("dp", "tensor"))
    own_width = model_width // dp_count
    vec_own = lax.dynamic_slice_in_dim(vectors, lax.axis_index("dp") * own_width, own_width, 1)
    bias_own = lax.dynamic_slice_in_dim(bias_total, tensor_pos * half_width, half_width, 1)
    return (
        layer_out,
        grad_tokens,
        sum_query,
        sum_key,
        sum_value,
        bias_own[0:1],
        bias_own[1:2],
        sum_out,
        vec_own[0],
        vec_own[1],
        vec_own[2],
        sum_inner,
        sum_bias_inner,
        sum_outer,
        vec_own[3],
        vec_own[4],
        vec_own[5],
    )


def solution(mesh):
    placed = (
        P("dp", "tensor", None),
        P("dp", "tensor", None),
        P("dp"),
        P("dp", None),
        P("dp", "tensor"),
        P("dp", "tensor"),
        P("dp", "tensor"),
        P("tensor", None),
        P("tensor", None),
        P("tensor", "dp"),
        P("dp"),
        P("dp"),
        P("dp"),
        P("dp", "tensor"),
        P("tensor", "dp"),
        P("tensor", "dp"),
        P("dp"),
        P("dp"),
        P("dp"),
    )
    dp_count = mesh.shape["dp"]

    def body(*args):
        tokens, w_query, b_inner = args[0], args[4], args[14]
        fits = (
            dp_count & (dp_count - 1) == 0
            and w_query.shape[0] % 16 == 0
            and tokens.shape[1] % 8 == 0
            and mesh.shape["tensor"] == 2
        )
        return (shards_fast if fits else shards)(*args)

    return jax.shard_map(
        body,
        mesh=mesh,
        in_specs=placed,
        out_specs=(
            P("dp", "tensor", None),
            P("dp", "tensor", None),
            P("dp", "tensor"),
            P("dp", "tensor"),
            P("dp", "tensor"),
            P("tensor", None),
            P("tensor", None),
            P("tensor", "dp"),
            P("dp"),
            P("dp"),
            P("dp"),
            P("dp", "tensor"),
            P("tensor", "dp"),
            P("tensor", "dp"),
            P("dp"),
            P("dp"),
            P("dp"),
        ),
        check_vma=False,
    )
```

```python
from functools import partial
import math

import jax
import jax.numpy as jnp
from jax import lax
from jax.experimental import pallas as pl
from jax.experimental.pallas import tpu as pltpu
from jax.sharding import PartitionSpec as P

HEADS = 12
HD = 64


EPS_NORM = 1e-12


def layer_norm(residual, norm_gain, norm_shift):
    centre = residual - jnp.mean(residual, axis=-1, keepdims=True)
    spread = lax.rsqrt(jnp.mean(centre * centre, axis=-1, keepdims=True) + EPS_NORM)
    normed = centre * spread
    return (normed * norm_gain + norm_shift, normed, spread)


def norm_back(grad_out, normed, spread, norm_gain):
    scaled = grad_out * norm_gain
    inner_term = (
        scaled
        - jnp.mean(scaled, axis=-1, keepdims=True)
        - normed * jnp.mean(scaled * normed, axis=-1, keepdims=True)
    )
    return (inner_term * spread, jnp.sum(grad_out * normed, axis=0), jnp.sum(grad_out, axis=0))


def segment_of(seq_lengths, count_rows):
    seq_ends = jnp.cumsum(seq_lengths)
    positions = jnp.arange(count_rows, dtype=jnp.int32)
    return jnp.sum((positions[:, None] >= seq_ends[None, :-1]).astype(jnp.int32), axis=1)


def masked_scores(query_block, key_heads, segment, first_row, block_rows, score_scale):
    scores = (
        jnp.einsum("qhd,khd->hqk", query_block, key_heads, preferred_element_type=jnp.float32)
        * score_scale
    )
    allowed = segment[first_row : first_row + block_rows, None] == segment[None, :]
    return jnp.where(allowed[None], scores, -1e30)


def attend_forward(query_heads, key_heads, value_heads, segment, block_rows, score_scale):
    scores = masked_scores(query_heads, key_heads, segment, 0, block_rows, score_scale)
    row_peak = jnp.max(scores, axis=-1, keepdims=True)
    exp_scores = jnp.exp(scores - row_peak)
    row_total = jnp.sum(exp_scores, axis=-1, keepdims=True)
    prob_low = (exp_scores / row_total).astype(jnp.bfloat16)
    out_block = jnp.einsum(
        "hqk,khd->qhd", prob_low, value_heads, preferred_element_type=jnp.float32
    )
    out_rows = out_block.astype(jnp.bfloat16)
    lse_rows = row_peak + jnp.log(row_total)
    return (out_rows, lse_rows)


def attend_backward(
    query_heads, key_heads, value_heads, grad_heads, log_totals, segment, block_rows, score_scale
):
    scores = masked_scores(query_heads, key_heads, segment, 0, block_rows, score_scale)
    probs_full = jnp.exp(scores - log_totals)
    prob_low = probs_full.astype(jnp.bfloat16)
    grad_values = jnp.einsum(
        "hqk,qhd->khd", prob_low, grad_heads, preferred_element_type=jnp.float32
    )
    grad_probs = jnp.einsum(
        "qhd,khd->hqk", grad_heads, value_heads, preferred_element_type=jnp.float32
    )
    row_inner = jnp.sum(probs_full * grad_probs, axis=-1, keepdims=True)
    grad_scores = (probs_full * (grad_probs - row_inner)).astype(jnp.bfloat16)
    grad_query_rows = (
        jnp.einsum("hqk,khd->qhd", grad_scores, key_heads, preferred_element_type=jnp.float32)
        * score_scale
    )
    grad_keys = (
        jnp.einsum("hqk,qhd->khd", grad_scores, query_heads, preferred_element_type=jnp.float32)
        * score_scale
    )
    return (grad_query_rows, grad_keys, grad_values)


MESH = pl.DeviceIdType.MESH
LANES = 128
NT = (((1,), (1,)), ((), ()))
NN = (((1,), (0,)), ((), ()))
F32 = jnp.float32
LOW = jnp.bfloat16
FAR_FIRST, NEAR_FIRST = range(2)
X, DY, OUT, GX = range(4)
(
    GATHER,
    REDUCE,
    NEAR,
    FAR,
    VECTORS,
    FIND_SLOTS,
    SEND_PIECES,
    ARRANGE_TOKENS,
    ARRANGE_COTANGENT,
    WHOLE_VECTORS,
    MASK_BINS,
    TAKE_TOKENS,
    PROJECT_HEADS,
    ATTEND_THIRD,
    ATTEND_BACK_THIRD,
    PROJECT_OUT,
    NORM_AFTER_ATTENTION,
    WIDEN_TOKENS,
    NARROW_TOKENS,
    NORM_AFTER_FFN,
    NORM_FFN_BACKWARD,
    GRAD_OUTER,
    FFN_BACKWARD,
    GRAD_INNER,
    GRAD_OUT,
    HEADS_BACKWARD,
    INPUT_AWAY,
    GRAD_HEADS,
    INPUT_BACKWARD,
    PAIR_VECTORS,
    TAKE_OUTPUT,
    TAKE_INPUT_GRAD,
) = range(32)

GATHERS = (
    (FAR_FIRST, 0, 3),
    (FAR_FIRST, 3, 6),
    (FAR_FIRST, 9, 7),
    (FAR_FIRST, 16, 8),
    (FAR_FIRST, 24, 4),
    (NEAR_FIRST, 28, 4),
    (NEAR_FIRST, 32, 4),
)
SCATTERS = (
    (FAR_FIRST, 24, 4),
    (NEAR_FIRST, 28, 8),
    (FAR_FIRST, 12, 12),
    (FAR_FIRST, 9, 3),
    (FAR_FIRST, 0, 5),
    (FAR_FIRST, 5, 4),
)
SCHEDULE = (
    (GATHER, 1),
    (GATHER, 5),
    (GATHER, 2),
    (SEND_PIECES,),
    (GATHER, 6),
    (GATHER, 0),
    (FIND_SLOTS,),
    (ARRANGE_TOKENS,),
    (GATHER, 5),
    (NEAR, X),
    (ARRANGE_COTANGENT,),
    (GATHER, 1),
    (GATHER, 0),
    (GATHER, 6),
    (GATHER, 2),
    (FAR, X),
    (GATHER, 3),
    (GATHER, 4),
    (GATHER, 1),
    (GATHER, 0),
    (WHOLE_VECTORS,),
    (GATHER, 0),
    (GATHER, 2),
    (GATHER, 3),
    (GATHER, 4),
    (GATHER, 5),
    (GATHER, 1),
    (MASK_BINS,),
    (GATHER, 6),
    (GATHER, 2),
    (TAKE_TOKENS,),
    (GATHER, 0),
    (GATHER, 5),
    (GATHER, 3),
    (GATHER, 1),
    (PROJECT_HEADS,),
    (NEAR, DY),
    (ATTEND_THIRD, 0),
    (GATHER, 2),
    (GATHER, 6),
    (ATTEND_THIRD, 1),
    (GATHER, 4),
    (ATTEND_THIRD, 2),
    (PROJECT_OUT,),
    (GATHER, 3),
    (GATHER, 4),
    (GATHER, 6),
    (FAR, DY),
    (NORM_AFTER_ATTENTION,),
    (GATHER, 3),
    (GATHER, 5),
    (WIDEN_TOKENS,),
    (GATHER, 4),
    (NARROW_TOKENS,),
    (NORM_AFTER_FFN,),
    (NEAR, OUT),
    (FAR, OUT),
    (NORM_FFN_BACKWARD,),
    (GRAD_OUTER, 0),
    (GRAD_OUTER, 1),
    (REDUCE, 0),
    (REDUCE, 1),
    (FFN_BACKWARD,),
    (GRAD_INNER,),
    (REDUCE, 2),
    (TAKE_OUTPUT,),
    (GRAD_OUT,),
    (HEADS_BACKWARD,),
    (ATTEND_BACK_THIRD, 0),
    (ATTEND_BACK_THIRD, 1),
    (ATTEND_BACK_THIRD, 2),
    (REDUCE, 0),
    (REDUCE, 1),
    (INPUT_AWAY,),
    (REDUCE, 2),
    (REDUCE, 3),
    (GRAD_HEADS,),
    (REDUCE, 5),
    (REDUCE, 4),
    (REDUCE, 0),
    (REDUCE, 2),
    (REDUCE, 0),
    (REDUCE, 5),
    (INPUT_BACKWARD,),
    (REDUCE, 2),
    (REDUCE, 1),
    (PAIR_VECTORS,),
    (NEAR, GX),
    (REDUCE, 5),
    (REDUCE, 3),
    (REDUCE, 4),
    (VECTORS,),
    (FAR, GX),
    (VECTORS,),
    (REDUCE, 4),
    (VECTORS,),
    (REDUCE, 2),
    (REDUCE, 3),
    (REDUCE, 5),
    (REDUCE, 1),
    (VECTORS,),
    (REDUCE, 0),
    (REDUCE, 4),
    (REDUCE, 3),
    (TAKE_INPUT_GRAD,),
    (REDUCE, 1),
    (REDUCE, 5),
    (VECTORS,),
    (REDUCE, 4),
    (REDUCE, 3),
)

VMEM_BYTES = 63 << 20


def flip(place, bit):
    return place + bit * (1 - 2 * ((place // bit) % 2))


def bit_of(place, bit):
    return (place // bit) % 2


def bits_of(count):
    return tuple(1 << i for i in range(count.bit_length() - 1))[::-1]


def orders_of(count):
    bits = bits_of(count)
    return (bits, bits[:-2] + bits[-2:][::-1])


def mm(left, right, dims=NN):
    return lax.dot_general(left, right, dims, preferred_element_type=F32)


class Gather:
    def __init__(self, dp_count, place, half, order, ref, start, size, send_sem, recv_sem):
        self.place, self.half, self.order = place, half, order
        self.bits = bits_of(dp_count)
        self.ref, self.cols = ref, pl.ds(start, size)
        self.send_sem, self.recv_sem = send_sem, recv_sem

    def copy(self, stage):
        done = self.order[:stage]
        index = tuple(
            slice(None) if bit in done else bit_of(self.place, bit) for bit in self.bits
        ) + (slice(None), self.cols)
        return pltpu.make_async_remote_copy(
            src_ref=self.ref.at[index],
            dst_ref=self.ref.at[index],
            send_sem=self.send_sem.at[stage],
            recv_sem=self.recv_sem.at[stage],
            device_id=(flip(self.place, self.order[stage]), self.half),
            device_id_type=MESH,
        )


class Scatter:
    def __init__(self, dp_count, place, half, order, ref, start, size, landing, send_sem, recv_sem):
        self.place, self.half = place, half
        self.order = order
        self.bits = bits_of(dp_count)
        self.ref, self.cols = ref, pl.ds(start, size)
        self.landing = landing
        self.send_sem, self.recv_sem = send_sem, recv_sem

    def view(self, stage, chosen):
        left = [bit for bit in self.bits if bit not in self.order[:stage]]
        own = bit_of(self.place, self.order[stage])
        index = tuple(
            (own if chosen == "own" else 1 - own) if bit == self.order[stage] else slice(None)
            for bit in left
        )
        if stage == 0:
            return self.ref.at[index + (slice(None), self.cols)]
        return self.landing[stage - 1].at[index]

    def copy(self, stage):
        return pltpu.make_async_remote_copy(
            src_ref=self.view(stage, "other"),
            dst_ref=self.landing[stage],
            send_sem=self.send_sem.at[stage],
            recv_sem=self.recv_sem.at[stage],
            device_id=(flip(self.place, self.order[stage]), self.half),
            device_id_type=MESH,
        )

    def add(self, stage):
        kept = self.view(stage, "own")
        land = self.landing[stage]
        lead = land.shape[:-2]
        count = math.prod(lead)

        def one(i, carry):
            index, rest = [], i
            for extent in lead[::-1]:
                index.append(lax.rem(rest, extent))
                rest = rest // extent
            index = tuple(index[::-1])
            land[index] = (kept[index].astype(F32) + land[index].astype(F32)).astype(land.dtype)
            return carry

        if count == 1:
            one(0, 0)
        else:
            lax.fori_loop(0, count, one, 0)

    def finish(self, stage, outs):
        kept = self.view(stage, "own")
        sums, refs, copy_out = outs
        sums[:, self.cols] = kept[...].astype(F32) + self.landing[stage][...].astype(F32)
        first, begin = self.cols.start, 0
        for ref in refs:
            low = max(first, begin)
            high = min(first + self.cols.size, begin + ref.shape[1])
            if low < high:
                copy_out(sums.at[:, pl.ds(low, high - low)], ref.at[:, pl.ds(low - begin, high - low)])
            begin += ref.shape[1]


def layer(sizes, gather_plan, scatter_plan, *refs):
    dp_count, micro, rows, width, heads_wide, ff = sizes
    (
        tokens_ref,
        cot_ref,
        route_ref,
        lengths_ref,
        wq_ref,
        wk_ref,
        wv_ref,
        wo_ref,
        wi_ref,
        wu_ref,
        *small_refs,
        bq_ref,
        bv_ref,
        bi_ref,
        layer_out_hbm,
        grad_tokens_hbm,
        gq_hbm,
        gk_hbm,
        gv_hbm,
        go_hbm,
        gi_hbm,
        gu_hbm,
    ) = refs[:28]
    vec_out_ref = refs[28]
    (
        inverse_ref,
        target_ref,
        tokens_in,
        cot_in,
        layer_out_ref,
        grad_tokens_ref,
        sums,
        full,
        grads,
        x_send,
        dy_send,
        x_land,
        dy_land,
        out_send,
        gx_send,
        out_land,
        gx_land,
        xs,
        hs,
        gs,
        gb,
        flipped,
        xs_flipped,
        hs_flipped,
        qkv,
        dqkv,
        attn,
        gattn,
        probs,
        bias,
        gelu_low,
        dgelu,
        ginner,
        normed,
        spread,
        spread_ffn,
        grad_keep,
        own_part,
        part_send,
        part_land,
        last_send,
        last_land,
        piece,
        pieces,
        vec,
        vec_pair,
        vecg_buf,
        vecg_land,
        vec_acc,
        *rest,
    ) = refs[29:]
    stages = dp_count.bit_length() - 1
    groups = max(group for group, _, _, _ in scatter_plan) + 1
    landings = [rest[i * stages : (i + 1) * stages] for i in range(groups)]
    (
        x_sems,
        dy_sems,
        out_sems,
        gx_sems,
        gather_sends,
        gather_recvs,
        scatter_sends,
        scatter_recvs,
        vec_sems,
        vecg_sems,
        pair_sems,
        in_sems,
        out_copy_sems,
    ) = rest[groups * stages :]
    place, half = lax.axis_index("dp"), lax.axis_index("tensor")
    other = 1 - half
    bits = bits_of(dp_count)
    orders = orders_of(dp_count)
    bin_half = dp_count * rows
    tall = micro * bin_half
    blocks = micro * dp_count
    own_width = width // dp_count
    block_len = 2 * rows
    pairs = heads_wide // LANES
    key_col, value_col, out_col = heads_wide, 2 * heads_wide, 3 * heads_wide
    inner_col, outer_col = 4 * heads_wide, 4 * heads_wide + ff
    tile = heads_wide

    def weights(start, size):
        return full[(slice(None),) * stages + (slice(None), pl.ds(start, size))].reshape(width, size)

    def pair_copy(src, dst, which):
        return pltpu.make_async_remote_copy(
            src_ref=src,
            dst_ref=dst,
            send_sem=pair_sems.at[0, which],
            recv_sem=pair_sems.at[1, which],
            device_id=(place, other),
            device_id_type=MESH,
        )

    group = dp_count // 2
    base, within_group = place - lax.rem(place, group), lax.rem(place, group)
    far_base = lax.rem(base + group, dp_count)

    def message(step, send_ref, recv_ref, sems, near):
        peer = (base if near else far_base) + lax.rem(within_group + step, group)
        return pltpu.make_async_remote_copy(
            src_ref=send_ref.at[peer],
            dst_ref=recv_ref.at[place],
            send_sem=sems.at[0],
            recv_sem=sems.at[1],
            device_id=(peer, half),
            device_id_type=MESH,
        )

    def push(send_ref, recv_ref, sems, near):
        def one(step, carry):
            message(step, send_ref, recv_ref, sems, near).start()
            return carry

        lax.fori_loop(1 if near else 0, group, one, 0)

    def settle(send_ref, recv_ref, sems):
        recv_ref[place] = send_ref[place]
        whole = pl.ds(0, dp_count - 1)
        every = pltpu.make_async_remote_copy(
            src_ref=send_ref.at[whole],
            dst_ref=recv_ref.at[whole],
            send_sem=sems.at[0],
            recv_sem=sems.at[1],
            device_id=(place, other),
            device_id_type=MESH,
        )
        every.wait_recv()
        every.wait_send()

    def arrange(src_ref, dst_ref):
        def one(i, carry):
            m, peer = i // dp_count, lax.rem(i, dp_count)
            dst_ref[peer, m] = src_ref[m * dp_count + inverse_ref[m, peer]]
            return carry

        lax.fori_loop(0, blocks, one, 0)

    barrier = pltpu.get_barrier_semaphore()

    def hello(step, carry):
        peer = lax.rem(place + step, dp_count)
        pl.semaphore_signal(barrier, inc=1, device_id=(peer, half), device_id_type=MESH)
        return carry

    lax.fori_loop(1, dp_count, hello, 0)
    pl.semaphore_signal(barrier, inc=1, device_id=(place, other), device_id_type=MESH)

    own = tuple(bit_of(place, bit) for bit in bits)
    fetches = [
        pltpu.make_async_copy(src, dst, in_sems.at[i])
        for i, (src, dst) in enumerate(
            [
                (ref, full.at[own + (slice(None), pl.ds(start, size))])
                for ref, start, size in (
                    (wq_ref, 0, heads_wide),
                    (wk_ref, key_col, heads_wide),
                    (wv_ref, value_col, heads_wide),
                    (wo_ref, out_col, heads_wide),
                    (wi_ref, inner_col, ff),
                    (wu_ref, outer_col, ff),
                )
            ]
            + [(tokens_ref, tokens_in), (cot_ref, cot_in)]
        )
    ]
    for fetch in fetches:
        fetch.start()
    leaving = []

    def copy_out(src, dst):
        copy = pltpu.make_async_copy(src, dst, out_copy_sems.at[len(leaving)])
        copy.start()
        leaving.append(copy)

    outs = (sums, (gq_hbm, gk_hbm, gv_hbm, go_hbm, gi_hbm, gu_hbm), copy_out)

    piece[...] = jnp.zeros((16, LANES), F32)
    for i, ref in enumerate(small_refs):
        piece[i : i + 1, 0:own_width] = ref[...].astype(F32).reshape(1, own_width)
    piece[8:16, 0 : bi_ref.shape[1]] = jnp.broadcast_to(bi_ref[...].astype(F32), (8, bi_ref.shape[1]))
    route = piece[6:7, 0:own_width]
    piece[7:8, 0:own_width] = route - dp_count * jnp.floor((route + 0.5) * (1.0 / dp_count))
    piece[6:7, 0:own_width] = jnp.floor((route + 0.5) * (1.0 / blocks))
    def find_target(i, carry):
        target_ref[i] = lax.div(route_ref[i], blocks)
        return carry


    def invert(i, carry):
        m, peer = lax.div(i, dp_count), lax.rem(i, dp_count)
        slot = jnp.int32(0)
        for k in range(dp_count):
            slot = jnp.where(target_ref[m * dp_count + k] == peer, k, slot)
        inverse_ref[m, peer] = slot
        return carry

    for fetch in fetches[:6]:
        fetch.wait()
    pl.semaphore_wait(barrier, dp_count)

    gathers = [
        Gather(
            dp_count,
            place,
            half,
            order,
            full,
            start,
            size,
            gather_sends,
            gather_recvs.at[i],
        )
        for i, (_, order, start, size) in enumerate(gather_plan)
    ]
    gone = {}

    def extent(plan, wanted):
        own_plan = [(start, start + size) for group, _, start, size in plan if group == wanted]
        start, stop = min(own_plan)[0], max(own_plan)[1]
        return pl.ds(start, stop - start)

    def shards_copy(ref, dropped, cols, send_sem, recv_sem):
        view = ref.at[(0,) * dropped + (slice(None),) * (stages - dropped + 1) + (cols,)]
        return pltpu.make_async_remote_copy(
            src_ref=view,
            dst_ref=view,
            send_sem=send_sem,
            recv_sem=recv_sem,
            device_id=(place, other),
            device_id_type=MESH,
        )

    def advance(*groups):
        for wanted in groups:
            stage = gone.get(wanted, 0)
            if stage > stages:
                continue
            gone[wanted] = stage + 1
            for (member, _, _, _), gather in zip(gather_plan, gathers):
                if member == wanted and stage > 0:
                    gather.copy(stage - 1).wait_recv()
                if member == wanted and stage < stages:
                    gather.copy(stage).start()

    def swing(buf, land, sems, stage, last_ref):
        copy = pltpu.make_async_remote_copy(
            src_ref=buf.at[stage],
            dst_ref=land.at[stage],
            send_sem=sems.at[0, stage],
            recv_sem=sems.at[1, stage],
            device_id=(flip(place, bits[stage]), half),
            device_id_type=MESH,
        )

        def fold():
            copy.wait()
            total = buf[stage] + land[stage]
            if stage < stages - 1:
                buf[stage + 1] = total
            else:
                last_ref[...] = total

        return copy.start, fold

    def push_piece(step, carry):
        peer = lax.rem(place + step, dp_count)
        pltpu.make_async_remote_copy(
            src_ref=piece,
            dst_ref=pieces.at[place],
            send_sem=vec_sems.at[0],
            recv_sem=vec_sems.at[1],
            device_id=(peer, half),
            device_id_type=MESH,
        ).start()
        return carry

    bits_shape = (2,) * stages
    scatters = [
        Scatter(
            dp_count,
            place,
            half,
            order,
            grads,
            start,
            size,
            [
                land.at[
                    (slice(None),) * (stages - stage)
                    + (pl.ds(start - extent(scatter_plan, group).start, size),)
                ]
                for stage, land in enumerate(landings[group])
            ],
            scatter_sends,
            scatter_recvs.at[i],
        )
        for i, (group, order, start, size) in enumerate(scatter_plan)
    ]
    sent = {}

    def reduce(*wanted_groups):
        for wanted in wanted_groups:
            stage = sent.get(wanted, 0)
            if stage > stages:
                continue
            sent[wanted] = stage + 1
            for (group, _, _, _), scatter in zip(scatter_plan, scatters):
                if group == wanted:
                    if stage > 0:
                        scatter.copy(stage - 1).wait_recv()
                    if 0 < stage < stages:
                        scatter.add(stage - 1)
                    elif stage == stages:
                        scatter.finish(stage - 1, outs)
                    if stage < stages:
                        scatter.copy(stage).start()

    def grad_columns(left_t, right_ref, start, columns, grads_start, tile=tile):
        for i in range(columns // tile):
            piece = mm(left_t, right_ref[:, :, start + i * tile : start + (i + 1) * tile].reshape(2 * tall, tile))
            grads[(slice(None),) * (stages + 1) + (pl.ds(grads_start + i * tile, tile),)] = piece.astype(
                LOW
            ).reshape(bits_shape + (own_width, tile))

    low_lane = lax.broadcasted_iota(jnp.int32, (2 * bin_half, LANES), 1) < HD
    nothing = jnp.zeros((2 * bin_half, LANES), LOW)

    def bin_of(ref, m, start):
        at = pl.ds(pl.multiple_of(m * bin_half, bin_half), bin_half)
        return jnp.concatenate([ref[0, at, pl.ds(start, LANES)], ref[1, at, pl.ds(start, LANES)]], axis=0)

    def put_bin(ref, m, start, value):
        at = pl.ds(pl.multiple_of(m * bin_half, bin_half), bin_half)
        ref[0, at, pl.ds(start, LANES)] = value[:bin_half].astype(ref.dtype)
        ref[1, at, pl.ds(start, LANES)] = value[bin_half:].astype(ref.dtype)

    def split_heads(value):
        return (jnp.where(low_lane, value, nothing), jnp.where(low_lane, nothing, value))

    def attend(m):
        for j in range(pairs):
            query = bin_of(qkv, m, j * LANES)
            key = bin_of(qkv, m, key_col + j * LANES)
            value = bin_of(qkv, m, value_col + j * LANES)
            total = None
            for e, (query_e, value_e) in enumerate(zip(split_heads(query), split_heads(value))):
                score = mm(query_e, key, NT) + bias[m]
                power = jnp.exp(score - jnp.max(score, axis=1, keepdims=True))
                prob = power * (1.0 / jnp.sum(power, axis=1, keepdims=True))
                probs[m, 2 * j + e] = prob.astype(probs.dtype)
                part = mm(prob.astype(LOW), value_e)
                total = part if total is None else total + part
            put_bin(attn, m, j * LANES, total)

    def two_halves(left_ref, columns, start, send_ref, which, land_ref):
        away = mm(left_ref[other], weights(start, columns), NT)
        send_ref[...] = away.astype(send_ref.dtype)
        copy = pair_copy(send_ref, land_ref, which)
        copy.start()
        own_part[...] = mm(left_ref[half], weights(start, columns), NT)
        return copy

    chunk = 4 * rows
    per_bin = bin_half // chunk
    chunks = tall // chunk
    ones = jnp.ones((8, tall), LOW)

    def mean_of(v):
        return jnp.sum(v, axis=1, keepdims=True) * (1.0 / width)

    def fold_rows(v):
        return jnp.sum(v.reshape(chunk // 8, 8, width), axis=0)

    def hand_back(land_ref, result_ref, hbm_ref):
        def one(i, carry):
            result_ref[i] = land_ref[target_ref[i], i // dp_count]
            return carry

        lax.fori_loop(0, blocks, one, 0)
        copy_out(result_ref, hbm_ref)

    def find_slots():
        lax.fori_loop(0, blocks, find_target, 0)
        lax.fori_loop(0, blocks, invert, 0)

    def send_pieces():
        lax.fori_loop(1, dp_count, push_piece, 0)

    def arrange_tokens():
        fetches[6].wait()
        arrange(tokens_in, x_send)

    def arrange_cotangent():
        fetches[7].wait()
        arrange(cot_in, dy_send)

    def whole_vectors():
        pieces[place] = piece[...]
        every_piece = pltpu.make_async_remote_copy(
            src_ref=pieces.at[pl.ds(0, dp_count - 1)],
            dst_ref=pieces.at[pl.ds(0, dp_count - 1)],
            send_sem=vec_sems.at[0],
            recv_sem=vec_sems.at[1],
            device_id=(place, other),
            device_id_type=MESH,
        )
        every_piece.wait_recv()
        every_piece.wait_send()

        def lay(source, total):
            block = pieces[source]

            def laid(block, size, extent):
                target = lax.broadcasted_iota(jnp.int32, (LANES, extent), 1)
                at = lax.broadcasted_iota(jnp.int32, (LANES, extent), 0)
                hit = (target == at + source * size) & (at < size)
                return mm(block.astype(LOW), hit.astype(F32).astype(LOW))

            return (
                total[0] + laid(block[0:8], own_width, width),
                total[1] + laid(block[8:16], bi_ref.shape[1], ff),
            )

        short, long = lax.fori_loop(
            0, dp_count, lay, (jnp.zeros((8, width), F32), jnp.zeros((8, ff), F32))
        )
        vec[0:8, :] = short
        for i in range(ff // width):
            vec[8 + i : 9 + i, :] = long[0:1, i * width : (i + 1) * width]

    def mask_bins():
        placed = jnp.where(vec[6:7, :] == place.astype(F32), vec[7:8, :], 0.0)
        placed_rows = jnp.broadcast_to(placed, (8, blocks * dp_count))

        def mask_bin(m, carry):
            shape = (2 * bin_half, blocks * dp_count)
            row = lax.broadcasted_iota(jnp.int32, shape, 0)
            lane = lax.broadcasted_iota(jnp.int32, shape, 1)
            source = lax.rem(row, bin_half) // rows
            chosen = (lane // dp_count) == source * micro + m
            tall_place = jnp.sum(jnp.where(chosen, placed, 0.0), axis=1, keepdims=True)
            wide_place = mm(placed_rows, chosen.astype(F32), NT)[0:1, :]
            ends, end = [], 0
            for i in range(lengths_ref.shape[1] - 1):
                end = end + lengths_ref[m, i]
                ends.append(end.astype(F32))

            def sequence(at, index):
                within = (lax.rem(index, rows) + (index // bin_half) * rows).astype(F32)
                position = at * block_len + within
                return sum((position >= end).astype(F32) for end in ends)

            down = sequence(
                tall_place, lax.broadcasted_iota(jnp.int32, (2 * bin_half, 1), 0)
            )
            across = sequence(
                wide_place, lax.broadcasted_iota(jnp.int32, (1, 2 * bin_half), 1)
            )
            bias[m] = jnp.where(down == across, 0.0, -1e30)
            return carry

        lax.fori_loop(0, micro, mask_bin, 0)

    def take_tokens():
        settle(x_send, x_land, x_sems)

        def order_rows(m, carry):
            block = x_land[:, m].astype(F32).reshape(bin_half, width)
            xs[half, pl.ds(pl.multiple_of(m * bin_half, bin_half), bin_half), :] = block.astype(LOW)
            return carry

        lax.fori_loop(0, micro, order_rows, 0)
        swap_x = pair_copy(xs.at[half], xs.at[half], 0)
        swap_x.start()
        swap_x.wait()

    def project_heads():
        def project(i, carry):
            h = lax.rem(half + i, 2)
            own_rows = xs[h]
            qkv[h, :, pl.ds(0, heads_wide)] = (
                (mm(own_rows, weights(0, heads_wide)) + bq_ref[...].astype(F32)).astype(LOW)
                * LOW(HD ** (-0.5))
            )
            qkv[h, :, pl.ds(key_col, heads_wide)] = mm(own_rows, weights(key_col, heads_wide)).astype(LOW)
            qkv[h, :, pl.ds(value_col, heads_wide)] = (
                mm(own_rows, weights(value_col, heads_wide)) + bv_ref[...].astype(F32)
            ).astype(LOW)
            return carry

        lax.fori_loop(0, 2, project, 0)

    def attend_back(m):
        for j in range(pairs):
            query = bin_of(qkv, m, j * LANES)
            key = bin_of(qkv, m, key_col + j * LANES)
            value = bin_of(qkv, m, value_col + j * LANES)
            grad = bin_of(gattn, m, j * LANES)
            keys, queries, upstream = split_heads(key), split_heads(query), split_heads(grad)
            d_query = d_key = d_value = None
            for e in range(2):
                prob = probs[m, 2 * j + e].astype(F32)
                d_prob = mm(upstream[e], value, NT)
                inner = jnp.sum(prob * d_prob, axis=1, keepdims=True)
                d_score = (prob * (d_prob - inner)).astype(LOW)
                part_q = mm(d_score, keys[e])
                part_k = mm(d_score.T, queries[e])
                part_v = mm(prob.astype(LOW).T, upstream[e])
                d_query = part_q if d_query is None else d_query + part_q
                d_key = part_k if d_key is None else d_key + part_k
                d_value = part_v if d_value is None else d_value + part_v
            put_bin(dqkv, m, j * LANES, d_query * (HD ** (-0.5)))
            put_bin(dqkv, m, key_col + j * LANES, d_key)
            put_bin(dqkv, m, value_col + j * LANES, d_value)

    def attend_third(third):
        for m in range(third * micro // 3, (third + 1) * micro // 3):
            attend(m)

    def attend_back_third(third):
        for m in range(third * micro // 3, (third + 1) * micro // 3):
            attend_back(m)

    def project_out():
        two_halves(attn, heads_wide, out_col, part_send, 1, part_land.at[0]).wait()

    pending = {}

    def norm_after_attention():
        def norm_attn(i, carry):
            at = pl.ds(pl.multiple_of(i * chunk, chunk), chunk)
            mid = xs[half, at, :].astype(F32) + (own_part[at, :] + part_land[0, at, :].astype(F32)) + vec[0:1, :]
            centre = mid - mean_of(mid)
            inverse_s = lax.rsqrt(mean_of(centre * centre) + EPS_NORM)
            unit = centre * inverse_s
            normed[at, :] = unit
            spread[at, :] = jnp.broadcast_to(inverse_s, (chunk, LANES))
            hs[half, at, :] = (unit * vec[1:2, :] + vec[2:3, :]).astype(LOW)
            return carry

        lax.fori_loop(0, chunks, norm_attn, 0)
        pending[2] = pair_copy(hs.at[half], hs.at[half], 2)
        pending[2].start()

    def widen_tokens():
        def widen(h):
            for i in range(ff // tile):
                start = i * tile
                row = 8 + start // width
                inner = mm(hs[h], weights(inner_col + start, tile)) + vec[
                    row : row + 1, start % width : start % width + tile
                ]
                cdf = 0.5 * (1.0 + lax.erf(inner * (0.5**0.5)))
                density = jnp.exp(-0.5 * inner * inner) * ((2.0 * math.pi) ** -0.5)
                gelu_low[h, :, start : start + tile] = (inner * cdf).astype(LOW)
                dgelu[h, :, start : start + tile] = (cdf + inner * density).astype(dgelu.dtype)

        def widen_step(i, carry):
            @pl.when(i == 1)
            def _():
                pending[2].wait()

            widen(lax.rem(half + i, 2))
            return carry

        lax.fori_loop(0, 2, widen_step, 0)
        xs_flipped[...] = xs[...].reshape(2 * tall, width).T
        hs_flipped[...] = hs[...].reshape(2 * tall, width).T

    def narrow_tokens():
        two_halves(gelu_low, ff, outer_col, part_send, 3, part_land.at[1]).wait()

    def norm_after_ffn():
        def norm_ffn(i, carry):
            at = pl.ds(pl.multiple_of(i * chunk, chunk), chunk)
            m, quarter = i // per_bin, lax.rem(i, per_bin)
            sources = pl.ds(quarter * (chunk // rows), chunk // rows)
            hidden = normed[at, :] * vec[1:2, :] + vec[2:3, :]
            top = hidden + (own_part[at, :] + part_land[1, at, :].astype(F32)) + vec[3:4, :]
            centre = top - mean_of(top)
            inverse_s = lax.rsqrt(mean_of(centre * centre) + EPS_NORM)
            unit = centre * inverse_s
            own_part[at, :] = unit
            spread_ffn[at, :] = jnp.broadcast_to(inverse_s, (chunk, LANES))
            result = unit * vec[4:5, :] + vec[5:6, :]
            out_send[sources, m] = result.reshape(chunk // rows, rows, width).astype(LOW)
            return carry

        lax.fori_loop(0, chunks, norm_ffn, 0)

    def norm_ffn_backward():
        settle(dy_send, dy_land, dy_sems)
        for i in range(3):
            vec_acc[i] = jnp.zeros((8, width), F32)

        def norm_ffn_back(i, carry):
            at = pl.ds(pl.multiple_of(i * chunk, chunk), chunk)
            m, quarter = i // per_bin, lax.rem(i, per_bin)
            sources = pl.ds(quarter * (chunk // rows), chunk // rows)
            unit = own_part[at, :]
            dy = dy_land[sources, m].astype(F32).reshape(chunk, width)
            vec_acc[0] = vec_acc[0] + fold_rows(dy * unit)
            vec_acc[1] = vec_acc[1] + fold_rows(dy)
            scaled = dy * vec[4:5, :]
            grad_top = (scaled - mean_of(scaled) - unit * mean_of(scaled * unit)) * spread_ffn[at, 0:1]
            grad_keep[at, :] = grad_top
            gs[half, at, :] = grad_top.astype(LOW)
            return carry

        swaps = []
        for i, which in enumerate((4, 9)):
            lax.fori_loop(i * (chunks // 2), (i + 1) * (chunks // 2), norm_ffn_back, 0)
            piece_of = gs.at[half, pl.ds(i * (tall // 2), tall // 2)]
            swap_g = pair_copy(piece_of, piece_of, which)
            swap_g.start()
            swaps.append(swap_g)
        for swap_g in swaps:
            swap_g.wait()
        flipped[...] = gs[...].reshape(2 * tall, width).T

    middle = scatter_plan[1][2] + scatter_plan[1][3] - outer_col

    def grad_outer(part):
        start, stop = ((0, middle), (middle, ff))[part]
        grad_columns(flipped[...], gelu_low, start, stop - start, outer_col + start, stop - start)

    def ffn_backward():
        def narrow(h):
            for i in range(ff // tile):
                start = i * tile
                grad = mm(gs[h], weights(outer_col + start, tile)) * dgelu[h, :, start : start + tile].astype(F32)
                ginner[h, :, start : start + tile] = grad.astype(LOW)

        vecg_buf[0, 4:5, :] = jnp.sum(vec_acc[0], axis=0, keepdims=True)
        vecg_buf[0, 5:6, :] = jnp.sum(vec_acc[1], axis=0, keepdims=True)
        vecg_buf[0, 3:4, :] = mm(ones, gs[half])[0:1, :]

        narrow(half)
        narrow(other)
        copy = two_halves(ginner, ff, inner_col, part_send, 5, part_land.at[2])
        for i in range(ff // width):
            columns = slice(i * width, (i + 1) * width)
            vecg_buf[0, 6 + i : 7 + i, :] = (mm(ones, ginner[0, :, columns]) + mm(ones, ginner[1, :, columns]))[0:1, :]
        copy.wait()
        for i in range(3):
            vec_acc[i] = jnp.zeros((8, width), F32)

        def norm_back(i, carry):
            at = pl.ds(pl.multiple_of(i * chunk, chunk), chunk)
            grad_hidden = grad_keep[at, :] + (own_part[at, :] + part_land[2, at, :].astype(F32))
            unit = normed[at, :]
            vec_acc[0] = vec_acc[0] + fold_rows(grad_hidden * unit)
            vec_acc[1] = vec_acc[1] + fold_rows(grad_hidden)
            scaled = grad_hidden * vec[1:2, :]
            grad_mid = (scaled - mean_of(scaled) - unit * mean_of(scaled * unit)) * spread[at, 0:1]
            grad_keep[at, :] = grad_mid
            gb[half, at, :] = grad_mid.astype(LOW)
            return carry

        lax.fori_loop(0, chunks, norm_back, 0)
        pending[6] = pair_copy(gb.at[half], gb.at[half], 6)
        pending[6].start()
        vecg_buf[0, 1:2, :] = jnp.sum(vec_acc[0], axis=0, keepdims=True)
        vecg_buf[0, 2:3, :] = jnp.sum(vec_acc[1], axis=0, keepdims=True)
        vecg_buf[0, 0:1, :] = mm(ones, gb[half])[0:1, :]

    def grad_inner():
        grad_columns(hs_flipped[...], ginner, 0, ff, inner_col)

    def grad_out():
        pending[6].wait()
        flipped[...] = gb[...].reshape(2 * tall, width).T
        grad_columns(flipped[...], attn, 0, heads_wide, out_col)

    def heads_backward():
        def to_heads(h, carry):
            gattn[h] = mm(gb[h], weights(out_col, heads_wide)).astype(LOW)
            return carry

        lax.fori_loop(0, 2, to_heads, 0)

    def input_away():
        last_send[...] = mm(dqkv[other], weights(0, 3 * heads_wide), NT).astype(LOW)
        pending[7] = pair_copy(last_send, last_land, 7)
        pending[7].start()

    def grad_heads():
        grad_columns(xs_flipped[...], dqkv, 0, 3 * heads_wide, 0)

    def input_backward():
        own_part[...] = mm(dqkv[half], weights(0, 3 * heads_wide), NT)
        pending[7].wait()

        def leave(i, carry):
            at = pl.ds(pl.multiple_of(i * chunk, chunk), chunk)
            m, quarter = i // per_bin, lax.rem(i, per_bin)
            sources = pl.ds(quarter * (chunk // rows), chunk // rows)
            grad_x = grad_keep[at, :] + (own_part[at, :] + last_land[at, :].astype(F32))
            gx_send[sources, m] = grad_x.reshape(chunk // rows, rows, width).astype(LOW)
            return carry

        lax.fori_loop(0, chunks, leave, 0)

    def pair_vectors():
        for i, start in enumerate((0, value_col)):
            columns = slice(start, start + heads_wide)
            vecg_buf[0, 8:9, i * heads_wide : (i + 1) * heads_wide] = (
                mm(ones, dqkv[0, :, columns]) + mm(ones, dqkv[1, :, columns])
            )[0:1, :]
        vecg_buf[0, 9:16, :] = jnp.zeros((7, width), F32)

        swap_v = pair_copy(vecg_buf.at[0], vec_pair, 8)
        swap_v.start()
        swap_v.wait()
        vecg_buf[0, 0:6, :] = vecg_buf[0, 0:6, :] + vec_pair[0:6, :]

    def take_output():
        settle(out_send, out_land, out_sems)
        hand_back(out_land, layer_out_ref, layer_out_hbm)

    def take_input_grad():
        settle(gx_send, gx_land, gx_sems)
        hand_back(gx_land, grad_tokens_ref, grad_tokens_hbm)

    folds = []

    def sum_vectors(turn=None):
        if folds:
            folds[-1]()
        if len(folds) < stages:
            begin, fold = swing(vecg_buf, vecg_land, vecg_sems, len(folds), vec_out_ref)
            begin()
            folds.append(fold)
        else:
            folds.append(lambda: None)

    exchanges = {
        X: (x_send, x_land, x_sems),
        DY: (dy_send, dy_land, dy_sems),
        OUT: (out_send, out_land, out_sems),
        GX: (gx_send, gx_land, gx_sems),
    }
    steps = {
        GATHER: advance,
        REDUCE: reduce,
        NEAR: lambda name: push(*exchanges[name], True),
        FAR: lambda name: push(*exchanges[name], False),
        VECTORS: sum_vectors,
        FIND_SLOTS: find_slots,
        SEND_PIECES: send_pieces,
        ARRANGE_TOKENS: arrange_tokens,
        ARRANGE_COTANGENT: arrange_cotangent,
        WHOLE_VECTORS: whole_vectors,
        MASK_BINS: mask_bins,
        TAKE_TOKENS: take_tokens,
        PROJECT_HEADS: project_heads,
        ATTEND_THIRD: attend_third,
        ATTEND_BACK_THIRD: attend_back_third,
        PROJECT_OUT: project_out,
        NORM_AFTER_ATTENTION: norm_after_attention,
        WIDEN_TOKENS: widen_tokens,
        NARROW_TOKENS: narrow_tokens,
        NORM_AFTER_FFN: norm_after_ffn,
        NORM_FFN_BACKWARD: norm_ffn_backward,
        GRAD_OUTER: grad_outer,
        FFN_BACKWARD: ffn_backward,
        GRAD_INNER: grad_inner,
        GRAD_OUT: grad_out,
        HEADS_BACKWARD: heads_backward,
        INPUT_AWAY: input_away,
        GRAD_HEADS: grad_heads,
        INPUT_BACKWARD: input_backward,
        PAIR_VECTORS: pair_vectors,
        TAKE_OUTPUT: take_output,
        TAKE_INPUT_GRAD: take_input_grad,
    }
    covered = {
        PROJECT_HEADS: (0, 3 * heads_wide),
        PROJECT_OUT: (out_col, inner_col),
        WIDEN_TOKENS: (inner_col, outer_col),
        NARROW_TOKENS: (outer_col, outer_col + ff),
    }
    for name, *which in SCHEDULE:
        low, high = covered.get(name, (0, 0))
        for number in sorted({plan[0] for plan in gather_plan}):
            cols = extent(gather_plan, number)
            while cols.start < high and cols.start + cols.size > low and gone.get(number, 0) <= stages:
                advance(number)
        steps[name](*which)
    for number in sorted({plan[0] for plan in scatter_plan}):
        while sent[number] <= stages:
            reduce(number)
    while len(folds) <= stages:
        sum_vectors()
    every_column = pl.ds(0, full.shape[-1])
    for stage in range(stages):
        shards_copy(
            full, stages - stage, every_column, gather_sends.at[stage], gather_recvs.at[0, stage]
        ).wait_send()
        shards_copy(
            grads, stage + 1, every_column, scatter_sends.at[stage], scatter_recvs.at[0, stage]
        ).wait_send()
    for copy in leaving:
        copy.wait()


def finish(*refs):
    sources, total_ref, targets = refs[:8], refs[8], refs[9:17]
    *own_refs, inner_ref, query_ref, value_ref = refs[17:26]
    *held, sems = refs[26:]
    loads = [pltpu.make_async_copy(src, hold, sems.at[0, i]) for i, (src, hold) in enumerate(zip(sources, held))]
    stores = [pltpu.make_async_copy(hold, dst, sems.at[1, i]) for i, (hold, dst) in enumerate(zip(held, targets))]
    for load in loads:
        load.start()
    for load, store in zip(loads, stores):
        load.wait()
        store.start()
    place = lax.axis_index("dp")

    def cut(row, size):
        extent = row.shape[1]
        source = lax.broadcasted_iota(jnp.int32, (extent, size), 0)
        at = lax.broadcasted_iota(jnp.int32, (extent, size), 1) + place * size
        return lax.dot_general(
            row,
            (source == at).astype(F32),
            NN,
            precision=lax.Precision.HIGHEST,
            preferred_element_type=F32,
        )

    own = cut(total_ref[0:8, :], own_refs[0].shape[0])
    for i, ref in enumerate(own_refs):
        ref[...] = own[i : i + 1, :].reshape(ref.shape)
    width, heads_wide = total_ref.shape[1], query_ref.shape[1]
    rows = inner_ref.shape[1] * lax.axis_size("dp") // width
    long = jnp.concatenate([total_ref[6 + i : 7 + i, :] for i in range(rows)], axis=1)
    inner_ref[...] = cut(jnp.broadcast_to(long, (8, long.shape[1])), inner_ref.shape[1])[0:1, :]
    query_ref[...] = total_ref[8:9, :heads_wide]
    value_ref[...] = total_ref[8:9, heads_wide:]
    for store in stores:
        store.wait()


def plans(dp_count, heads_wide, ff):
    bits = bits_of(dp_count)
    far, near = bits[:-2], bits[-2:]
    orders = {
        FAR_FIRST: (far + near, far + near[::-1]),
        NEAR_FIRST: (near[::-1] + far, near + far),
    }

    def plan_of(groups, turned):
        plan = []
        for group, (kind, first, tiles) in enumerate(groups):
            start, size = first * LANES, (tiles + 1) // 2 * LANES
            one, two = (order[::-1] if turned else order for order in orders[kind])
            plan.append((group, one, start, size))
            plan.append((group, two, start + size, tiles * LANES - size))
        return plan

    return plan_of(GATHERS, False), plan_of(SCATTERS, True)


def shards_fast(
    tokens,
    cotangent,
    block_route,
    lengths,
    w_query,
    w_key,
    w_value,
    b_query,
    b_value,
    w_out,
    b_out,
    gain_attn,
    shift_attn,
    w_inner,
    b_inner,
    w_outer,
    b_outer,
    gain_ffn,
    shift_ffn,
):
    dp_count = lax.axis_size("dp")
    micro, rows, width = lengths.shape[0], tokens.shape[1], tokens.shape[2]
    heads_wide, ff = w_query.shape[1], w_inner.shape[1]
    place = lax.axis_index("dp")
    blocks = micro * dp_count
    own_width = width // dp_count
    columns = 4 * heads_wide + 2 * ff
    stages = dp_count.bit_length() - 1
    bits = (2,) * stages
    inner_col, outer_col = 4 * heads_wide, 4 * heads_wide + ff
    gather_plan, scatter_plan = plans(dp_count, heads_wide, ff)
    bin_half = dp_count * rows
    tall = micro * bin_half
    vmem, smem = pl.BlockSpec(memory_space=pltpu.VMEM), pl.BlockSpec(memory_space=pltpu.SMEM)
    dma = pltpu.SemaphoreType.DMA
    swap_shape = (dp_count, micro, rows, width)
    scratch = [
        pltpu.SMEM((micro, dp_count), jnp.int32),
        pltpu.SMEM((blocks,), jnp.int32),
        pltpu.VMEM(tokens.shape, LOW),
        pltpu.VMEM(tokens.shape, LOW),
        pltpu.VMEM(tokens.shape, LOW),
        pltpu.VMEM(tokens.shape, LOW),
        pltpu.VMEM((own_width, columns), F32),
        pltpu.VMEM(bits + (own_width, columns), LOW),
        pltpu.VMEM(bits + (own_width, columns), LOW),
    ]
    scratch += [pltpu.VMEM(swap_shape, LOW) for _ in range(8)]
    scratch += [pltpu.VMEM((2, tall, width), LOW) for _ in range(4)]
    scratch += [pltpu.VMEM((width, 2 * tall), LOW) for _ in range(3)]
    scratch += [pltpu.VMEM((2, tall, 3 * heads_wide), LOW) for _ in range(2)]
    scratch += [pltpu.VMEM((2, tall, heads_wide), LOW) for _ in range(2)]
    scratch += [
        pltpu.VMEM((micro, heads_wide // HD, 2 * bin_half, 2 * bin_half), LOW),
        pltpu.VMEM((micro, 2 * bin_half, 2 * bin_half), F32),
    ]
    scratch += [pltpu.VMEM((2, tall, ff), LOW) for _ in range(3)]
    scratch += [
        pltpu.VMEM((tall, width), F32),
        pltpu.VMEM((tall, LANES), F32),
        pltpu.VMEM((tall, LANES), F32),
        pltpu.VMEM((tall, width), F32),
        pltpu.VMEM((tall, width), F32),
        pltpu.VMEM((tall, width), LOW),
        pltpu.VMEM((3, tall, width), LOW),
        pltpu.VMEM((tall, width), LOW),
        pltpu.VMEM((tall, width), LOW),
        pltpu.VMEM((16, LANES), F32),
        pltpu.VMEM((dp_count, 16, LANES), F32),
        pltpu.VMEM((16, width), F32),
        pltpu.VMEM((16, width), F32),
        pltpu.VMEM((stages, 16, width), F32),
        pltpu.VMEM((stages, 16, width), F32),
        pltpu.VMEM((3, 8, width), F32),
    ]
    scratch += [
        pltpu.VMEM(
            (2,) * (stages - 1 - stage)
            + (own_width, sum(size for group, _, _, size in scatter_plan if group == wanted)),
            LOW,
        )
        for wanted in range(max(group for group, _, _, _ in scatter_plan) + 1)
        for stage in range(stages)
    ]
    scratch += [dma((2,)) for _ in range(4)]
    scratch += [
        dma((stages,)),
        dma((len(gather_plan), stages)),
        dma((stages,)),
        dma((len(scatter_plan), stages)),
        dma((2,)),
        dma((2, stages)),
        dma((2, 10)),
        dma((8,)),
        dma((24,)),
    ]
    sizes = (dp_count, micro, rows, width, heads_wide, ff)
    hbm = pl.BlockSpec(memory_space=pl.ANY)
    grad_shapes = [jax.ShapeDtypeStruct((own_width, size), F32) for size in (heads_wide,) * 4 + (ff,) * 2]
    made = (
        jax.ShapeDtypeStruct(tokens.shape, tokens.dtype),
        jax.ShapeDtypeStruct(tokens.shape, tokens.dtype),
        *grad_shapes,
    )
    *big, total = pl.pallas_call(
        partial(layer, sizes, gather_plan, scatter_plan),
        out_shape=(*made, jax.ShapeDtypeStruct((16, width), F32)),
        in_specs=[hbm] * 2 + [smem] * 2 + [hbm] * 6 + [vmem] * 10,
        out_specs=[hbm] * 8 + [vmem],
        scratch_shapes=scratch,
        compiler_params=pltpu.CompilerParams(
            collective_id=0, has_side_effects=True, vmem_limit_bytes=VMEM_BYTES
        ),
        name="layer",
    )(
        tokens,
        cotangent,
        block_route,
        lengths,
        w_query,
        w_key,
        w_value,
        w_out.T,
        w_inner,
        w_outer.T,
        b_out,
        gain_attn,
        shift_attn,
        b_outer,
        gain_ffn,
        shift_ffn,
        block_route,
        b_query,
        b_value,
        b_inner,
    )
    own_inner = b_inner.shape[1]
    results = pl.pallas_call(
        finish,
        out_shape=(
            *made,
            *[jax.ShapeDtypeStruct((own_width,), F32) for _ in range(6)],
            jax.ShapeDtypeStruct((1, own_inner), F32),
            jax.ShapeDtypeStruct((1, heads_wide), F32),
            jax.ShapeDtypeStruct((1, heads_wide), F32),
        ),
        in_specs=[hbm] * 8 + [vmem],
        out_specs=[hbm] * 8 + [vmem] * 9,
        scratch_shapes=[pltpu.VMEM(result.shape, result.dtype) for result in made] + [dma((2, 8))],
        name="finish",
    )(*big, total)
    layer_out, grad_tokens, gq, gk, gv, go, gi, gu = results[:8]
    own, (bias_inner, bias_query, bias_value) = results[8:14], results[14:]
    return (
        layer_out,
        grad_tokens,
        gq,
        gk,
        gv,
        bias_query,
        bias_value,
        go.T,
        own[0],
        own[1],
        own[2],
        gi,
        bias_inner,
        gu.T,
        own[3],
        own[4],
        own[5],
    )


def shards(
    tokens,
    cotangent,
    block_route,
    lengths,
    w_query,
    w_key,
    w_value,
    b_query,
    b_value,
    w_out,
    b_out,
    gain_attn,
    shift_attn,
    w_inner,
    b_inner,
    w_outer,
    b_outer,
    gain_ffn,
    shift_ffn,
):
    dp_count = lax.axis_size("dp")
    micro_count = lengths.shape[0]
    half_rows = tokens.shape[1]
    model_width = tokens.shape[2]
    local_heads = HEADS // lax.axis_size("tensor")
    score_scale = HD ** (-0.5)
    blocks = tokens.reshape(micro_count, dp_count, half_rows, model_width)
    upstream = cotangent.reshape(micro_count, dp_count, half_rows, model_width)
    target = block_route.reshape(micro_count, dp_count)
    dest_dev = target // (micro_count * dp_count)
    bin_place = target % dp_count
    micro_ids = jnp.broadcast_to(
        jnp.arange(micro_count, dtype=jnp.int32)[:, None], (micro_count, dp_count)
    )
    slot_ids = jnp.broadcast_to(
        jnp.arange(dp_count, dtype=jnp.int32)[None, :], (micro_count, dp_count)
    )
    inverse = jnp.zeros((micro_count, dp_count), jnp.int32).at[micro_ids, dest_dev].set(slot_ids)
    by_dest = jnp.take_along_axis(blocks, inverse[:, :, None, None], axis=1)
    grad_dest = jnp.take_along_axis(upstream, inverse[:, :, None, None], axis=1)
    place_dest = jnp.take_along_axis(bin_place, inverse, axis=1)
    arrived, arrived_grad, arrived_place = (
        lax.all_to_all(by_dest, "dp", split_axis=1, concat_axis=1, tiled=True),
        lax.all_to_all(grad_dest, "dp", split_axis=1, concat_axis=1, tiled=True),
        lax.all_to_all(place_dest, "dp", split_axis=1, concat_axis=1, tiled=True),
    )
    anchor = (
        jnp.zeros((micro_count, dp_count), jnp.int32).at[micro_ids, arrived_place].set(slot_ids)
    )
    bin_tokens = jnp.take_along_axis(arrived, anchor[:, :, None, None], axis=1)
    bin_grads = jnp.take_along_axis(arrived_grad, anchor[:, :, None, None], axis=1)
    acc_query = jnp.zeros((model_width, w_query.shape[1]), jnp.float32)
    acc_key = jnp.zeros((model_width, w_key.shape[1]), jnp.float32)
    acc_value = jnp.zeros((model_width, w_value.shape[1]), jnp.float32)
    acc_out = jnp.zeros((w_out.shape[0], model_width), jnp.float32)
    acc_inner = jnp.zeros((model_width, w_inner.shape[1]), jnp.float32)
    acc_outer = jnp.zeros((w_outer.shape[0], model_width), jnp.float32)
    acc_bias_query = jnp.zeros((1, w_query.shape[1]), jnp.float32)
    acc_bias_value = jnp.zeros((1, w_value.shape[1]), jnp.float32)
    acc_bias_inner = jnp.zeros((1, w_inner.shape[1]), jnp.float32)
    acc_vectors = jnp.zeros((6, model_width), jnp.float32)
    out_bins = []
    grad_bins = []
    for micro_step in range(micro_count):
        gathered = (
            lax.all_gather(w_query, "dp", axis=0, tiled=True),
            lax.all_gather(w_key, "dp", axis=0, tiled=True),
            lax.all_gather(w_value, "dp", axis=0, tiled=True),
            lax.all_gather(w_out, "dp", axis=1, tiled=True),
            lax.all_gather(w_inner, "dp", axis=0, tiled=True),
            lax.all_gather(w_outer, "dp", axis=1, tiled=True),
            lax.all_gather(b_inner, "dp", axis=1, tiled=True),
            lax.all_gather(b_out, "dp", axis=0, tiled=True),
            lax.all_gather(gain_attn, "dp", axis=0, tiled=True),
            lax.all_gather(shift_attn, "dp", axis=0, tiled=True),
            lax.all_gather(b_outer, "dp", axis=0, tiled=True),
            lax.all_gather(gain_ffn, "dp", axis=0, tiled=True),
            lax.all_gather(shift_ffn, "dp", axis=0, tiled=True),
        )
        (
            full_query,
            full_key,
            full_value,
            full_out,
            full_inner,
            full_outer,
            bias_inner,
            bias_out,
            full_gain_attn,
            full_shift_attn,
            bias_outer,
            full_gain_ffn,
            full_shift_ffn,
        ) = gathered
        own_rows = bin_tokens[micro_step]
        whole_bin = lax.all_gather(own_rows, "tensor", axis=1, tiled=True).reshape(-1, model_width)
        bin_rows = whole_bin.shape[0]
        block_rows = math.gcd(bin_rows, 512)
        segment = segment_of(lengths[micro_step], bin_rows)
        query = (
            jnp.dot(whole_bin, full_query, preferred_element_type=jnp.float32) + b_query[0]
        ).astype(jnp.bfloat16)
        keys = jnp.dot(whole_bin, full_key, preferred_element_type=jnp.float32).astype(jnp.bfloat16)
        values = (
            jnp.dot(whole_bin, full_value, preferred_element_type=jnp.float32) + b_value[0]
        ).astype(jnp.bfloat16)
        query_heads = query.reshape(bin_rows, local_heads, HD)
        key_heads = keys.reshape(bin_rows, local_heads, HD)
        value_heads = values.reshape(bin_rows, local_heads, HD)
        attn_heads, log_totals = attend_forward(
            query_heads, key_heads, value_heads, segment, block_rows, score_scale
        )
        attn = attn_heads.reshape(bin_rows, local_heads * HD)
        attn_partial = jnp.dot(attn, full_out, preferred_element_type=jnp.float32).reshape(
            dp_count, -1, model_width
        )
        branch = lax.psum_scatter(attn_partial, "tensor", scatter_dimension=1, tiled=True).reshape(
            -1, model_width
        )
        mid = own_rows.reshape(-1, model_width).astype(jnp.float32) + branch + bias_out
        hidden, normed_attn, spread_attn = layer_norm(mid, full_gain_attn, full_shift_attn)
        hidden_low = hidden.astype(jnp.bfloat16).reshape(dp_count, half_rows, model_width)
        hidden_whole = lax.all_gather(hidden_low, "tensor", axis=1, tiled=True).reshape(
            -1, model_width
        )
        inner = (
            jnp.dot(hidden_whole, full_inner, preferred_element_type=jnp.float32) + bias_inner[0]
        )
        gelu_value, gelu_pull = jax.vjp(partial(jax.nn.gelu, approximate=False), inner)
        gelu_low = gelu_value.astype(jnp.bfloat16)
        ffn_partial = jnp.dot(gelu_low, full_outer, preferred_element_type=jnp.float32).reshape(
            dp_count, -1, model_width
        )
        ffn = lax.psum_scatter(ffn_partial, "tensor", scatter_dimension=1, tiled=True).reshape(
            -1, model_width
        )
        top = hidden + ffn + bias_outer
        result, normed_ffn, spread_ffn = layer_norm(top, full_gain_ffn, full_shift_ffn)
        out_bins.append(result.astype(jnp.bfloat16).reshape(dp_count, half_rows, model_width))
        back_full = (
            lax.all_gather(w_query, "dp", axis=0, tiled=True),
            lax.all_gather(w_key, "dp", axis=0, tiled=True),
            lax.all_gather(w_value, "dp", axis=0, tiled=True),
            lax.all_gather(w_out, "dp", axis=1, tiled=True),
            lax.all_gather(w_inner, "dp", axis=0, tiled=True),
            lax.all_gather(w_outer, "dp", axis=1, tiled=True),
            lax.all_gather(gain_attn, "dp", axis=0, tiled=True),
            lax.all_gather(gain_ffn, "dp", axis=0, tiled=True),
        )
        (
            back_query,
            back_key,
            back_value,
            back_out,
            back_inner,
            back_outer,
            back_gain_attn,
            back_gain_ffn,
        ) = back_full
        grad_result = bin_grads[micro_step].reshape(-1, model_width).astype(jnp.float32)
        grad_top, grad_gain_ffn, grad_shift_ffn = norm_back(
            grad_result, normed_ffn, spread_ffn, back_gain_ffn
        )
        grad_ffn_low = grad_top.astype(jnp.bfloat16)
        grad_bias_outer = jnp.sum(grad_ffn_low.astype(jnp.float32), axis=0)
        grad_ffn_whole = lax.all_gather(
            grad_ffn_low.reshape(dp_count, half_rows, model_width), "tensor", axis=1, tiled=True
        ).reshape(-1, model_width)
        acc_outer = acc_outer + jnp.einsum(
            "nf,nd->fd", gelu_low, grad_ffn_whole, preferred_element_type=jnp.float32
        )
        grad_gelu = jnp.einsum(
            "nd,fd->nf", grad_ffn_whole, back_outer, preferred_element_type=jnp.float32
        )
        grad_inner_low = gelu_pull(grad_gelu)[0].astype(jnp.bfloat16)
        acc_bias_inner = acc_bias_inner + jnp.sum(grad_inner_low.astype(jnp.float32), axis=0)[None]
        acc_inner = acc_inner + jnp.einsum(
            "nd,nf->df", hidden_whole, grad_inner_low, preferred_element_type=jnp.float32
        )
        hidden_partial = jnp.einsum(
            "nf,df->nd", grad_inner_low, back_inner, preferred_element_type=jnp.float32
        ).reshape(dp_count, -1, model_width)
        grad_hidden = grad_top + lax.psum_scatter(
            hidden_partial, "tensor", scatter_dimension=1, tiled=True
        ).reshape(-1, model_width)
        grad_mid, grad_gain_attn, grad_shift_attn = norm_back(
            grad_hidden, normed_attn, spread_attn, back_gain_attn
        )
        grad_branch_low = grad_mid.astype(jnp.bfloat16)
        grad_bias_out = jnp.sum(grad_branch_low.astype(jnp.float32), axis=0)
        grad_branch_whole = lax.all_gather(
            grad_branch_low.reshape(dp_count, half_rows, model_width), "tensor", axis=1, tiled=True
        ).reshape(-1, model_width)
        acc_out = acc_out + jnp.einsum(
            "nh,nd->hd", attn, grad_branch_whole, preferred_element_type=jnp.float32
        )
        grad_attn_low = jnp.einsum(
            "nd,hd->nh", grad_branch_whole, back_out, preferred_element_type=jnp.float32
        ).astype(jnp.bfloat16)
        grad_heads = grad_attn_low.reshape(bin_rows, local_heads, HD)
        grad_query, grad_keys, grad_values = attend_backward(
            query_heads,
            key_heads,
            value_heads,
            grad_heads,
            log_totals,
            segment,
            block_rows,
            score_scale,
        )
        grad_query_low = grad_query.reshape(bin_rows, -1).astype(jnp.bfloat16)
        grad_key_low = grad_keys.reshape(bin_rows, -1).astype(jnp.bfloat16)
        grad_value_low = grad_values.reshape(bin_rows, -1).astype(jnp.bfloat16)
        acc_bias_query = acc_bias_query + jnp.sum(grad_query_low.astype(jnp.float32), axis=0)[None]
        acc_bias_value = acc_bias_value + jnp.sum(grad_value_low.astype(jnp.float32), axis=0)[None]
        acc_query = acc_query + jnp.einsum(
            "nd,nh->dh", whole_bin, grad_query_low, preferred_element_type=jnp.float32
        )
        acc_key = acc_key + jnp.einsum(
            "nd,nh->dh", whole_bin, grad_key_low, preferred_element_type=jnp.float32
        )
        acc_value = acc_value + jnp.einsum(
            "nd,nh->dh", whole_bin, grad_value_low, preferred_element_type=jnp.float32
        )
        input_partial = (
            jnp.einsum("nh,dh->nd", grad_query_low, back_query, preferred_element_type=jnp.float32)
            + jnp.einsum("nh,dh->nd", grad_key_low, back_key, preferred_element_type=jnp.float32)
            + jnp.einsum(
                "nh,dh->nd", grad_value_low, back_value, preferred_element_type=jnp.float32
            )
        )
        grad_input = grad_mid + lax.psum_scatter(
            input_partial.reshape(dp_count, -1, model_width).astype(jnp.bfloat16),
            "tensor",
            scatter_dimension=1,
            tiled=True,
        ).astype(jnp.float32).reshape(-1, model_width)
        grad_bins.append(grad_input.astype(jnp.bfloat16).reshape(dp_count, half_rows, model_width))
        acc_vectors = acc_vectors + jnp.stack(
            [
                grad_bias_out,
                grad_gain_attn,
                grad_shift_attn,
                grad_bias_outer,
                grad_gain_ffn,
                grad_shift_ffn,
            ]
        )
    out_stack = jnp.stack(out_bins)
    grad_stack = jnp.stack(grad_bins)
    send_out = jnp.take_along_axis(out_stack, arrived_place[:, :, None, None], axis=1)
    send_grad = jnp.take_along_axis(grad_stack, arrived_place[:, :, None, None], axis=1)
    back_out_rows, back_grad_rows = (
        lax.all_to_all(send_out, "dp", split_axis=1, concat_axis=1, tiled=True),
        lax.all_to_all(send_grad, "dp", split_axis=1, concat_axis=1, tiled=True),
    )
    layer_out = jnp.take_along_axis(back_out_rows, dest_dev[:, :, None, None], axis=1).reshape(
        tokens.shape
    )
    grad_tokens = jnp.take_along_axis(back_grad_rows, dest_dev[:, :, None, None], axis=1).reshape(
        tokens.shape
    )
    sum_query, sum_key, sum_value, sum_out, sum_inner, sum_outer, sum_bias_inner = (
        lax.psum_scatter(acc_query, "dp", scatter_dimension=0, tiled=True),
        lax.psum_scatter(acc_key, "dp", scatter_dimension=0, tiled=True),
        lax.psum_scatter(acc_value, "dp", scatter_dimension=0, tiled=True),
        lax.psum_scatter(acc_out, "dp", scatter_dimension=1, tiled=True),
        lax.psum_scatter(acc_inner, "dp", scatter_dimension=0, tiled=True),
        lax.psum_scatter(acc_outer, "dp", scatter_dimension=1, tiled=True),
        lax.psum_scatter(acc_bias_inner, "dp", scatter_dimension=1, tiled=True),
    )
    half_width = w_query.shape[1]
    tensor_pos = lax.axis_index("tensor")
    bias_pair = lax.dynamic_update_slice(
        jnp.zeros((2, model_width), jnp.float32),
        jnp.concatenate([acc_bias_query, acc_bias_value], axis=0),
        (jnp.int32(0), tensor_pos * half_width),
    )
    vectors, bias_total = lax.psum((acc_vectors, bias_pair), ("dp", "tensor"))
    own_width = model_width // dp_count
    vec_own = lax.dynamic_slice_in_dim(vectors, lax.axis_index("dp") * own_width, own_width, 1)
    bias_own = lax.dynamic_slice_in_dim(bias_total, tensor_pos * half_width, half_width, 1)
    return (
        layer_out,
        grad_tokens,
        sum_query,
        sum_key,
        sum_value,
        bias_own[0:1],
        bias_own[1:2],
        sum_out,
        vec_own[0],
        vec_own[1],
        vec_own[2],
        sum_inner,
        sum_bias_inner,
        sum_outer,
        vec_own[3],
        vec_own[4],
        vec_own[5],
    )


def solution(mesh):
    placed = (
        P("dp", "tensor", None),
        P("dp", "tensor", None),
        P("dp"),
        P("dp", None),
        P("dp", "tensor"),
        P("dp", "tensor"),
        P("dp", "tensor"),
        P("tensor", None),
        P("tensor", None),
        P("tensor", "dp"),
        P("dp"),
        P("dp"),
        P("dp"),
        P("dp", "tensor"),
        P("tensor", "dp"),
        P("tensor", "dp"),
        P("dp"),
        P("dp"),
        P("dp"),
    )
    dp_count = mesh.shape["dp"]

    def body(*args):
        tokens, w_query, b_inner = args[0], args[4], args[14]
        fits = (
            dp_count & (dp_count - 1) == 0
            and w_query.shape[0] % 16 == 0
            and tokens.shape[1] % 8 == 0
            and mesh.shape["tensor"] == 2
        )
        return (shards_fast if fits else shards)(*args)

    return jax.shard_map(
        body,
        mesh=mesh,
        in_specs=placed,
        out_specs=(
            P("dp", "tensor", None),
            P("dp", "tensor", None),
            P("dp", "tensor"),
            P("dp", "tensor"),
            P("dp", "tensor"),
            P("tensor", None),
            P("tensor", None),
            P("tensor", "dp"),
            P("dp"),
            P("dp"),
            P("dp"),
            P("dp", "tensor"),
            P("tensor", "dp"),
            P("tensor", "dp"),
            P("dp"),
            P("dp"),
            P("dp"),
        ),
        check_vma=False,
    )
```

```python
from functools import partial
import math

import jax
import jax.numpy as jnp
from jax import lax
from jax.experimental import pallas as pl
from jax.experimental.pallas import tpu as pltpu
from jax.sharding import PartitionSpec as P

HEADS = 12
HD = 64


EPS_NORM = 1e-12


def layer_norm(residual, norm_gain, norm_shift):
    centre = residual - jnp.mean(residual, axis=-1, keepdims=True)
    spread = lax.rsqrt(jnp.mean(centre * centre, axis=-1, keepdims=True) + EPS_NORM)
    normed = centre * spread
    return (normed * norm_gain + norm_shift, normed, spread)


def norm_back(grad_out, normed, spread, norm_gain):
    scaled = grad_out * norm_gain
    inner_term = (
        scaled
        - jnp.mean(scaled, axis=-1, keepdims=True)
        - normed * jnp.mean(scaled * normed, axis=-1, keepdims=True)
    )
    return (inner_term * spread, jnp.sum(grad_out * normed, axis=0), jnp.sum(grad_out, axis=0))


def segment_of(seq_lengths, count_rows):
    seq_ends = jnp.cumsum(seq_lengths)
    positions = jnp.arange(count_rows, dtype=jnp.int32)
    return jnp.sum((positions[:, None] >= seq_ends[None, :-1]).astype(jnp.int32), axis=1)


def masked_scores(query_block, key_heads, segment, first_row, block_rows, score_scale):
    scores = (
        jnp.einsum("qhd,khd->hqk", query_block, key_heads, preferred_element_type=jnp.float32)
        * score_scale
    )
    allowed = segment[first_row : first_row + block_rows, None] == segment[None, :]
    return jnp.where(allowed[None], scores, -1e30)


def attend_forward(query_heads, key_heads, value_heads, segment, block_rows, score_scale):
    scores = masked_scores(query_heads, key_heads, segment, 0, block_rows, score_scale)
    row_peak = jnp.max(scores, axis=-1, keepdims=True)
    exp_scores = jnp.exp(scores - row_peak)
    row_total = jnp.sum(exp_scores, axis=-1, keepdims=True)
    prob_low = (exp_scores / row_total).astype(jnp.bfloat16)
    out_block = jnp.einsum(
        "hqk,khd->qhd", prob_low, value_heads, preferred_element_type=jnp.float32
    )
    out_rows = out_block.astype(jnp.bfloat16)
    lse_rows = row_peak + jnp.log(row_total)
    return (out_rows, lse_rows)


def attend_backward(
    query_heads, key_heads, value_heads, grad_heads, log_totals, segment, block_rows, score_scale
):
    scores = masked_scores(query_heads, key_heads, segment, 0, block_rows, score_scale)
    probs_full = jnp.exp(scores - log_totals)
    prob_low = probs_full.astype(jnp.bfloat16)
    grad_values = jnp.einsum(
        "hqk,qhd->khd", prob_low, grad_heads, preferred_element_type=jnp.float32
    )
    grad_probs = jnp.einsum(
        "qhd,khd->hqk", grad_heads, value_heads, preferred_element_type=jnp.float32
    )
    row_inner = jnp.sum(probs_full * grad_probs, axis=-1, keepdims=True)
    grad_scores = (probs_full * (grad_probs - row_inner)).astype(jnp.bfloat16)
    grad_query_rows = (
        jnp.einsum("hqk,khd->qhd", grad_scores, key_heads, preferred_element_type=jnp.float32)
        * score_scale
    )
    grad_keys = (
        jnp.einsum("hqk,qhd->khd", grad_scores, query_heads, preferred_element_type=jnp.float32)
        * score_scale
    )
    return (grad_query_rows, grad_keys, grad_values)


MESH = pl.DeviceIdType.MESH
LANES = 128
NT = (((1,), (1,)), ((), ()))
NN = (((1,), (0,)), ((), ()))
F32 = jnp.float32
LOW = jnp.bfloat16
FAR_FIRST, NEAR_FIRST = range(2)
X, DY, OUT, GX = range(4)
(
    GATHER,
    REDUCE,
    NEAR,
    FAR,
    VECTORS,
    FIND_SLOTS,
    SEND_PIECES,
    ARRANGE_TOKENS,
    ARRANGE_COTANGENT,
    WHOLE_VECTORS,
    MASK_BINS,
    TAKE_TOKENS,
    PROJECT_HEADS,
    ATTEND_THIRD,
    ATTEND_BACK_THIRD,
    PROJECT_OUT,
    NORM_AFTER_ATTENTION,
    WIDEN_TOKENS,
    NARROW_TOKENS,
    NORM_AFTER_FFN,
    NORM_FFN_BACKWARD,
    GRAD_OUTER,
    FFN_BACKWARD,
    GRAD_INNER,
    GRAD_OUT,
    HEADS_BACKWARD,
    INPUT_AWAY,
    GRAD_HEADS,
    INPUT_BACKWARD,
    PAIR_VECTORS,
    TAKE_OUTPUT,
    TAKE_INPUT_GRAD,
) = range(32)

GATHERS = (
    (FAR_FIRST, 0, 3),
    (FAR_FIRST, 3, 6),
    (FAR_FIRST, 9, 7),
    (FAR_FIRST, 16, 8),
    (FAR_FIRST, 24, 4),
    (NEAR_FIRST, 28, 4),
    (NEAR_FIRST, 32, 4),
)
SCATTERS = (
    (FAR_FIRST, 24, 4),
    (NEAR_FIRST, 28, 8),
    (FAR_FIRST, 12, 12),
    (FAR_FIRST, 9, 3),
    (FAR_FIRST, 0, 5),
    (FAR_FIRST, 5, 4),
)
SCHEDULE = (
    (GATHER, 1),
    (GATHER, 6),
    (GATHER, 2),
    (SEND_PIECES,),
    (FIND_SLOTS,),
    (GATHER, 5),
    (GATHER, 0),
    (ARRANGE_TOKENS,),
    (NEAR, X),
    (GATHER, 1),
    (GATHER, 5),
    (GATHER, 0),
    (GATHER, 2),
    (GATHER, 6),
    (FAR, X),
    (GATHER, 3),
    (GATHER, 0),
    (GATHER, 1),
    (GATHER, 0),
    (GATHER, 4),
    (GATHER, 2),
    (GATHER, 1),
    (GATHER, 5),
    (WHOLE_VECTORS,),
    (GATHER, 3),
    (TAKE_TOKENS,),
    (GATHER, 6),
    (GATHER, 2),
    (ARRANGE_COTANGENT,),
    (GATHER, 4),
    (GATHER, 1),
    (GATHER, 0),
    (PROJECT_HEADS,),
    (GATHER, 3),
    (GATHER, 5),
    (MASK_BINS,),
    (ATTEND_THIRD, 0),
    (NEAR, DY),
    (GATHER, 4),
    (GATHER, 2),
    (ATTEND_THIRD, 1),
    (GATHER, 6),
    (ATTEND_THIRD, 2),
    (GATHER, 3),
    (GATHER, 4),
    (PROJECT_OUT,),
    (GATHER, 5),
    (FAR, DY),
    (NORM_AFTER_ATTENTION,),
    (GATHER, 3),
    (WIDEN_TOKENS,),
    (GATHER, 4),
    (GATHER, 6),
    (NARROW_TOKENS,),
    (NORM_AFTER_FFN,),
    (NEAR, OUT),
    (FAR, OUT),
    (NORM_FFN_BACKWARD,),
    (GRAD_OUTER, 0),
    (GRAD_OUTER, 1),
    (REDUCE, 1),
    (REDUCE, 0),
    (FFN_BACKWARD,),
    (GRAD_INNER,),
    (REDUCE, 2),
    (GRAD_OUT,),
    (REDUCE, 0),
    (HEADS_BACKWARD,),
    (ATTEND_BACK_THIRD, 0),
    (ATTEND_BACK_THIRD, 1),
    (ATTEND_BACK_THIRD, 2),
    (REDUCE, 1),
    (REDUCE, 3),
    (TAKE_OUTPUT,),
    (INPUT_AWAY,),
    (GRAD_HEADS,),
    (REDUCE, 2),
    (REDUCE, 5),
    (REDUCE, 0),
    (REDUCE, 2),
    (REDUCE, 4),
    (REDUCE, 0),
    (REDUCE, 5),
    (INPUT_BACKWARD,),
    (REDUCE, 2),
    (NEAR, GX),
    (REDUCE, 1),
    (REDUCE, 0),
    (REDUCE, 3),
    (PAIR_VECTORS,),
    (VECTORS,),
    (REDUCE, 4),
    (FAR, GX),
    (REDUCE, 5),
    (VECTORS,),
    (REDUCE, 4),
    (REDUCE, 5),
    (REDUCE, 3),
    (REDUCE, 1),
    (VECTORS,),
    (REDUCE, 4),
    (REDUCE, 1),
    (TAKE_INPUT_GRAD,),
    (REDUCE, 2),
    (REDUCE, 3),
    (VECTORS,),
    (VECTORS,),
    (REDUCE, 5),
    (REDUCE, 4),
    (REDUCE, 3),
)

VMEM_BYTES = 63 << 20


def flip(place, bit):
    return place + bit * (1 - 2 * ((place // bit) % 2))


def bit_of(place, bit):
    return (place // bit) % 2


def bits_of(count):
    return tuple(1 << i for i in range(count.bit_length() - 1))[::-1]


def orders_of(count):
    bits = bits_of(count)
    return (bits, bits[:-2] + bits[-2:][::-1])


def mm(left, right, dims=NN):
    return lax.dot_general(left, right, dims, preferred_element_type=F32)


class Gather:
    def __init__(self, dp_count, place, half, order, ref, start, size, send_sem, recv_sem):
        self.place, self.half, self.order = place, half, order
        self.bits = bits_of(dp_count)
        self.ref, self.cols = ref, pl.ds(start, size)
        self.send_sem, self.recv_sem = send_sem, recv_sem

    def copy(self, stage):
        done = self.order[:stage]
        index = tuple(
            slice(None) if bit in done else bit_of(self.place, bit) for bit in self.bits
        ) + (slice(None), self.cols)
        return pltpu.make_async_remote_copy(
            src_ref=self.ref.at[index],
            dst_ref=self.ref.at[index],
            send_sem=self.send_sem.at[stage],
            recv_sem=self.recv_sem.at[stage],
            device_id=(flip(self.place, self.order[stage]), self.half),
            device_id_type=MESH,
        )


class Scatter:
    def __init__(self, dp_count, place, half, order, ref, start, size, landing, send_sem, recv_sem):
        self.place, self.half = place, half
        self.order = order
        self.bits = bits_of(dp_count)
        self.ref, self.cols = ref, pl.ds(start, size)
        self.landing = landing
        self.send_sem, self.recv_sem = send_sem, recv_sem

    def view(self, stage, chosen):
        left = [bit for bit in self.bits if bit not in self.order[:stage]]
        own = bit_of(self.place, self.order[stage])
        index = tuple(
            (own if chosen == "own" else 1 - own) if bit == self.order[stage] else slice(None)
            for bit in left
        )
        if stage == 0:
            return self.ref.at[index + (slice(None), self.cols)]
        return self.landing[stage - 1].at[index]

    def copy(self, stage):
        return pltpu.make_async_remote_copy(
            src_ref=self.view(stage, "other"),
            dst_ref=self.landing[stage],
            send_sem=self.send_sem.at[stage],
            recv_sem=self.recv_sem.at[stage],
            device_id=(flip(self.place, self.order[stage]), self.half),
            device_id_type=MESH,
        )

    def add(self, stage):
        kept = self.view(stage, "own")
        land = self.landing[stage]
        lead = land.shape[:-2]
        count = math.prod(lead)

        def one(i, carry):
            index, rest = [], i
            for extent in lead[::-1]:
                index.append(lax.rem(rest, extent))
                rest = rest // extent
            index = tuple(index[::-1])
            land[index] = (kept[index].astype(F32) + land[index].astype(F32)).astype(land.dtype)
            return carry

        if count == 1:
            one(0, 0)
        else:
            lax.fori_loop(0, count, one, 0)

    def finish(self, stage, outs):
        kept = self.view(stage, "own")
        sums, refs, copy_out = outs
        sums[:, self.cols] = kept[...].astype(F32) + self.landing[stage][...].astype(F32)
        first, begin = self.cols.start, 0
        for ref in refs:
            low = max(first, begin)
            high = min(first + self.cols.size, begin + ref.shape[1])
            if low < high:
                copy_out(sums.at[:, pl.ds(low, high - low)], ref.at[:, pl.ds(low - begin, high - low)])
            begin += ref.shape[1]


def layer(sizes, gather_plan, scatter_plan, *refs):
    dp_count, micro, rows, width, heads_wide, ff = sizes
    (
        tokens_ref,
        cot_ref,
        route_ref,
        lengths_ref,
        wq_ref,
        wk_ref,
        wv_ref,
        wo_ref,
        wi_ref,
        wu_ref,
        *small_refs,
        bq_ref,
        bv_ref,
        bi_ref,
        layer_out_hbm,
        grad_tokens_hbm,
        gq_hbm,
        gk_hbm,
        gv_hbm,
        go_hbm,
        gi_hbm,
        gu_hbm,
    ) = refs[:28]
    vec_out_hbm = refs[28]
    (
        inverse_ref,
        target_ref,
        tokens_in,
        cot_in,
        layer_out_ref,
        grad_tokens_ref,
        sums,
        full,
        grads,
        x_send,
        dy_send,
        x_land,
        dy_land,
        out_send,
        gx_send,
        out_land,
        gx_land,
        xs,
        hs,
        gs,
        gb,
        flipped,
        xs_flipped,
        hs_flipped,
        qkv,
        dqkv,
        attn,
        gattn,
        probs,
        bias,
        gelu_low,
        dgelu,
        ginner,
        normed,
        spread,
        spread_ffn,
        grad_keep,
        own_part,
        part_send,
        part_land,
        last_send,
        last_land,
        piece,
        pieces,
        vec,
        vec_pair,
        vecg_buf,
        vecg_land,
        vec_acc,
        vec_total,
        *rest,
    ) = refs[29:]
    stages = dp_count.bit_length() - 1
    groups = max(group for group, _, _, _ in scatter_plan) + 1
    landings = [rest[i * stages : (i + 1) * stages] for i in range(groups)]
    (
        x_sems,
        dy_sems,
        out_sems,
        gx_sems,
        gather_sends,
        gather_recvs,
        scatter_sends,
        scatter_recvs,
        vec_sems,
        vecg_sems,
        pair_sems,
        in_sems,
        out_copy_sems,
    ) = rest[groups * stages :]
    place, half = lax.axis_index("dp"), lax.axis_index("tensor")
    other = 1 - half
    bits = bits_of(dp_count)
    orders = orders_of(dp_count)
    bin_half = dp_count * rows
    tall = micro * bin_half
    blocks = micro * dp_count
    own_width = width // dp_count
    block_len = 2 * rows
    pairs = heads_wide // LANES
    key_col, value_col, out_col = heads_wide, 2 * heads_wide, 3 * heads_wide
    inner_col, outer_col = 4 * heads_wide, 4 * heads_wide + ff
    tile = heads_wide

    def weights(start, size):
        return full[(slice(None),) * stages + (slice(None), pl.ds(start, size))].reshape(width, size)

    def pair_copy(src, dst, which):
        return pltpu.make_async_remote_copy(
            src_ref=src,
            dst_ref=dst,
            send_sem=pair_sems.at[0, which],
            recv_sem=pair_sems.at[1, which],
            device_id=(place, other),
            device_id_type=MESH,
        )

    group = dp_count // 2
    base, within_group = place - lax.rem(place, group), lax.rem(place, group)
    far_base = lax.rem(base + group, dp_count)

    def message(step, send_ref, recv_ref, sems, near):
        peer = (base if near else far_base) + lax.rem(within_group + step, group)
        return pltpu.make_async_remote_copy(
            src_ref=send_ref.at[peer],
            dst_ref=recv_ref.at[place],
            send_sem=sems.at[0],
            recv_sem=sems.at[1],
            device_id=(peer, half),
            device_id_type=MESH,
        )

    def push(send_ref, recv_ref, sems, near):
        def one(step, carry):
            message(step, send_ref, recv_ref, sems, near).start()
            return carry

        lax.fori_loop(1 if near else 0, group, one, 0)

    def settle(send_ref, recv_ref, sems):
        recv_ref[place] = send_ref[place]
        whole = pl.ds(0, dp_count - 1)
        every = pltpu.make_async_remote_copy(
            src_ref=send_ref.at[whole],
            dst_ref=recv_ref.at[whole],
            send_sem=sems.at[0],
            recv_sem=sems.at[1],
            device_id=(place, other),
            device_id_type=MESH,
        )
        every.wait_recv()
        every.wait_send()

    def arrange(src_ref, dst_ref):
        def one(i, carry):
            m, peer = i // dp_count, lax.rem(i, dp_count)
            dst_ref[peer, m] = src_ref[m * dp_count + inverse_ref[m, peer]]
            return carry

        lax.fori_loop(0, blocks, one, 0)

    barrier = pltpu.get_barrier_semaphore()

    def hello(step, carry):
        peer = lax.rem(place + step, dp_count)
        pl.semaphore_signal(barrier, inc=1, device_id=(peer, half), device_id_type=MESH)
        return carry

    lax.fori_loop(1, dp_count, hello, 0)
    pl.semaphore_signal(barrier, inc=1, device_id=(place, other), device_id_type=MESH)

    own = tuple(bit_of(place, bit) for bit in bits)
    fetches = [
        pltpu.make_async_copy(src, dst, in_sems.at[i])
        for i, (src, dst) in enumerate(
            [
                (ref, full.at[own + (slice(None), pl.ds(start, size))])
                for ref, start, size in (
                    (wq_ref, 0, heads_wide),
                    (wk_ref, key_col, heads_wide),
                    (wv_ref, value_col, heads_wide),
                    (wo_ref, out_col, heads_wide),
                    (wi_ref, inner_col, ff),
                    (wu_ref, outer_col, ff),
                )
            ]
            + [(tokens_ref, tokens_in), (cot_ref, cot_in)]
        )
    ]
    for fetch in fetches:
        fetch.start()
    leaving = []

    def copy_out(src, dst):
        copy = pltpu.make_async_copy(src, dst, out_copy_sems.at[len(leaving)])
        copy.start()
        leaving.append(copy)

    outs = (sums, (gq_hbm, gk_hbm, gv_hbm, go_hbm, gi_hbm, gu_hbm), copy_out)

    piece[...] = jnp.zeros((16, LANES), F32)
    for i, ref in enumerate(small_refs):
        piece[i : i + 1, 0:own_width] = ref[...].astype(F32).reshape(1, own_width)
    piece[8:16, 0 : bi_ref.shape[1]] = jnp.broadcast_to(bi_ref[...].astype(F32), (8, bi_ref.shape[1]))
    route = piece[6:7, 0:own_width]
    piece[7:8, 0:own_width] = route - dp_count * jnp.floor((route + 0.5) * (1.0 / dp_count))
    piece[6:7, 0:own_width] = jnp.floor((route + 0.5) * (1.0 / blocks))
    def find_target(i, carry):
        target_ref[i] = lax.div(route_ref[i], blocks)
        return carry


    def invert(i, carry):
        m, peer = lax.div(i, dp_count), lax.rem(i, dp_count)
        slot = jnp.int32(0)
        for k in range(dp_count):
            slot = jnp.where(target_ref[m * dp_count + k] == peer, k, slot)
        inverse_ref[m, peer] = slot
        return carry

    for fetch in fetches[:6]:
        fetch.wait()
    pl.semaphore_wait(barrier, dp_count)

    gathers = [
        Gather(
            dp_count,
            place,
            half,
            order,
            full,
            start,
            size,
            gather_sends,
            gather_recvs.at[i],
        )
        for i, (_, order, start, size) in enumerate(gather_plan)
    ]
    gone = {}

    def extent(plan, wanted):
        own_plan = [(start, start + size) for group, _, start, size in plan if group == wanted]
        start, stop = min(own_plan)[0], max(own_plan)[1]
        return pl.ds(start, stop - start)

    def shards_copy(ref, dropped, cols, send_sem, recv_sem):
        view = ref.at[(0,) * dropped + (slice(None),) * (stages - dropped + 1) + (cols,)]
        return pltpu.make_async_remote_copy(
            src_ref=view,
            dst_ref=view,
            send_sem=send_sem,
            recv_sem=recv_sem,
            device_id=(place, other),
            device_id_type=MESH,
        )

    def advance(*groups):
        for wanted in groups:
            stage = gone.get(wanted, 0)
            if stage > stages:
                continue
            gone[wanted] = stage + 1
            for (member, _, _, _), gather in zip(gather_plan, gathers):
                if member == wanted and stage > 0:
                    gather.copy(stage - 1).wait_recv()
                if member == wanted and stage < stages:
                    gather.copy(stage).start()

    def swing(buf, land, sems, stage, last_ref):
        copy = pltpu.make_async_remote_copy(
            src_ref=buf.at[stage],
            dst_ref=land.at[stage],
            send_sem=sems.at[0, stage],
            recv_sem=sems.at[1, stage],
            device_id=(flip(place, bits[stage]), half),
            device_id_type=MESH,
        )

        def fold():
            copy.wait()
            total = buf[stage] + land[stage]
            if stage < stages - 1:
                buf[stage + 1] = total
            else:
                last_ref[...] = total

        return copy.start, fold

    def push_piece(step, carry):
        peer = lax.rem(place + step, dp_count)
        pltpu.make_async_remote_copy(
            src_ref=piece,
            dst_ref=pieces.at[place],
            send_sem=vec_sems.at[0],
            recv_sem=vec_sems.at[1],
            device_id=(peer, half),
            device_id_type=MESH,
        ).start()
        return carry

    bits_shape = (2,) * stages
    scatters = [
        Scatter(
            dp_count,
            place,
            half,
            order,
            grads,
            start,
            size,
            [
                land.at[
                    (slice(None),) * (stages - stage)
                    + (pl.ds(start - extent(scatter_plan, group).start, size),)
                ]
                for stage, land in enumerate(landings[group])
            ],
            scatter_sends,
            scatter_recvs.at[i],
        )
        for i, (group, order, start, size) in enumerate(scatter_plan)
    ]
    sent = {}

    def reduce(*wanted_groups):
        for wanted in wanted_groups:
            stage = sent.get(wanted, 0)
            if stage > stages:
                continue
            sent[wanted] = stage + 1
            for (group, _, _, _), scatter in zip(scatter_plan, scatters):
                if group == wanted:
                    if stage > 0:
                        scatter.copy(stage - 1).wait_recv()
                    if 0 < stage < stages:
                        scatter.add(stage - 1)
                    elif stage == stages:
                        scatter.finish(stage - 1, outs)
                    if stage < stages:
                        scatter.copy(stage).start()

    def grad_columns(left_t, right_ref, start, columns, grads_start, tile=tile):
        for i in range(columns // tile):
            piece = mm(left_t, right_ref[:, :, start + i * tile : start + (i + 1) * tile].reshape(2 * tall, tile))
            grads[(slice(None),) * (stages + 1) + (pl.ds(grads_start + i * tile, tile),)] = piece.astype(
                LOW
            ).reshape(bits_shape + (own_width, tile))

    low_lane = lax.broadcasted_iota(jnp.int32, (2 * bin_half, LANES), 1) < HD
    nothing = jnp.zeros((2 * bin_half, LANES), LOW)

    def bin_of(ref, m, start):
        at = pl.ds(pl.multiple_of(m * bin_half, bin_half), bin_half)
        return jnp.concatenate([ref[0, at, pl.ds(start, LANES)], ref[1, at, pl.ds(start, LANES)]], axis=0)

    def put_bin(ref, m, start, value):
        at = pl.ds(pl.multiple_of(m * bin_half, bin_half), bin_half)
        ref[0, at, pl.ds(start, LANES)] = value[:bin_half].astype(ref.dtype)
        ref[1, at, pl.ds(start, LANES)] = value[bin_half:].astype(ref.dtype)

    def split_heads(value):
        return (jnp.where(low_lane, value, nothing), jnp.where(low_lane, nothing, value))

    def attend(m):
        for j in range(pairs):
            query = bin_of(qkv, m, j * LANES)
            key = bin_of(qkv, m, key_col + j * LANES)
            value = bin_of(qkv, m, value_col + j * LANES)
            total = None
            for e, (query_e, value_e) in enumerate(zip(split_heads(query), split_heads(value))):
                score = mm(query_e, key, NT) + bias[m]
                power = jnp.exp(score - jnp.max(score, axis=1, keepdims=True))
                prob = power * (1.0 / jnp.sum(power, axis=1, keepdims=True))
                probs[m, 2 * j + e] = prob.astype(probs.dtype)
                part = mm(prob.astype(LOW), value_e)
                total = part if total is None else total + part
            put_bin(attn, m, j * LANES, total)

    def two_halves(left_ref, columns, start, send_ref, which, land_ref):
        away = mm(left_ref[other], weights(start, columns), NT)
        send_ref[...] = away.astype(send_ref.dtype)
        copy = pair_copy(send_ref, land_ref, which)
        copy.start()
        own_part[...] = mm(left_ref[half], weights(start, columns), NT)
        return copy

    chunk = 4 * rows
    per_bin = bin_half // chunk
    chunks = tall // chunk
    ones = jnp.ones((8, tall), LOW)

    def mean_of(v):
        return jnp.sum(v, axis=1, keepdims=True) * (1.0 / width)

    def fold_rows(v):
        return jnp.sum(v.reshape(chunk // 8, 8, width), axis=0)

    def hand_back(land_ref, result_ref, hbm_ref):
        def one(i, carry):
            result_ref[i] = land_ref[target_ref[i], i // dp_count]
            return carry

        lax.fori_loop(0, blocks, one, 0)
        copy_out(result_ref, hbm_ref)

    def find_slots():
        lax.fori_loop(0, blocks, find_target, 0)
        lax.fori_loop(0, blocks, invert, 0)

    def send_pieces():
        lax.fori_loop(1, dp_count, push_piece, 0)

    def arrange_tokens():
        fetches[6].wait()
        arrange(tokens_in, x_send)

    def arrange_cotangent():
        fetches[7].wait()
        arrange(cot_in, dy_send)

    def whole_vectors():
        pieces[place] = piece[...]
        every_piece = pltpu.make_async_remote_copy(
            src_ref=pieces.at[pl.ds(0, dp_count - 1)],
            dst_ref=pieces.at[pl.ds(0, dp_count - 1)],
            send_sem=vec_sems.at[0],
            recv_sem=vec_sems.at[1],
            device_id=(place, other),
            device_id_type=MESH,
        )
        every_piece.wait_recv()
        every_piece.wait_send()

        def lay(source, total):
            block = pieces[source]

            def laid(block, size, extent):
                target = lax.broadcasted_iota(jnp.int32, (size, extent), 1)
                at = lax.broadcasted_iota(jnp.int32, (size, extent), 0)
                hit = target == at + source * size
                return mm(block[:, :size].astype(LOW), hit.astype(F32).astype(LOW))

            return (
                total[0] + laid(block[0:8], own_width, width),
                total[1] + laid(block[8:16], bi_ref.shape[1], ff),
            )

        short, long = lax.fori_loop(
            0, dp_count, lay, (jnp.zeros((8, width), F32), jnp.zeros((8, ff), F32))
        )
        vec[0:8, :] = short
        for i in range(ff // width):
            vec[8 + i : 9 + i, :] = long[0:1, i * width : (i + 1) * width]

    def mask_bins():
        placed = jnp.where(vec[6:7, :] == place.astype(F32), vec[7:8, :], 0.0)
        placed_rows = jnp.broadcast_to(placed, (8, blocks * dp_count))

        def mask_bin(m, carry):
            shape = (2 * bin_half, blocks * dp_count)
            row = lax.broadcasted_iota(jnp.int32, shape, 0)
            lane = lax.broadcasted_iota(jnp.int32, shape, 1)
            source = lax.rem(row, bin_half) // rows
            chosen = (lane // dp_count) == source * micro + m
            tall_place = jnp.sum(jnp.where(chosen, placed, 0.0), axis=1, keepdims=True)
            wide_place = mm(placed_rows, chosen.astype(F32), NT)[0:1, :]
            ends, end = [], 0
            for i in range(lengths_ref.shape[1] - 1):
                end = end + lengths_ref[m, i]
                ends.append(end.astype(F32))

            def sequence(at, index):
                within = (lax.rem(index, rows) + (index // bin_half) * rows).astype(F32)
                position = at * block_len + within
                return sum((position >= end).astype(F32) for end in ends)

            down = sequence(
                tall_place, lax.broadcasted_iota(jnp.int32, (2 * bin_half, 1), 0)
            )
            across = sequence(
                wide_place, lax.broadcasted_iota(jnp.int32, (1, 2 * bin_half), 1)
            )
            bias[m] = jnp.where(down == across, 0.0, -1e30)
            return carry

        lax.fori_loop(0, micro, mask_bin, 0)

    def take_tokens():
        settle(x_send, x_land, x_sems)

        def order_rows(m, carry):
            block = x_land[:, m].astype(F32).reshape(bin_half, width)
            xs[half, pl.ds(pl.multiple_of(m * bin_half, bin_half), bin_half), :] = block.astype(LOW)
            return carry

        lax.fori_loop(0, micro, order_rows, 0)
        swap_x = pair_copy(xs.at[half], xs.at[half], 0)
        swap_x.start()
        swap_x.wait()

    def project_heads():
        def project(i, carry):
            h = lax.rem(half + i, 2)
            own_rows = xs[h]
            qkv[h, :, pl.ds(0, heads_wide)] = (
                (mm(own_rows, weights(0, heads_wide)) + bq_ref[...].astype(F32)).astype(LOW)
                * LOW(HD ** (-0.5))
            )
            qkv[h, :, pl.ds(key_col, heads_wide)] = mm(own_rows, weights(key_col, heads_wide)).astype(LOW)
            qkv[h, :, pl.ds(value_col, heads_wide)] = (
                mm(own_rows, weights(value_col, heads_wide)) + bv_ref[...].astype(F32)
            ).astype(LOW)
            return carry

        lax.fori_loop(0, 2, project, 0)

    def attend_back(m):
        for j in range(pairs):
            query = bin_of(qkv, m, j * LANES)
            key = bin_of(qkv, m, key_col + j * LANES)
            value = bin_of(qkv, m, value_col + j * LANES)
            grad = bin_of(gattn, m, j * LANES)
            keys, queries, upstream = split_heads(key), split_heads(query), split_heads(grad)
            d_query = d_key = d_value = None
            for e in range(2):
                prob = probs[m, 2 * j + e].astype(F32)
                d_prob = mm(upstream[e], value, NT)
                inner = jnp.sum(prob * d_prob, axis=1, keepdims=True)
                d_score = (prob * (d_prob - inner)).astype(LOW)
                part_q = mm(d_score, keys[e])
                part_k = mm(d_score.T, queries[e])
                part_v = mm(prob.astype(LOW).T, upstream[e])
                d_query = part_q if d_query is None else d_query + part_q
                d_key = part_k if d_key is None else d_key + part_k
                d_value = part_v if d_value is None else d_value + part_v
            put_bin(dqkv, m, j * LANES, d_query * (HD ** (-0.5)))
            put_bin(dqkv, m, key_col + j * LANES, d_key)
            put_bin(dqkv, m, value_col + j * LANES, d_value)

    def attend_third(third):
        for m in range(third * micro // 3, (third + 1) * micro // 3):
            attend(m)

    def attend_back_third(third):
        for m in range(third * micro // 3, (third + 1) * micro // 3):
            attend_back(m)

    def project_out():
        two_halves(attn, heads_wide, out_col, part_send, 1, part_land.at[0]).wait()

    pending = {}

    def turn(ref, h):
        columns = pl.ds(pl.multiple_of(h * tall, LANES), tall)
        flipped[:, columns] = ref[h].T

    def norm_after_attention():
        def norm_attn(i, carry):
            at = pl.ds(pl.multiple_of(i * chunk, chunk), chunk)
            mid = xs[half, at, :].astype(F32) + (own_part[at, :] + part_land[0, at, :].astype(F32)) + vec[0:1, :]
            centre = mid - mean_of(mid)
            inverse_s = lax.rsqrt(mean_of(centre * centre) + EPS_NORM)
            unit = centre * inverse_s
            normed[at, :] = unit
            spread[at, :] = jnp.broadcast_to(inverse_s, (chunk, LANES))
            hs[half, at, :] = (unit * vec[1:2, :] + vec[2:3, :]).astype(LOW)
            return carry

        lax.fori_loop(0, chunks, norm_attn, 0)
        pending[2] = pair_copy(hs.at[half], hs.at[half], 2)
        pending[2].start()

    def widen_tokens():
        def widen(h):
            for i in range(ff // tile):
                start = i * tile
                row = 8 + start // width
                inner = mm(hs[h], weights(inner_col + start, tile)) + vec[
                    row : row + 1, start % width : start % width + tile
                ]
                cdf = 0.5 * (1.0 + lax.erf(inner * (0.5**0.5)))
                density = jnp.exp(-0.5 * inner * inner) * ((2.0 * math.pi) ** -0.5)
                gelu_low[h, :, start : start + tile] = (inner * cdf).astype(LOW)
                dgelu[h, :, start : start + tile] = (cdf + inner * density).astype(dgelu.dtype)

        def widen_step(i, carry):
            @pl.when(i == 1)
            def _():
                pending[2].wait()

            widen(lax.rem(half + i, 2))
            return carry

        lax.fori_loop(0, 2, widen_step, 0)
        xs_flipped[...] = xs[...].reshape(2 * tall, width).T
        hs_flipped[...] = hs[...].reshape(2 * tall, width).T

    def narrow_tokens():
        two_halves(gelu_low, ff, outer_col, part_send, 3, part_land.at[1]).wait()

    def norm_after_ffn():
        def norm_ffn(i, carry):
            at = pl.ds(pl.multiple_of(i * chunk, chunk), chunk)
            m, quarter = i // per_bin, lax.rem(i, per_bin)
            sources = pl.ds(quarter * (chunk // rows), chunk // rows)
            hidden = normed[at, :] * vec[1:2, :] + vec[2:3, :]
            top = hidden + (own_part[at, :] + part_land[1, at, :].astype(F32)) + vec[3:4, :]
            centre = top - mean_of(top)
            inverse_s = lax.rsqrt(mean_of(centre * centre) + EPS_NORM)
            unit = centre * inverse_s
            own_part[at, :] = unit
            spread_ffn[at, :] = jnp.broadcast_to(inverse_s, (chunk, LANES))
            result = unit * vec[4:5, :] + vec[5:6, :]
            out_send[sources, m] = result.reshape(chunk // rows, rows, width).astype(LOW)
            return carry

        lax.fori_loop(0, chunks, norm_ffn, 0)

    def norm_ffn_backward():
        settle(dy_send, dy_land, dy_sems)
        for i in range(3):
            vec_acc[i] = jnp.zeros((8, width), F32)

        def norm_ffn_back(i, carry):
            at = pl.ds(pl.multiple_of(i * chunk, chunk), chunk)
            m, quarter = i // per_bin, lax.rem(i, per_bin)
            sources = pl.ds(quarter * (chunk // rows), chunk // rows)
            unit = own_part[at, :]
            dy = dy_land[sources, m].astype(F32).reshape(chunk, width)
            vec_acc[0] = vec_acc[0] + fold_rows(dy * unit)
            vec_acc[1] = vec_acc[1] + fold_rows(dy)
            scaled = dy * vec[4:5, :]
            grad_top = (scaled - mean_of(scaled) - unit * mean_of(scaled * unit)) * spread_ffn[at, 0:1]
            grad_keep[at, :] = grad_top
            gs[half, at, :] = grad_top.astype(LOW)
            return carry

        swaps = []
        for i, which in enumerate((4, 9)):
            lax.fori_loop(i * (chunks // 2), (i + 1) * (chunks // 2), norm_ffn_back, 0)
            piece_of = gs.at[half, pl.ds(i * (tall // 2), tall // 2)]
            swap_g = pair_copy(piece_of, piece_of, which)
            swap_g.start()
            swaps.append(swap_g)
        turn(gs, half)
        for swap_g in swaps:
            swap_g.wait()
        turn(gs, other)

    middle = scatter_plan[1][2] + scatter_plan[1][3] - outer_col

    def grad_outer(part):
        start, stop = ((0, middle), (middle, ff))[part]
        grad_columns(flipped[...], gelu_low, start, stop - start, outer_col + start, stop - start)

    def ffn_backward():
        def narrow(h):
            for i in range(ff // tile):
                start = i * tile
                grad = mm(gs[h], weights(outer_col + start, tile)) * dgelu[h, :, start : start + tile].astype(F32)
                ginner[h, :, start : start + tile] = grad.astype(LOW)

        vecg_buf[0, 4:5, :] = jnp.sum(vec_acc[0], axis=0, keepdims=True)
        vecg_buf[0, 5:6, :] = jnp.sum(vec_acc[1], axis=0, keepdims=True)
        vecg_buf[0, 3:4, :] = mm(ones, gs[half])[0:1, :]

        narrow(half)
        narrow(other)
        copy = two_halves(ginner, ff, inner_col, part_send, 5, part_land.at[2])
        for i in range(ff // width):
            columns = slice(i * width, (i + 1) * width)
            vecg_buf[0, 6 + i : 7 + i, :] = (mm(ones, ginner[0, :, columns]) + mm(ones, ginner[1, :, columns]))[0:1, :]
        copy.wait()
        for i in range(3):
            vec_acc[i] = jnp.zeros((8, width), F32)

        def norm_back(i, carry):
            at = pl.ds(pl.multiple_of(i * chunk, chunk), chunk)
            grad_hidden = grad_keep[at, :] + (own_part[at, :] + part_land[2, at, :].astype(F32))
            unit = normed[at, :]
            vec_acc[0] = vec_acc[0] + fold_rows(grad_hidden * unit)
            vec_acc[1] = vec_acc[1] + fold_rows(grad_hidden)
            scaled = grad_hidden * vec[1:2, :]
            grad_mid = (scaled - mean_of(scaled) - unit * mean_of(scaled * unit)) * spread[at, 0:1]
            grad_keep[at, :] = grad_mid
            gb[half, at, :] = grad_mid.astype(LOW)
            return carry

        lax.fori_loop(0, chunks, norm_back, 0)
        pending[6] = pair_copy(gb.at[half], gb.at[half], 6)
        pending[6].start()
        vecg_buf[0, 1:2, :] = jnp.sum(vec_acc[0], axis=0, keepdims=True)
        vecg_buf[0, 2:3, :] = jnp.sum(vec_acc[1], axis=0, keepdims=True)
        vecg_buf[0, 0:1, :] = mm(ones, gb[half])[0:1, :]

    def grad_inner():
        grad_columns(hs_flipped[...], ginner, 0, ff, inner_col)

    def grad_out():
        turn(gb, half)
        pending[6].wait()
        turn(gb, other)
        grad_columns(flipped[...], attn, 0, heads_wide, out_col)

    def heads_backward():
        def to_heads(h, carry):
            gattn[h] = mm(gb[h], weights(out_col, heads_wide)).astype(LOW)
            return carry

        lax.fori_loop(0, 2, to_heads, 0)

    def input_away():
        last_send[...] = mm(dqkv[other], weights(0, 3 * heads_wide), NT).astype(LOW)
        pending[7] = pair_copy(last_send, last_land, 7)
        pending[7].start()

    def grad_heads():
        grad_columns(xs_flipped[...], dqkv, 0, 3 * heads_wide, 0)

    def input_backward():
        own_part[...] = mm(dqkv[half], weights(0, 3 * heads_wide), NT)
        pending[7].wait()

        def leave(i, carry):
            at = pl.ds(pl.multiple_of(i * chunk, chunk), chunk)
            m, quarter = i // per_bin, lax.rem(i, per_bin)
            sources = pl.ds(quarter * (chunk // rows), chunk // rows)
            grad_x = grad_keep[at, :] + (own_part[at, :] + last_land[at, :].astype(F32))
            gx_send[sources, m] = grad_x.reshape(chunk // rows, rows, width).astype(LOW)
            return carry

        lax.fori_loop(0, chunks, leave, 0)

    def pair_vectors():
        for i, start in enumerate((0, value_col)):
            columns = slice(start, start + heads_wide)
            vecg_buf[0, 8:9, i * heads_wide : (i + 1) * heads_wide] = (
                mm(ones, dqkv[0, :, columns]) + mm(ones, dqkv[1, :, columns])
            )[0:1, :]
        vecg_buf[0, 9:16, :] = jnp.zeros((7, width), F32)

        swap_v = pair_copy(vecg_buf.at[0], vec_pair, 8)
        swap_v.start()
        swap_v.wait()
        vecg_buf[0, 0:6, :] = vecg_buf[0, 0:6, :] + vec_pair[0:6, :]

    def take_output():
        settle(out_send, out_land, out_sems)
        hand_back(out_land, layer_out_ref, layer_out_hbm)

    def take_input_grad():
        settle(gx_send, gx_land, gx_sems)
        hand_back(gx_land, grad_tokens_ref, grad_tokens_hbm)

    folds = []

    def sum_vectors(turn=None):
        if folds:
            folds[-1]()
        if len(folds) < stages:
            begin, fold = swing(vecg_buf, vecg_land, vecg_sems, len(folds), vec_total)
            begin()
            folds.append(fold)
        else:
            copy_out(vec_total, vec_out_hbm)
            folds.append(lambda: None)

    exchanges = {
        X: (x_send, x_land, x_sems),
        DY: (dy_send, dy_land, dy_sems),
        OUT: (out_send, out_land, out_sems),
        GX: (gx_send, gx_land, gx_sems),
    }
    steps = {
        GATHER: advance,
        REDUCE: reduce,
        NEAR: lambda name: push(*exchanges[name], True),
        FAR: lambda name: push(*exchanges[name], False),
        VECTORS: sum_vectors,
        FIND_SLOTS: find_slots,
        SEND_PIECES: send_pieces,
        ARRANGE_TOKENS: arrange_tokens,
        ARRANGE_COTANGENT: arrange_cotangent,
        WHOLE_VECTORS: whole_vectors,
        MASK_BINS: mask_bins,
        TAKE_TOKENS: take_tokens,
        PROJECT_HEADS: project_heads,
        ATTEND_THIRD: attend_third,
        ATTEND_BACK_THIRD: attend_back_third,
        PROJECT_OUT: project_out,
        NORM_AFTER_ATTENTION: norm_after_attention,
        WIDEN_TOKENS: widen_tokens,
        NARROW_TOKENS: narrow_tokens,
        NORM_AFTER_FFN: norm_after_ffn,
        NORM_FFN_BACKWARD: norm_ffn_backward,
        GRAD_OUTER: grad_outer,
        FFN_BACKWARD: ffn_backward,
        GRAD_INNER: grad_inner,
        GRAD_OUT: grad_out,
        HEADS_BACKWARD: heads_backward,
        INPUT_AWAY: input_away,
        GRAD_HEADS: grad_heads,
        INPUT_BACKWARD: input_backward,
        PAIR_VECTORS: pair_vectors,
        TAKE_OUTPUT: take_output,
        TAKE_INPUT_GRAD: take_input_grad,
    }
    covered = {
        PROJECT_HEADS: (0, 3 * heads_wide),
        PROJECT_OUT: (out_col, inner_col),
        WIDEN_TOKENS: (inner_col, outer_col),
        NARROW_TOKENS: (outer_col, outer_col + ff),
    }
    for name, *which in SCHEDULE:
        low, high = covered.get(name, (0, 0))
        for number in sorted({plan[0] for plan in gather_plan}):
            cols = extent(gather_plan, number)
            while cols.start < high and cols.start + cols.size > low and gone.get(number, 0) <= stages:
                advance(number)
        steps[name](*which)
    for number in sorted({plan[0] for plan in scatter_plan}):
        while sent[number] <= stages:
            reduce(number)
    while len(folds) <= stages:
        sum_vectors()
    every_column = pl.ds(0, full.shape[-1])
    for stage in range(stages):
        shards_copy(
            full, stages - stage, every_column, gather_sends.at[stage], gather_recvs.at[0, stage]
        ).wait_send()
        shards_copy(
            grads, stage + 1, every_column, scatter_sends.at[stage], scatter_recvs.at[0, stage]
        ).wait_send()
    for copy in leaving:
        copy.wait()


def finish(*refs):
    sources, total_ref, targets = refs[:8], refs[8], refs[9:17]
    *own_refs, inner_ref, query_ref, value_ref = refs[17:26]
    *held, sems = refs[26:]
    loads = [pltpu.make_async_copy(src, hold, sems.at[0, i]) for i, (src, hold) in enumerate(zip(sources, held))]
    stores = [pltpu.make_async_copy(hold, dst, sems.at[1, i]) for i, (hold, dst) in enumerate(zip(held, targets))]
    for load in loads:
        load.start()
    for load, store in zip(loads, stores):
        load.wait()
        store.start()
    place = lax.axis_index("dp")

    def cut(row, size):
        extent = row.shape[1]
        source = lax.broadcasted_iota(jnp.int32, (extent, size), 0)
        at = lax.broadcasted_iota(jnp.int32, (extent, size), 1) + place * size
        return lax.dot_general(
            row,
            (source == at).astype(F32),
            NN,
            precision=lax.Precision.HIGHEST,
            preferred_element_type=F32,
        )

    own = cut(total_ref[0:8, :], own_refs[0].shape[0])
    for i, ref in enumerate(own_refs):
        ref[...] = own[i : i + 1, :].reshape(ref.shape)
    width, heads_wide = total_ref.shape[1], query_ref.shape[1]
    rows = inner_ref.shape[1] * lax.axis_size("dp") // width
    long = jnp.concatenate([total_ref[6 + i : 7 + i, :] for i in range(rows)], axis=1)
    inner_ref[...] = cut(jnp.broadcast_to(long, (8, long.shape[1])), inner_ref.shape[1])[0:1, :]
    query_ref[...] = total_ref[8:9, :heads_wide]
    value_ref[...] = total_ref[8:9, heads_wide:]
    for store in stores:
        store.wait()


def plans(dp_count, heads_wide, ff):
    bits = bits_of(dp_count)
    far, near = bits[:-2], bits[-2:]
    orders = {
        FAR_FIRST: (far + near, far + near[::-1]),
        NEAR_FIRST: (near[::-1] + far, near + far),
    }

    def plan_of(groups, turned):
        plan = []
        for group, (kind, first, tiles) in enumerate(groups):
            start, size = first * LANES, (tiles + 1) // 2 * LANES
            one, two = (order[::-1] if turned else order for order in orders[kind])
            plan.append((group, one, start, size))
            plan.append((group, two, start + size, tiles * LANES - size))
        return plan

    return plan_of(GATHERS, False), plan_of(SCATTERS, True)


def shards_fast(
    tokens,
    cotangent,
    block_route,
    lengths,
    w_query,
    w_key,
    w_value,
    b_query,
    b_value,
    w_out,
    b_out,
    gain_attn,
    shift_attn,
    w_inner,
    b_inner,
    w_outer,
    b_outer,
    gain_ffn,
    shift_ffn,
):
    dp_count = lax.axis_size("dp")
    micro, rows, width = lengths.shape[0], tokens.shape[1], tokens.shape[2]
    heads_wide, ff = w_query.shape[1], w_inner.shape[1]
    place = lax.axis_index("dp")
    blocks = micro * dp_count
    own_width = width // dp_count
    columns = 4 * heads_wide + 2 * ff
    stages = dp_count.bit_length() - 1
    bits = (2,) * stages
    inner_col, outer_col = 4 * heads_wide, 4 * heads_wide + ff
    gather_plan, scatter_plan = plans(dp_count, heads_wide, ff)
    bin_half = dp_count * rows
    tall = micro * bin_half
    vmem, smem = pl.BlockSpec(memory_space=pltpu.VMEM), pl.BlockSpec(memory_space=pltpu.SMEM)
    dma = pltpu.SemaphoreType.DMA
    swap_shape = (dp_count, micro, rows, width)
    scratch = [
        pltpu.SMEM((micro, dp_count), jnp.int32),
        pltpu.SMEM((blocks,), jnp.int32),
        pltpu.VMEM(tokens.shape, LOW),
        pltpu.VMEM(tokens.shape, LOW),
        pltpu.VMEM(tokens.shape, LOW),
        pltpu.VMEM(tokens.shape, LOW),
        pltpu.VMEM((own_width, columns), F32),
        pltpu.VMEM(bits + (own_width, columns), LOW),
        pltpu.VMEM(bits + (own_width, columns), LOW),
    ]
    scratch += [pltpu.VMEM(swap_shape, LOW) for _ in range(8)]
    scratch += [pltpu.VMEM((2, tall, width), LOW) for _ in range(4)]
    scratch += [pltpu.VMEM((width, 2 * tall), LOW) for _ in range(3)]
    scratch += [pltpu.VMEM((2, tall, 3 * heads_wide), LOW) for _ in range(2)]
    scratch += [pltpu.VMEM((2, tall, heads_wide), LOW) for _ in range(2)]
    scratch += [
        pltpu.VMEM((micro, heads_wide // HD, 2 * bin_half, 2 * bin_half), LOW),
        pltpu.VMEM((micro, 2 * bin_half, 2 * bin_half), F32),
    ]
    scratch += [pltpu.VMEM((2, tall, ff), LOW) for _ in range(3)]
    scratch += [
        pltpu.VMEM((tall, width), F32),
        pltpu.VMEM((tall, LANES), F32),
        pltpu.VMEM((tall, LANES), F32),
        pltpu.VMEM((tall, width), F32),
        pltpu.VMEM((tall, width), F32),
        pltpu.VMEM((tall, width), LOW),
        pltpu.VMEM((3, tall, width), LOW),
        pltpu.VMEM((tall, width), LOW),
        pltpu.VMEM((tall, width), LOW),
        pltpu.VMEM((16, LANES), F32),
        pltpu.VMEM((dp_count, 16, LANES), F32),
        pltpu.VMEM((16, width), F32),
        pltpu.VMEM((16, width), F32),
        pltpu.VMEM((stages, 16, width), F32),
        pltpu.VMEM((stages, 16, width), F32),
        pltpu.VMEM((3, 8, width), F32),
        pltpu.VMEM((16, width), F32),
    ]
    scratch += [
        pltpu.VMEM(
            (2,) * (stages - 1 - stage)
            + (own_width, sum(size for group, _, _, size in scatter_plan if group == wanted)),
            LOW,
        )
        for wanted in range(max(group for group, _, _, _ in scatter_plan) + 1)
        for stage in range(stages)
    ]
    scratch += [dma((2,)) for _ in range(4)]
    scratch += [
        dma((stages,)),
        dma((len(gather_plan), stages)),
        dma((stages,)),
        dma((len(scatter_plan), stages)),
        dma((2,)),
        dma((2, stages)),
        dma((2, 10)),
        dma((8,)),
        dma((24,)),
    ]
    sizes = (dp_count, micro, rows, width, heads_wide, ff)
    hbm = pl.BlockSpec(memory_space=pl.ANY)
    grad_shapes = [jax.ShapeDtypeStruct((own_width, size), F32) for size in (heads_wide,) * 4 + (ff,) * 2]
    made = (
        jax.ShapeDtypeStruct(tokens.shape, tokens.dtype),
        jax.ShapeDtypeStruct(tokens.shape, tokens.dtype),
        *grad_shapes,
    )
    *big, total = pl.pallas_call(
        partial(layer, sizes, gather_plan, scatter_plan),
        out_shape=(*made, jax.ShapeDtypeStruct((16, width), F32)),
        in_specs=[hbm] * 2 + [smem] * 2 + [hbm] * 6 + [vmem] * 10,
        out_specs=[hbm] * 9,
        scratch_shapes=scratch,
        compiler_params=pltpu.CompilerParams(
            collective_id=0, has_side_effects=True, vmem_limit_bytes=VMEM_BYTES
        ),
        name="layer",
    )(
        tokens,
        cotangent,
        block_route,
        lengths,
        w_query,
        w_key,
        w_value,
        w_out.T,
        w_inner,
        w_outer.T,
        b_out,
        gain_attn,
        shift_attn,
        b_outer,
        gain_ffn,
        shift_ffn,
        block_route,
        b_query,
        b_value,
        b_inner,
    )
    own_inner = b_inner.shape[1]
    results = pl.pallas_call(
        finish,
        out_shape=(
            *made,
            *[jax.ShapeDtypeStruct((own_width,), F32) for _ in range(6)],
            jax.ShapeDtypeStruct((1, own_inner), F32),
            jax.ShapeDtypeStruct((1, heads_wide), F32),
            jax.ShapeDtypeStruct((1, heads_wide), F32),
        ),
        in_specs=[hbm] * 8 + [vmem],
        out_specs=[hbm] * 8 + [vmem] * 9,
        scratch_shapes=[pltpu.VMEM(result.shape, result.dtype) for result in made] + [dma((2, 8))],
        name="finish",
    )(*big, total)
    layer_out, grad_tokens, gq, gk, gv, go, gi, gu = results[:8]
    own, (bias_inner, bias_query, bias_value) = results[8:14], results[14:]
    return (
        layer_out,
        grad_tokens,
        gq,
        gk,
        gv,
        bias_query,
        bias_value,
        go.T,
        own[0],
        own[1],
        own[2],
        gi,
        bias_inner,
        gu.T,
        own[3],
        own[4],
        own[5],
    )


def shards(
    tokens,
    cotangent,
    block_route,
    lengths,
    w_query,
    w_key,
    w_value,
    b_query,
    b_value,
    w_out,
    b_out,
    gain_attn,
    shift_attn,
    w_inner,
    b_inner,
    w_outer,
    b_outer,
    gain_ffn,
    shift_ffn,
):
    dp_count = lax.axis_size("dp")
    micro_count = lengths.shape[0]
    half_rows = tokens.shape[1]
    model_width = tokens.shape[2]
    local_heads = HEADS // lax.axis_size("tensor")
    score_scale = HD ** (-0.5)
    blocks = tokens.reshape(micro_count, dp_count, half_rows, model_width)
    upstream = cotangent.reshape(micro_count, dp_count, half_rows, model_width)
    target = block_route.reshape(micro_count, dp_count)
    dest_dev = target // (micro_count * dp_count)
    bin_place = target % dp_count
    micro_ids = jnp.broadcast_to(
        jnp.arange(micro_count, dtype=jnp.int32)[:, None], (micro_count, dp_count)
    )
    slot_ids = jnp.broadcast_to(
        jnp.arange(dp_count, dtype=jnp.int32)[None, :], (micro_count, dp_count)
    )
    inverse = jnp.zeros((micro_count, dp_count), jnp.int32).at[micro_ids, dest_dev].set(slot_ids)
    by_dest = jnp.take_along_axis(blocks, inverse[:, :, None, None], axis=1)
    grad_dest = jnp.take_along_axis(upstream, inverse[:, :, None, None], axis=1)
    place_dest = jnp.take_along_axis(bin_place, inverse, axis=1)
    arrived, arrived_grad, arrived_place = (
        lax.all_to_all(by_dest, "dp", split_axis=1, concat_axis=1, tiled=True),
        lax.all_to_all(grad_dest, "dp", split_axis=1, concat_axis=1, tiled=True),
        lax.all_to_all(place_dest, "dp", split_axis=1, concat_axis=1, tiled=True),
    )
    anchor = (
        jnp.zeros((micro_count, dp_count), jnp.int32).at[micro_ids, arrived_place].set(slot_ids)
    )
    bin_tokens = jnp.take_along_axis(arrived, anchor[:, :, None, None], axis=1)
    bin_grads = jnp.take_along_axis(arrived_grad, anchor[:, :, None, None], axis=1)
    acc_query = jnp.zeros((model_width, w_query.shape[1]), jnp.float32)
    acc_key = jnp.zeros((model_width, w_key.shape[1]), jnp.float32)
    acc_value = jnp.zeros((model_width, w_value.shape[1]), jnp.float32)
    acc_out = jnp.zeros((w_out.shape[0], model_width), jnp.float32)
    acc_inner = jnp.zeros((model_width, w_inner.shape[1]), jnp.float32)
    acc_outer = jnp.zeros((w_outer.shape[0], model_width), jnp.float32)
    acc_bias_query = jnp.zeros((1, w_query.shape[1]), jnp.float32)
    acc_bias_value = jnp.zeros((1, w_value.shape[1]), jnp.float32)
    acc_bias_inner = jnp.zeros((1, w_inner.shape[1]), jnp.float32)
    acc_vectors = jnp.zeros((6, model_width), jnp.float32)
    out_bins = []
    grad_bins = []
    for micro_step in range(micro_count):
        gathered = (
            lax.all_gather(w_query, "dp", axis=0, tiled=True),
            lax.all_gather(w_key, "dp", axis=0, tiled=True),
            lax.all_gather(w_value, "dp", axis=0, tiled=True),
            lax.all_gather(w_out, "dp", axis=1, tiled=True),
            lax.all_gather(w_inner, "dp", axis=0, tiled=True),
            lax.all_gather(w_outer, "dp", axis=1, tiled=True),
            lax.all_gather(b_inner, "dp", axis=1, tiled=True),
            lax.all_gather(b_out, "dp", axis=0, tiled=True),
            lax.all_gather(gain_attn, "dp", axis=0, tiled=True),
            lax.all_gather(shift_attn, "dp", axis=0, tiled=True),
            lax.all_gather(b_outer, "dp", axis=0, tiled=True),
            lax.all_gather(gain_ffn, "dp", axis=0, tiled=True),
            lax.all_gather(shift_ffn, "dp", axis=0, tiled=True),
        )
        (
            full_query,
            full_key,
            full_value,
            full_out,
            full_inner,
            full_outer,
            bias_inner,
            bias_out,
            full_gain_attn,
            full_shift_attn,
            bias_outer,
            full_gain_ffn,
            full_shift_ffn,
        ) = gathered
        own_rows = bin_tokens[micro_step]
        whole_bin = lax.all_gather(own_rows, "tensor", axis=1, tiled=True).reshape(-1, model_width)
        bin_rows = whole_bin.shape[0]
        block_rows = math.gcd(bin_rows, 512)
        segment = segment_of(lengths[micro_step], bin_rows)
        query = (
            jnp.dot(whole_bin, full_query, preferred_element_type=jnp.float32) + b_query[0]
        ).astype(jnp.bfloat16)
        keys = jnp.dot(whole_bin, full_key, preferred_element_type=jnp.float32).astype(jnp.bfloat16)
        values = (
            jnp.dot(whole_bin, full_value, preferred_element_type=jnp.float32) + b_value[0]
        ).astype(jnp.bfloat16)
        query_heads = query.reshape(bin_rows, local_heads, HD)
        key_heads = keys.reshape(bin_rows, local_heads, HD)
        value_heads = values.reshape(bin_rows, local_heads, HD)
        attn_heads, log_totals = attend_forward(
            query_heads, key_heads, value_heads, segment, block_rows, score_scale
        )
        attn = attn_heads.reshape(bin_rows, local_heads * HD)
        attn_partial = jnp.dot(attn, full_out, preferred_element_type=jnp.float32).reshape(
            dp_count, -1, model_width
        )
        branch = lax.psum_scatter(attn_partial, "tensor", scatter_dimension=1, tiled=True).reshape(
            -1, model_width
        )
        mid = own_rows.reshape(-1, model_width).astype(jnp.float32) + branch + bias_out
        hidden, normed_attn, spread_attn = layer_norm(mid, full_gain_attn, full_shift_attn)
        hidden_low = hidden.astype(jnp.bfloat16).reshape(dp_count, half_rows, model_width)
        hidden_whole = lax.all_gather(hidden_low, "tensor", axis=1, tiled=True).reshape(
            -1, model_width
        )
        inner = (
            jnp.dot(hidden_whole, full_inner, preferred_element_type=jnp.float32) + bias_inner[0]
        )
        gelu_value, gelu_pull = jax.vjp(partial(jax.nn.gelu, approximate=False), inner)
        gelu_low = gelu_value.astype(jnp.bfloat16)
        ffn_partial = jnp.dot(gelu_low, full_outer, preferred_element_type=jnp.float32).reshape(
            dp_count, -1, model_width
        )
        ffn = lax.psum_scatter(ffn_partial, "tensor", scatter_dimension=1, tiled=True).reshape(
            -1, model_width
        )
        top = hidden + ffn + bias_outer
        result, normed_ffn, spread_ffn = layer_norm(top, full_gain_ffn, full_shift_ffn)
        out_bins.append(result.astype(jnp.bfloat16).reshape(dp_count, half_rows, model_width))
        back_full = (
            lax.all_gather(w_query, "dp", axis=0, tiled=True),
            lax.all_gather(w_key, "dp", axis=0, tiled=True),
            lax.all_gather(w_value, "dp", axis=0, tiled=True),
            lax.all_gather(w_out, "dp", axis=1, tiled=True),
            lax.all_gather(w_inner, "dp", axis=0, tiled=True),
            lax.all_gather(w_outer, "dp", axis=1, tiled=True),
            lax.all_gather(gain_attn, "dp", axis=0, tiled=True),
            lax.all_gather(gain_ffn, "dp", axis=0, tiled=True),
        )
        (
            back_query,
            back_key,
            back_value,
            back_out,
            back_inner,
            back_outer,
            back_gain_attn,
            back_gain_ffn,
        ) = back_full
        grad_result = bin_grads[micro_step].reshape(-1, model_width).astype(jnp.float32)
        grad_top, grad_gain_ffn, grad_shift_ffn = norm_back(
            grad_result, normed_ffn, spread_ffn, back_gain_ffn
        )
        grad_ffn_low = grad_top.astype(jnp.bfloat16)
        grad_bias_outer = jnp.sum(grad_ffn_low.astype(jnp.float32), axis=0)
        grad_ffn_whole = lax.all_gather(
            grad_ffn_low.reshape(dp_count, half_rows, model_width), "tensor", axis=1, tiled=True
        ).reshape(-1, model_width)
        acc_outer = acc_outer + jnp.einsum(
            "nf,nd->fd", gelu_low, grad_ffn_whole, preferred_element_type=jnp.float32
        )
        grad_gelu = jnp.einsum(
            "nd,fd->nf", grad_ffn_whole, back_outer, preferred_element_type=jnp.float32
        )
        grad_inner_low = gelu_pull(grad_gelu)[0].astype(jnp.bfloat16)
        acc_bias_inner = acc_bias_inner + jnp.sum(grad_inner_low.astype(jnp.float32), axis=0)[None]
        acc_inner = acc_inner + jnp.einsum(
            "nd,nf->df", hidden_whole, grad_inner_low, preferred_element_type=jnp.float32
        )
        hidden_partial = jnp.einsum(
            "nf,df->nd", grad_inner_low, back_inner, preferred_element_type=jnp.float32
        ).reshape(dp_count, -1, model_width)
        grad_hidden = grad_top + lax.psum_scatter(
            hidden_partial, "tensor", scatter_dimension=1, tiled=True
        ).reshape(-1, model_width)
        grad_mid, grad_gain_attn, grad_shift_attn = norm_back(
            grad_hidden, normed_attn, spread_attn, back_gain_attn
        )
        grad_branch_low = grad_mid.astype(jnp.bfloat16)
        grad_bias_out = jnp.sum(grad_branch_low.astype(jnp.float32), axis=0)
        grad_branch_whole = lax.all_gather(
            grad_branch_low.reshape(dp_count, half_rows, model_width), "tensor", axis=1, tiled=True
        ).reshape(-1, model_width)
        acc_out = acc_out + jnp.einsum(
            "nh,nd->hd", attn, grad_branch_whole, preferred_element_type=jnp.float32
        )
        grad_attn_low = jnp.einsum(
            "nd,hd->nh", grad_branch_whole, back_out, preferred_element_type=jnp.float32
        ).astype(jnp.bfloat16)
        grad_heads = grad_attn_low.reshape(bin_rows, local_heads, HD)
        grad_query, grad_keys, grad_values = attend_backward(
            query_heads,
            key_heads,
            value_heads,
            grad_heads,
            log_totals,
            segment,
            block_rows,
            score_scale,
        )
        grad_query_low = grad_query.reshape(bin_rows, -1).astype(jnp.bfloat16)
        grad_key_low = grad_keys.reshape(bin_rows, -1).astype(jnp.bfloat16)
        grad_value_low = grad_values.reshape(bin_rows, -1).astype(jnp.bfloat16)
        acc_bias_query = acc_bias_query + jnp.sum(grad_query_low.astype(jnp.float32), axis=0)[None]
        acc_bias_value = acc_bias_value + jnp.sum(grad_value_low.astype(jnp.float32), axis=0)[None]
        acc_query = acc_query + jnp.einsum(
            "nd,nh->dh", whole_bin, grad_query_low, preferred_element_type=jnp.float32
        )
        acc_key = acc_key + jnp.einsum(
            "nd,nh->dh", whole_bin, grad_key_low, preferred_element_type=jnp.float32
        )
        acc_value = acc_value + jnp.einsum(
            "nd,nh->dh", whole_bin, grad_value_low, preferred_element_type=jnp.float32
        )
        input_partial = (
            jnp.einsum("nh,dh->nd", grad_query_low, back_query, preferred_element_type=jnp.float32)
            + jnp.einsum("nh,dh->nd", grad_key_low, back_key, preferred_element_type=jnp.float32)
            + jnp.einsum(
                "nh,dh->nd", grad_value_low, back_value, preferred_element_type=jnp.float32
            )
        )
        grad_input = grad_mid + lax.psum_scatter(
            input_partial.reshape(dp_count, -1, model_width).astype(jnp.bfloat16),
            "tensor",
            scatter_dimension=1,
            tiled=True,
        ).astype(jnp.float32).reshape(-1, model_width)
        grad_bins.append(grad_input.astype(jnp.bfloat16).reshape(dp_count, half_rows, model_width))
        acc_vectors = acc_vectors + jnp.stack(
            [
                grad_bias_out,
                grad_gain_attn,
                grad_shift_attn,
                grad_bias_outer,
                grad_gain_ffn,
                grad_shift_ffn,
            ]
        )
    out_stack = jnp.stack(out_bins)
    grad_stack = jnp.stack(grad_bins)
    send_out = jnp.take_along_axis(out_stack, arrived_place[:, :, None, None], axis=1)
    send_grad = jnp.take_along_axis(grad_stack, arrived_place[:, :, None, None], axis=1)
    back_out_rows, back_grad_rows = (
        lax.all_to_all(send_out, "dp", split_axis=1, concat_axis=1, tiled=True),
        lax.all_to_all(send_grad, "dp", split_axis=1, concat_axis=1, tiled=True),
    )
    layer_out = jnp.take_along_axis(back_out_rows, dest_dev[:, :, None, None], axis=1).reshape(
        tokens.shape
    )
    grad_tokens = jnp.take_along_axis(back_grad_rows, dest_dev[:, :, None, None], axis=1).reshape(
        tokens.shape
    )
    sum_query, sum_key, sum_value, sum_out, sum_inner, sum_outer, sum_bias_inner = (
        lax.psum_scatter(acc_query, "dp", scatter_dimension=0, tiled=True),
        lax.psum_scatter(acc_key, "dp", scatter_dimension=0, tiled=True),
        lax.psum_scatter(acc_value, "dp", scatter_dimension=0, tiled=True),
        lax.psum_scatter(acc_out, "dp", scatter_dimension=1, tiled=True),
        lax.psum_scatter(acc_inner, "dp", scatter_dimension=0, tiled=True),
        lax.psum_scatter(acc_outer, "dp", scatter_dimension=1, tiled=True),
        lax.psum_scatter(acc_bias_inner, "dp", scatter_dimension=1, tiled=True),
    )
    half_width = w_query.shape[1]
    tensor_pos = lax.axis_index("tensor")
    bias_pair = lax.dynamic_update_slice(
        jnp.zeros((2, model_width), jnp.float32),
        jnp.concatenate([acc_bias_query, acc_bias_value], axis=0),
        (jnp.int32(0), tensor_pos * half_width),
    )
    vectors, bias_total = lax.psum((acc_vectors, bias_pair), ("dp", "tensor"))
    own_width = model_width // dp_count
    vec_own = lax.dynamic_slice_in_dim(vectors, lax.axis_index("dp") * own_width, own_width, 1)
    bias_own = lax.dynamic_slice_in_dim(bias_total, tensor_pos * half_width, half_width, 1)
    return (
        layer_out,
        grad_tokens,
        sum_query,
        sum_key,
        sum_value,
        bias_own[0:1],
        bias_own[1:2],
        sum_out,
        vec_own[0],
        vec_own[1],
        vec_own[2],
        sum_inner,
        sum_bias_inner,
        sum_outer,
        vec_own[3],
        vec_own[4],
        vec_own[5],
    )


def solution(mesh):
    placed = (
        P("dp", "tensor", None),
        P("dp", "tensor", None),
        P("dp"),
        P("dp", None),
        P("dp", "tensor"),
        P("dp", "tensor"),
        P("dp", "tensor"),
        P("tensor", None),
        P("tensor", None),
        P("tensor", "dp"),
        P("dp"),
        P("dp"),
        P("dp"),
        P("dp", "tensor"),
        P("tensor", "dp"),
        P("tensor", "dp"),
        P("dp"),
        P("dp"),
        P("dp"),
    )
    dp_count = mesh.shape["dp"]

    def body(*args):
        tokens, w_query, b_inner = args[0], args[4], args[14]
        fits = (
            dp_count & (dp_count - 1) == 0
            and w_query.shape[0] % 16 == 0
            and tokens.shape[1] % 8 == 0
            and mesh.shape["tensor"] == 2
        )
        return (shards_fast if fits else shards)(*args)

    return jax.shard_map(
        body,
        mesh=mesh,
        in_specs=placed,
        out_specs=(
            P("dp", "tensor", None),
            P("dp", "tensor", None),
            P("dp", "tensor"),
            P("dp", "tensor"),
            P("dp", "tensor"),
            P("tensor", None),
            P("tensor", None),
            P("tensor", "dp"),
            P("dp"),
            P("dp"),
            P("dp"),
            P("dp", "tensor"),
            P("tensor", "dp"),
            P("tensor", "dp"),
            P("dp"),
            P("dp"),
            P("dp"),
        ),
        check_vma=False,
    )
```
